128 devices in a mesh: grp: 4 (over y), seq: 32 (over z, x, core).
Axes of the slice: x: 4, y: 4, z: 4, core: 2. Of those that a mesh axis runs over, the one named last changes fastest.
Arguments:
- hidden_in: bfloat16 [114688, 1024], P(('grp', 'seq')), may hold values from -16 to 16
- attn_gain: float32 [1024], replicated, may hold values from 0.1 to 1.9
- w_qkv: bfloat16 [1024, 3072], replicated
- head_gain: float32 [1024], replicated, may hold values from 0.1 to 1.9
- w_out: bfloat16 [1024, 1024], replicated, may hold values from -0.1875 to 0.1875
- ffn_gain: float32 [1024], replicated, may hold values from 0.1 to 1.9
- w_gate: bfloat16 [32, 1024, 896], P('seq'), may hold values from -0.1875 to 0.1875
- w_up: bfloat16 [32, 1024, 896], P('seq'), may hold values from -0.1875 to 0.1875
- w_down: bfloat16 [32, 896, 1024], P('seq'), may hold values from -0.1875 to 0.1875
- pair_ids: int32 [896, 2], P(('grp', 'seq')), may hold values from 0 to 31, as said below
- gate_codes: int32 [896, 2], P(('grp', 'seq')), may hold values from 1 to 255
Outputs:
- layer_out: bfloat16 [114688, 1024], P(('grp', 'seq'))
The draws below stay inside these ranges and needn't reach their ends.
Inputs may be any that keep to these rules, and one draw needn't show every extreme that they name: `pair_ids`: each row names two different experts. Within the 7 rows of one device (aligned blocks of 7 rows) no expert is named more than 2 times, and some expert exactly 2 times. Within the rows of one group (aligned blocks of 224 rows) exactly one expert is named 28 times, every other at most 14 times and some other exactly 14 times; the expert named 28 times differs from group to group.
All inputs are finite; a program needn't handle non-finite values.
Results may differ from the reference program's by a relative error of at most 0.0055.
Values may be sent and summed in bfloat16 or wider, within the bound.
A program may use at most 192 MiB of HBM per device.

```python
import math
import jax
import jax.numpy as jnp
from jax import lax

D = 1024
HEADS = 8
HEAD_DIM = 128
FF = 896
ROWS = 128
SPAN = 128
CAP = 2
TOK_DEV = 896
TOKENS = 114688
BLK_DEV = 7
BLOCKS = 896
EXPERTS = 32


def group_pairs(key, favored):
    owners = EXPERTS
    limit = min(4 * BLK_DEV, CAP * EXPERTS)
    hot_count = limit // 2
    cycle = 2 * (EXPERTS - 1)
    key_perm, key_dev, key_off, key_rows, key_flip = jax.random.split(key, 5)
    numbers = jnp.arange(EXPERTS, dtype=jnp.int32)
    scores = jax.random.randint(key_perm, (EXPERTS,), 0, 1 << 20) * EXPERTS + numbers
    scores = jnp.where(numbers == favored, -1, scores)
    ranking = jnp.argsort(scores).astype(jnp.int32)
    device_rank = jax.random.permutation(key_dev, owners).astype(jnp.int32)
    is_hot = (device_rank < hot_count).astype(jnp.int32)
    lengths = 2 * BLK_DEV - 2 * is_hot
    offset = jax.random.randint(key_off, (), 0, cycle)
    starts = (jnp.cumsum(lengths) - lengths).astype(jnp.int32) + offset
    places = jnp.arange(2 * BLK_DEV, dtype=jnp.int32)
    index = (starts[:, None] + places[None, :] - 2 * is_hot[:, None]) % cycle
    cold = jnp.take(ranking, 1 + index // 2)
    visits = jnp.where((is_hot[:, None] == 1) & (places[None, :] < 2), favored, cold)
    pairs = jnp.stack([visits[:, :BLK_DEV], visits[:, BLK_DEV:]], axis=-1)
    mixing = jax.random.randint(key_rows, (owners, BLK_DEV), 0, 1 << 16) * BLK_DEV + jnp.arange(BLK_DEV, dtype=jnp.int32)[None, :]
    order = jnp.argsort(mixing, axis=1)
    pairs = jnp.take_along_axis(pairs, order[..., None], axis=1)
    flip = jax.random.randint(key_flip, (owners, BLK_DEV), 0, 2)
    pairs = jnp.where(flip[..., None] == 1, pairs[..., ::-1], pairs)
    return pairs.astype(jnp.int32)


def draw_pair_ids(key, part):
    groups = BLOCKS // (BLK_DEV * EXPERTS)
    base_key = jax.random.fold_in(key, 17)
    group_keys = jax.random.split(base_key, groups)
    leaders = jax.random.permutation(jax.random.fold_in(base_key, 23), EXPERTS)[:groups].astype(jnp.int32)
    return jax.vmap(group_pairs)(group_keys, leaders).reshape(BLOCKS, 2).astype(jnp.int32)


def draw_hidden_in(key, part):
    regions = TOKENS // TOK_DEV
    key_noise, key_common, key_amp = jax.random.split(jax.random.fold_in(key, 31), 3)
    noise = jnp.clip(jax.random.normal(key_noise, (regions, TOK_DEV, D), jnp.float32), -4.0, 4.0)
    amp = jnp.exp(jax.random.uniform(key_amp, (regions,), jnp.float32, math.log(0.3), math.log(3.0)))
    common = jnp.clip(jax.random.normal(key_common, (regions, D), jnp.float32), -4.0, 4.0)
    values = noise + amp[:, None, None] * common[:, None, :]
    return jnp.clip(values, -16.0, 16.0).reshape(TOKENS, D).astype(jnp.bfloat16)


def draw_w_qkv(key, part):
    key_base, key_query, key_keys, key_values = jax.random.split(jax.random.fold_in(key, 29), 4)
    base = jnp.clip(jax.random.normal(key_base, (D, 3 * D), jnp.float32), -4.0, 4.0)
    lowest = 0.5
    highest = 2.5
    query_scale = jnp.exp(jax.random.uniform(key_query, (HEADS,), jnp.float32, math.log(lowest), math.log(highest)))
    keys_scale = jnp.exp(jax.random.uniform(key_keys, (HEADS,), jnp.float32, math.log(lowest), math.log(highest)))
    values_scale = jnp.exp(jax.random.uniform(key_values, (HEADS,), jnp.float32, math.log(0.5), math.log(2.0)))
    columns = jnp.concatenate([jnp.repeat(query_scale, HEAD_DIM), jnp.repeat(keys_scale, HEAD_DIM), jnp.repeat(values_scale, HEAD_DIM)])
    return (base * columns[None, :] / math.sqrt(D)).astype(jnp.bfloat16)


def touch_ends(values, rng, smallest, high):
    longest = values.shape.index(max(values.shape))
    spots = []
    for shift in (0, 1):
        where = [jax.random.randint(jax.random.fold_in(rng, axis), (), 0, length) for axis, length in enumerate(values.shape)]
        where[longest] = (where[longest] + shift) % values.shape[longest]
        spots.append(tuple(where))
    return values.at[spots[0]].set(smallest).at[spots[1]].set(high)


def levels(key, extent, cuts, low, top_value):
    level, own = 1.0, jax.random.fold_in(key, 6)
    for axis_at, blocks in cuts:
        steps = jnp.exp(jax.random.uniform(jax.random.fold_in(own, axis_at), (blocks,), jnp.float32, low / len(cuts), top_value / len(cuts)))
        level = level * jnp.repeat(steps, extent[axis_at] // blocks).reshape([-1 if axis == axis_at else 1 for axis in range(len(extent))])
    return level


def centred(key, extent, deviation, reach, cuts=(), kind=jnp.bfloat16):
    drawn = jax.random.normal(key, extent, jnp.float32) * deviation
    if len(cuts) > 0:
        drawn = levels(key, extent, cuts, -0.22, 0.18) * drawn
    return jnp.clip(drawn, min=-reach, max=reach).astype(kind)


def setup_inputs(seed: int = 0) -> dict:
    key_of = jax.random.split(jax.random.key(seed), 12)
    hidden_in = draw_hidden_in(jax.random.fold_in(key_of[11], 71), 0)
    attn_gain = jnp.clip(1.0 + 0.18 * jax.random.normal(key_of[1], (D,), jnp.float32), 0.1, 1.9)
    w_qkv = draw_w_qkv(jax.random.fold_in(key_of[11], 71), 0)
    head_gain = jnp.clip(1.0 + 0.18 * jax.random.normal(key_of[3], (D,), jnp.float32), 0.1, 1.9)
    w_out = centred(key_of[4], (D, D), D ** -0.5, 0.1875)
    ffn_gain = jnp.clip(1.0 + 0.18 * jax.random.normal(key_of[5], (D,), jnp.float32), 0.1, 1.9)
    w_gate = centred(key_of[6], (EXPERTS, D, FF), D ** -0.5, 0.1875, ((0, 32),))
    w_up = centred(key_of[7], (EXPERTS, D, FF), D ** -0.5, 0.1875, ((0, 32),))
    w_down = centred(key_of[8], (EXPERTS, FF, D), FF ** -0.5, 0.1875, ((0, 32),))
    pair_ids = draw_pair_ids(jax.random.fold_in(key_of[11], 71), 0)
    gate_codes = touch_ends(jax.random.randint(key_of[10], (BLOCKS, 2), 1, 256), jax.random.fold_in(key_of[10], 1), 1, 255).astype(jnp.int32)
    return {"hidden_in": hidden_in, "attn_gain": attn_gain, "w_qkv": w_qkv, "head_gain": head_gain, "w_out": w_out, "ffn_gain": ffn_gain, "w_gate": w_gate, "w_up": w_up, "w_down": w_down, "pair_ids": pair_ids, "gate_codes": gate_codes}


EPS = 1e-06
HIGH = lax.Precision.HIGHEST

def norm_rows(values, gain):
    return values * lax.rsqrt(lax.optimization_barrier(jnp.mean(values * values, axis=-1, keepdims=True)) + EPS) * gain

def round_back(values):
    return lax.optimization_barrier(values.astype(jnp.bfloat16)).astype(jnp.float32)

def reference(hidden_in, attn_gain, w_qkv, head_gain, w_out, ffn_gain, w_gate, w_up, w_down, pair_ids, gate_codes):
    pieces = hidden_in.reshape(TOKENS // SPAN, SPAN, D)
    causal = jnp.arange(SPAN)[:, None] >= jnp.arange(SPAN)[None, :]

    def step(carry, block):
        state, key_sum = carry
        inputs = block.astype(jnp.float32)
        normed = norm_rows(inputs, attn_gain).astype(jnp.bfloat16)
        mixed = jnp.dot(normed, w_qkv, preferred_element_type=jnp.float32)
        query = round_back(jax.nn.elu(mixed[:, :D]) + 1.0).reshape(SPAN, HEADS, HEAD_DIM)
        keys = round_back(jax.nn.elu(mixed[:, D:2 * D]) + 1.0).reshape(SPAN, HEADS, HEAD_DIM)
        values = round_back(mixed[:, 2 * D:]).reshape(SPAN, HEADS, HEAD_DIM)
        scores = jnp.einsum('chd,shd->hcs', query, keys, precision=HIGH)
        scores = jnp.where(causal[None], scores, jnp.float32(0.0))
        numer = jnp.einsum('hcs,she->che', scores, values, precision=HIGH)
        numer = numer + jnp.einsum('chd,hde->che', query, state, precision=HIGH)
        denom = lax.optimization_barrier(jnp.sum(scores, axis=-1)).T + jnp.einsum('chd,hd->ch', query, key_sum, precision=HIGH)
        ratio = (numer / denom[..., None]).reshape(SPAN, D)
        attended = norm_rows(ratio, head_gain).astype(jnp.bfloat16)
        resid = (inputs + jnp.dot(attended, w_out, preferred_element_type=jnp.float32)).astype(jnp.bfloat16)
        ffn_in = norm_rows(resid.astype(jnp.float32), ffn_gain).astype(jnp.bfloat16)
        state = state + jnp.einsum('shd,she->hde', keys, values, precision=HIGH)
        key_sum = key_sum + lax.optimization_barrier(jnp.sum(keys, axis=0))
        return ((state, key_sum), (resid, ffn_in))
    start = (jnp.zeros((HEADS, HEAD_DIM, HEAD_DIM), jnp.float32), jnp.zeros((HEADS, HEAD_DIM), jnp.float32))
    _, (resid, ffn_in) = lax.scan(step, start, pieces)
    resid = resid.reshape(BLOCKS, ROWS, D)
    ffn_in = ffn_in.reshape(BLOCKS, ROWS, D)

    def expert_apply(rows_in, expert):
        gate = jnp.dot(rows_in, lax.dynamic_index_in_dim(w_gate, expert, 0, keepdims=False), preferred_element_type=jnp.float32)
        upper = jnp.dot(rows_in, lax.dynamic_index_in_dim(w_up, expert, 0, keepdims=False), preferred_element_type=jnp.float32)
        inner = (jax.nn.silu(gate) * upper).astype(jnp.bfloat16)
        return jnp.dot(inner, lax.dynamic_index_in_dim(w_down, expert, 0, keepdims=False), preferred_element_type=jnp.float32).astype(jnp.bfloat16)

    def one_block(item):
        rows_in, base, experts, codes = item
        weights = codes.astype(jnp.float32)
        shares = weights / jnp.sum(weights)
        first = expert_apply(rows_in, experts[0])
        second = expert_apply(rows_in, experts[1])
        total = base.astype(jnp.float32) + shares[0] * first.astype(jnp.float32) + shares[1] * second.astype(jnp.float32)
        return total.astype(jnp.bfloat16)
    result = lax.map(one_block, (ffn_in, resid, pair_ids, gate_codes))
    return result.reshape(TOKENS, D)
```

```python
import functools

import jax
import jax.numpy as jnp
from jax import lax
from jax.experimental import pallas as pl
from jax.experimental.pallas import tpu as pltpu
from jax.sharding import PartitionSpec as P

HEADS = 8
HEAD_DIM = 128
ROWS = 128
EPS = 1e-06
WAYS = 4
CORES = 2
SLOTS = 4
CHUNKS = 8
STATE = 144
LIMIT = 14
MESH = pl.DeviceIdType.MESH
F32 = jnp.float32
BF16 = jnp.bfloat16
LIMIT_BYTES = 60 * 1024 * 1024


def place():
    seq = lax.axis_index("seq")
    return lax.axis_index("grp"), seq // (WAYS * CORES), (seq // CORES) % WAYS, seq % CORES


def remote(src, dst, send, recv, device):
    return pltpu.make_async_remote_copy(
        src_ref=src, dst_ref=dst, send_sem=send, recv_sem=recv, device_id=device, device_id_type=MESH
    )


def greet(devices):
    barrier = pltpu.get_barrier_semaphore()
    for device in devices:
        pl.semaphore_signal(barrier, inc=1, device_id=device, device_id_type=MESH)
    pl.semaphore_wait(barrier, len(devices))


def norm_rows(values, gain):
    return values * lax.rsqrt(jnp.mean(values * values, axis=-1, keepdims=True) + EPS) * gain


def dot_last(a, b):
    return lax.dot_general(a, b, (((1,), (1,)), ((), ())), preferred_element_type=F32)


def dot_first(a, b):
    return lax.dot_general(a, b, (((0,), (0,)), ((), ())), preferred_element_type=F32)


def lifted(values):
    return jnp.where(values > 0.0, values + 1.0, jnp.exp(jnp.minimum(values, 0.0))).astype(BF16)


def qkv_kernel(x_ref, gain_ref, wq_ref, wk_ref, wv_ref, q_ref, k_ref, v_ref, st_ref, normed):
    tokens = x_ref.shape[0]

    @pl.when(pl.program_id(0) == 0)
    def _():
        @pl.loop(0, tokens // ROWS)
        def _(i):
            rows = pl.ds(pl.multiple_of(i * ROWS, ROWS), ROWS)
            normed[rows, :] = norm_rows(x_ref[rows, :].astype(F32), gain_ref[...]).astype(BF16)

    q_ref[...] = lifted(jnp.dot(normed[...], wq_ref[...], preferred_element_type=F32))
    k_ref[...] = lifted(jnp.dot(normed[...], wk_ref[...], preferred_element_type=F32))
    v_ref[...] = jnp.dot(normed[...], wv_ref[...], preferred_element_type=F32).astype(BF16)
    for head in range(q_ref.shape[1] // HEAD_DIM):
        cols = slice(head * HEAD_DIM, (head + 1) * HEAD_DIM)
        keys = k_ref[:, cols]
        st_ref[head, :HEAD_DIM, :] = dot_first(v_ref[:, cols], keys)
        total = jnp.sum(keys.astype(F32), axis=0, keepdims=True)
        st_ref[head, HEAD_DIM:, :] = jnp.broadcast_to(total, (STATE - HEAD_DIM, HEAD_DIM))


def qkv(x, gain, w_qkv):
    tokens, width = x.shape
    step = 2 * HEAD_DIM
    steps = width // step
    column = pl.BlockSpec((tokens, step), lambda j: (0, j))
    return pl.pallas_call(
        qkv_kernel,
        grid=(steps,),
        out_shape=[jax.ShapeDtypeStruct((tokens, width), BF16)] * 3
        + [jax.ShapeDtypeStruct((width // HEAD_DIM, STATE, HEAD_DIM), F32)],
        in_specs=[
            pl.BlockSpec((tokens, width), lambda j: (0, 0)),
            pl.BlockSpec((1, width), lambda j: (0, 0)),
            pl.BlockSpec((width, step), lambda j: (0, j)),
            pl.BlockSpec((width, step), lambda j: (0, steps + j)),
            pl.BlockSpec((width, step), lambda j: (0, 2 * steps + j)),
        ],
        out_specs=[column] * 3 + [pl.BlockSpec((2, STATE, HEAD_DIM), lambda j: (j, 0, 0))],
        scratch_shapes=[pltpu.VMEM((tokens, width), BF16)],
        compiler_params=pltpu.CompilerParams(vmem_limit_bytes=LIMIT_BYTES),
        name="qkv",
    )(x, gain, w_qkv, w_qkv, w_qkv)


def prefix_kernel(
    groups, st_ref, out_ref, mine, sib, chips, xs, row_sum, zs, plane_sum, ys, back, heads_in, sib2,
    send, recv,
):
    y, z, x, c = place()
    lane = WAYS * CORES

    def at(yy, zz, xx, cc):
        return (yy, zz * lane + xx * CORES + cc)

    sibling = at(y, z, x, 1 - c)
    along_x = [at(y, z, (x + d) % WAYS, c) for d in range(1, WAYS)]
    along_z = [at(y, (z + d) % WAYS, x, c) for d in range(1, WAYS)]
    along_y = [at((y + d) % groups, z, x, c) for d in range(1, groups)]
    greet([sibling] + along_x + along_z + along_y)
    copies = []

    def go(src, dst, device):
        n = len(copies)
        copy = remote(src, dst, send.at[n], recv.at[n], device)
        copy.start()
        copies.append(copy)
        return copy

    mine[...] = st_ref[...].astype(BF16)
    swap = go(mine, sib, sibling)
    swap.wait_recv()
    base = c * WAYS
    for i in range(WAYS):
        chips[i] = (st_ref[base + i] + sib[base + i].astype(F32)).astype(BF16)
    xs[x] = chips[x]
    waits = [go(chips.at[(x + d) % WAYS], xs.at[x], along_x[d - 1]) for d in range(1, WAYS)]
    for copy in waits:
        copy.wait_recv()
    row_sum[...] = sum(xs[i].astype(F32) for i in range(WAYS)).astype(BF16)
    zs[z] = row_sum[...]
    waits = [go(row_sum, zs.at[z], along_z[d - 1]) for d in range(1, WAYS)]
    for copy in waits:
        copy.wait_recv()
    plane_sum[...] = sum(zs[i].astype(F32) for i in range(WAYS)).astype(BF16)
    waits = [go(plane_sum, ys.at[y], along_y[d - 1]) for d in range(1, groups)]
    total = jnp.zeros(row_sum.shape, F32)
    for i in range(WAYS):
        total = total + zs[i].astype(F32) * jnp.where(i < z, 1.0, 0.0)
    for copy in waits:
        copy.wait_recv()
    ys[y] = plane_sum[...]
    for i in range(groups):
        total = total + ys[i].astype(F32) * jnp.where(i < y, 1.0, 0.0)
    for i in range(WAYS):
        back[i] = total.astype(BF16)
        total = total + xs[i].astype(F32)
    heads_in[x] = back[x]
    waits = [go(back.at[(x + d) % WAYS], heads_in.at[x], along_x[d - 1]) for d in range(1, WAYS)]
    for copy in waits:
        copy.wait_recv()
    swap = go(heads_in, sib2, sibling)
    later = jnp.where(c == 1, 1.0, 0.0)
    for i in range(WAYS):
        mixed = heads_in[i].astype(F32) + sib[base + i].astype(F32) * later
        out_ref[base + i] = mixed.astype(BF16)
    swap.wait_recv()
    base = (1 - c) * WAYS
    for i in range(WAYS):
        mixed = sib2[i].astype(F32) + sib[base + i].astype(F32) * later
        out_ref[base + i] = mixed.astype(BF16)
    for copy in copies:
        copy.wait_send()


def prefix(state, groups):
    one = (STATE, HEAD_DIM)
    some = (WAYS,) + one
    count = 2 + 2 * (WAYS - 1) + (WAYS - 1) + groups - 1
    return pl.pallas_call(
        functools.partial(prefix_kernel, groups),
        out_shape=jax.ShapeDtypeStruct(state.shape, BF16),
        in_specs=[pl.BlockSpec(memory_space=pltpu.VMEM)],
        out_specs=pl.BlockSpec(memory_space=pltpu.VMEM),
        scratch_shapes=[
            pltpu.VMEM(state.shape, BF16),
            pltpu.VMEM(state.shape, BF16),
            pltpu.VMEM(some, BF16),
            pltpu.VMEM(some, BF16),
            pltpu.VMEM(one, BF16),
            pltpu.VMEM(some, BF16),
            pltpu.VMEM(one, BF16),
            pltpu.VMEM((groups,) + one, BF16),
            pltpu.VMEM(some, BF16),
            pltpu.VMEM(some, BF16),
            pltpu.VMEM(some, BF16),
            pltpu.SemaphoreType.DMA((count,)),
            pltpu.SemaphoreType.DMA((count,)),
        ],
        compiler_params=pltpu.CompilerParams(collective_id=0, has_side_effects=True),
        name="prefix",
    )(state)


def attend_kernel(
    x_ref, q_ref, k_ref, v_ref, prior_ref, hgain_ref, wout_ref, fgain_ref, resid_ref, ffn_ref, ratio
):
    tokens = x_ref.shape[0]
    tiles = tokens // ROWS
    causal = lax.broadcasted_iota(jnp.int32, (ROWS, ROWS), 0) >= lax.broadcasted_iota(
        jnp.int32, (ROWS, ROWS), 1
    )

    @pl.loop(0, HEADS)
    def _(head):
        cols = pl.ds(pl.multiple_of(head * HEAD_DIM, HEAD_DIM), HEAD_DIM)
        keys = k_ref[:, cols]
        wide = jnp.concatenate([v_ref[:, cols], jnp.ones((tokens, HEAD_DIM), BF16)], axis=1)
        prior = prior_ref[head]
        counts = jnp.broadcast_to(prior[HEAD_DIM : HEAD_DIM + 1, :], (HEAD_DIM, HEAD_DIM))
        carried = jnp.concatenate([prior[:HEAD_DIM, :], counts], axis=0)
        for tile in range(tiles):
            rows = slice(tile * ROWS, (tile + 1) * ROWS)
            query = q_ref[rows, cols]
            numer = dot_last(query, carried)
            scores = jnp.where(causal, dot_last(query, keys[rows, :]), 0.0).astype(BF16)
            numer = numer + jnp.dot(scores, wide[rows, :], preferred_element_type=F32)
            if tile > 0:
                scores = dot_last(query, keys[: tile * ROWS, :]).astype(BF16)
                numer = numer + jnp.dot(
                    scores, wide[: tile * ROWS, :], preferred_element_type=F32
                )
            ratio[rows, cols] = numer[:, :HEAD_DIM] / numer[:, HEAD_DIM:]

    half = tokens // 2
    for part in range(2):
        rows = slice(part * half, (part + 1) * half)
        attended = norm_rows(ratio[rows, :], hgain_ref[...]).astype(BF16)
        resid = x_ref[rows, :].astype(F32) + jnp.dot(
            attended, wout_ref[...], preferred_element_type=F32
        )
        resid = resid.astype(BF16)
        resid_ref[rows, :] = resid
        ffn_ref[rows, :] = norm_rows(resid.astype(F32), fgain_ref[...]).astype(BF16)


def attend(x, q, k, v, prior, head_gain, w_out, ffn_gain):
    tokens, width = x.shape
    return pl.pallas_call(
        attend_kernel,
        out_shape=[jax.ShapeDtypeStruct((tokens, width), BF16)] * 2,
        in_specs=[pl.BlockSpec(memory_space=pltpu.VMEM)] * 8,
        out_specs=[pl.BlockSpec(memory_space=pltpu.VMEM)] * 2,
        scratch_shapes=[pltpu.VMEM((tokens, width), F32)],
        compiler_params=pltpu.CompilerParams(vmem_limit_bytes=LIMIT_BYTES),
        name="attend",
    )(x, q, k, v, prior, head_gain, w_out, ffn_gain)


def neighbours():
    y, z, x, c = place()
    lane = WAYS * CORES

    def at(zz, xx, cc):
        return (y, ((zz + WAYS) % WAYS) * lane + ((xx + WAYS) % WAYS) * CORES + cc)

    return (
        at(z, x, 1 - c), at(z, x + 1, c), at(z, x - 1, c), at(z + 1, x, c), at(z - 1, x, c)
    )


def dispatch_kernel(blocks, table, f_ref, out_ref, *rest):
    chunks = out_ref.shape[0]
    depth = out_ref.shape[2]
    gather = rest[:chunks]
    stage, relay, local, send, recv = rest[chunks:]
    y, z, x, c = place()
    sibling, right, left, up, down = neighbours()
    greet([sibling, right, left, up, down])
    me = (x * CORES + c) * blocks
    from_left = (((x + WAYS - 1) % WAYS) * CORES + c) * blocks
    from_right = (((x + 1) % WAYS) * CORES + c) * blocks
    from_far = (((x + 2) % WAYS) * CORES + c) * blocks
    pending = []

    def go(k, n, src, dst, device):
        copy = remote(src, dst, send.at[k, n], recv.at[k, n], device)
        copy.start()
        pending.append(copy)
        return copy

    made = {}

    def begin(k):
        own = f_ref.at[:, pl.ds(k * depth, depth), :]
        here = gather[k].at[pl.ds(me, blocks)]
        made[k, 0] = go(k, 0, own, here, right)
        made[k, 1] = go(k, 1, own, here, left)
        made[k, 2] = go(k, 2, own, here, sibling)
        keep = pltpu.make_async_copy(own, here, local.at[k])
        keep.start()
        made[k, "keep"] = keep

    def spread(k):
        def pass_on(n, start):
            part = gather[k].at[pl.ds(start, blocks)]
            made[k, n] = go(k, n, part, part, sibling)

        first, second = (0, 1) if k % 2 == 0 else (1, 0)
        nearer, farther = (from_left, from_right) if k % 2 == 0 else (from_right, from_left)
        made[k, first].wait_recv()
        part = gather[k].at[pl.ds(nearer, blocks)]
        made[k, 3] = go(k, 3, part, part, right if k % 2 == 0 else left)
        if k + 2 < chunks:
            begin(k + 2)
        pass_on(4, nearer) if k % 2 == 0 else pass_on(5, nearer)
        made[k, second].wait_recv()
        pass_on(5, farther) if k % 2 == 0 else pass_on(4, farther)
        made[k, 3].wait_recv()
        pass_on(6, from_far)

    def select(k):
        made[k, "keep"].wait()
        for n in (2, 4, 5, 6):
            made[k, n].wait_recv()
        for d in (2, 1, 3, 0):
            target = (z + d) % WAYS
            for j in range(SLOTS):
                rows = gather[k][table[target * SLOTS + j]]
                if d == 0:
                    out_ref[k, z * SLOTS + j] = rows
                else:
                    stage[k, d - 1, j] = rows
            if d == 2:
                made[k, 7] = go(k, 7, stage.at[k, 1], relay.at[k], up if k % 2 == 0 else down)
            if d == 1:
                made[k, 8] = go(k, 8, stage.at[k, 0], out_ref.at[k, pl.ds(z * SLOTS, SLOTS)], up)
            if d == 3:
                made[k, 9] = go(k, 9, stage.at[k, 2], out_ref.at[k, pl.ds(z * SLOTS, SLOTS)], down)

    def forward(k):
        made[k, 7].wait_recv()
        origin = (z + WAYS - 1) % WAYS if k % 2 == 0 else (z + 1) % WAYS
        made[k, 10] = go(
            k, 10, relay.at[k], out_ref.at[k, pl.ds(origin * SLOTS, SLOTS)],
            up if k % 2 == 0 else down,
        )

    begin(0)
    if chunks > 1:
        begin(1)
    for step in range(chunks + 2):
        if step < chunks:
            spread(step)
        if 1 <= step <= chunks:
            select(step - 1)
        if step >= 2:
            forward(step - 2)
    for k in range(chunks):
        for n in (8, 9, 10):
            made[k, n].wait_recv()
    for copy in pending:
        copy.wait_send()


def dispatch(table, ffn_in):
    blocks, rows, width = ffn_in.shape
    chunks = CHUNKS
    depth = rows // chunks
    slots = WAYS * SLOTS
    row = WAYS * CORES * blocks
    return pl.pallas_call(
        functools.partial(dispatch_kernel, blocks),
        out_shape=jax.ShapeDtypeStruct((chunks, slots, depth, width), BF16),
        in_specs=[
            pl.BlockSpec(memory_space=pltpu.SMEM),
            pl.BlockSpec(memory_space=pltpu.VMEM),
        ],
        out_specs=pl.BlockSpec(memory_space=pltpu.VMEM),
        scratch_shapes=[pltpu.VMEM((row, depth, width), BF16)] * chunks
        + [
            pltpu.VMEM((chunks, WAYS - 1, SLOTS, depth, width), BF16),
            pltpu.VMEM((chunks, SLOTS, depth, width), BF16),
            pltpu.SemaphoreType.DMA((chunks,)),
            pltpu.SemaphoreType.DMA((chunks, 11)),
            pltpu.SemaphoreType.DMA((chunks, 11)),
        ],
        compiler_params=pltpu.CompilerParams(
            collective_id=1, has_side_effects=True, vmem_limit_bytes=LIMIT_BYTES
        ),
        name="dispatch",
    )(table, ffn_in)


def combine_kernel(
    blocks, index, weight, hot_index, hot_weight, res_ref, resid_ref, hot_ref, out_ref, *rest
):
    chunks, slots, depth, width = res_ref.shape
    results = rest[:chunks]
    partial, relay, merge, final, local, send, recv = rest[chunks:]
    y, z, x, c = place()
    sibling, right, left, up, down = neighbours()
    greet([sibling, right, left, up, down])
    pending = []
    made = {}

    def go(k, n, src, dst, device):
        copy = remote(src, dst, send.at[k, n], recv.at[k, n], device)
        copy.start()
        pending.append(copy)
        made[k, n] = copy

    def slot(row):
        return pl.ds(c * slots + row * SLOTS, SLOTS)

    def part(row):
        return pl.ds(((row + WAYS) % WAYS) * SLOTS, SLOTS)

    def begin(k):
        far = up if k % 2 == 0 else down
        go(k, 2, res_ref.at[k, part(z + 2)], relay.at[k], far)
        go(k, 0, res_ref.at[k, part(z + 1)], results[k].at[slot(z)], up)
        go(k, 1, res_ref.at[k, part(z - 1)], results[k].at[slot(z)], down)
        keep = pltpu.make_async_copy(res_ref.at[k, part(z)], results[k].at[slot(z)], local.at[k])
        keep.start()
        made[k, "keep"] = keep

    def share(k):
        made[k, 2].wait_recv()
        origin = (z + WAYS - 1) % WAYS if k % 2 == 0 else (z + 1) % WAYS
        go(k, 3, relay.at[k], results[k].at[slot(origin)], up if k % 2 == 0 else down)
        if k + 2 < chunks:
            begin(k + 2)
        made[k, "keep"].wait()
        for n in (0, 1, 3):
            made[k, n].wait_recv()
        here = results[k].at[pl.ds(c * slots, slots)]
        go(k, 4, here, here, sibling)

    def build(k):
        made[k, 4].wait_recv()

        def one(n, carry):
            first = results[k][index[2 * n]].astype(F32) * weight[2 * n]
            second = results[k][index[2 * n + 1]].astype(F32) * weight[2 * n + 1]
            partial[k, n] = (first + second).astype(BF16)
            return carry

        def ways(d):
            return partial.at[k, pl.ds(d * blocks, blocks)]

        lax.fori_loop(2 * blocks, 3 * blocks, one, 0)
        go(k, 5, ways(2), merge.at[k], right if k % 2 == 0 else left)
        if k % 2 == 0:
            lax.fori_loop(3 * blocks, 4 * blocks, one, 0)
            go(k, 7, ways(3), final.at[k, 1], left)
            lax.fori_loop(0, 2 * blocks, one, 0)
        else:
            lax.fori_loop(blocks, 2 * blocks, one, 0)
            go(k, 6, ways(1), final.at[k, 0], right)
            lax.fori_loop(3 * blocks, 4 * blocks, one, 0)
            lax.fori_loop(0, blocks, one, 0)

    def join(k):
        made[k, 5].wait_recv()
        d = 1 if k % 2 == 0 else 3

        def one(b, carry):
            there = d * blocks + b
            partial[k, there] = (
                partial[k, there].astype(F32) + merge[k, b].astype(F32)
            ).astype(BF16)
            return carry

        lax.fori_loop(0, blocks, one, 0)
        ready = partial.at[k, pl.ds(d * blocks, blocks)]
        if k % 2 == 0:
            go(k, 6, ready, final.at[k, 0], right)
        else:
            go(k, 7, ready, final.at[k, 1], left)

    def finish(k):
        made[k, 6].wait_recv()
        made[k, 7].wait_recv()
        rows = slice(k * depth, (k + 1) * depth)

        def one(b, carry):
            total = resid_ref[b, rows, :].astype(F32) + partial[k, b].astype(F32)
            total = total + final[k, 0, b].astype(F32) + final[k, 1, b].astype(F32)
            total = total + hot_ref[hot_index[b]][rows, :].astype(F32) * hot_weight[b]
            out_ref[b, rows, :] = total.astype(BF16)
            return carry

        lax.fori_loop(0, blocks, one, 0)

    begin(0)
    if chunks > 1:
        begin(1)
    for step in range(chunks + 3):
        if step < chunks:
            share(step)
        if 1 <= step <= chunks:
            build(step - 1)
        if 2 <= step <= chunks + 1:
            join(step - 2)
        if step >= 3:
            finish(step - 3)
    for copy in pending:
        copy.wait_send()


def combine(tables, results, resid, hot_out):
    chunks, slots, depth, width = results.shape
    blocks = resid.shape[0]
    return pl.pallas_call(
        functools.partial(combine_kernel, blocks),
        out_shape=jax.ShapeDtypeStruct(resid.shape, BF16),
        in_specs=[pl.BlockSpec(memory_space=pltpu.SMEM)] * 4
        + [pl.BlockSpec(memory_space=pltpu.VMEM)] * 3,
        out_specs=pl.BlockSpec(memory_space=pltpu.VMEM),
        scratch_shapes=[pltpu.VMEM((CORES * slots, depth, width), BF16)] * chunks
        + [
            pltpu.VMEM((chunks, WAYS * blocks, depth, width), BF16),
            pltpu.VMEM((chunks, SLOTS, depth, width), BF16),
            pltpu.VMEM((chunks, blocks, depth, width), BF16),
            pltpu.VMEM((chunks, 2, blocks, depth, width), BF16),
            pltpu.SemaphoreType.DMA((chunks,)),
            pltpu.SemaphoreType.DMA((chunks, 8)),
            pltpu.SemaphoreType.DMA((chunks, 8)),
        ],
        compiler_params=pltpu.CompilerParams(
            collective_id=2, has_side_effects=True, vmem_limit_bytes=LIMIT_BYTES
        ),
        name="combine",
    )(*tables, results, resid, hot_out)


def expert_kernel(x_ref, gate_ref, up_ref, down_ref, out_ref):
    rows = x_ref[...]
    gate = jnp.dot(rows, gate_ref[...], preferred_element_type=F32)
    upper = jnp.dot(rows, up_ref[...], preferred_element_type=F32)
    inner = (jax.nn.silu(gate) * upper).astype(BF16)
    out_ref[...] = jnp.dot(inner, down_ref[...], preferred_element_type=F32).astype(BF16)


def experts(rows, w_gate, w_up, w_down, step):
    count, width = rows.shape
    hidden = w_gate.shape[1]
    once = pl.Buffered(1)
    return pl.pallas_call(
        expert_kernel,
        grid=(count // step,),
        out_shape=jax.ShapeDtypeStruct((count, width), BF16),
        in_specs=[
            pl.BlockSpec((step, width), lambda i: (i, 0)),
            pl.BlockSpec((width, hidden), lambda i: (0, 0), pipeline_mode=once),
            pl.BlockSpec((width, hidden), lambda i: (0, 0), pipeline_mode=once),
            pl.BlockSpec((hidden, width), lambda i: (0, 0), pipeline_mode=once),
        ],
        out_specs=pl.BlockSpec((step, width), lambda i: (i, 0)),
        compiler_params=pltpu.CompilerParams(vmem_limit_bytes=LIMIT_BYTES),
        name="experts",
    )(rows, w_gate, w_up, w_down)


def hot_kernel(pick, x_ref, gate_ref, up_ref, down_ref, out_ref):
    expert_kernel(x_ref.at[0], gate_ref, up_ref, down_ref, out_ref.at[0])


def hot_experts(pick, ffn_in, w_gate, w_up, w_down):
    blocks, rows, width = ffn_in.shape
    hidden = w_gate.shape[1]
    return pl.pallas_call(
        hot_kernel,
        grid_spec=pltpu.PrefetchScalarGridSpec(
            num_scalar_prefetch=1,
            grid=(2,),
            in_specs=[
                pl.BlockSpec((1, rows, width), lambda i, pick: (pick[i], 0, 0)),
                pl.BlockSpec((width, hidden), lambda i, pick: (0, 0)),
                pl.BlockSpec((width, hidden), lambda i, pick: (0, 0)),
                pl.BlockSpec((hidden, width), lambda i, pick: (0, 0)),
            ],
            out_specs=pl.BlockSpec((1, rows, width), lambda i, pick: (i, 0, 0)),
        ),
        out_shape=jax.ShapeDtypeStruct((2, rows, width), BF16),
        compiler_params=pltpu.CompilerParams(vmem_limit_bytes=LIMIT_BYTES),
        name="hot_experts",
    )(pick, ffn_in, w_gate, w_up, w_down)


def routing(pair_ids, gate_codes):
    y, z, x, c = place()
    blocks = pair_ids.shape[0]
    row = WAYS * CORES * blocks * 2
    mine = jnp.concatenate([pair_ids, gate_codes], axis=1)
    everyone = lax.all_gather(mine, ("grp", "seq"))
    ids = everyone[:, :, :2].reshape(-1, row)
    groups = ids.shape[0] // WAYS
    owners = lax.axis_size("seq")
    before = lax.broadcasted_iota(jnp.int32, (row, row), 1) < lax.broadcasted_iota(
        jnp.int32, (row, row), 0
    )
    same = ids[:, :, None] == ids[:, None, :]
    rank = jnp.sum((same & before[None]).astype(jnp.int32), axis=2)
    numbers = jnp.arange(owners, dtype=jnp.int32)
    counts = jnp.sum(
        (ids.reshape(groups, -1)[:, :, None] == numbers[None, None, :]).astype(jnp.int32), axis=1
    )
    hot = jnp.argmax(counts, axis=1).astype(jnp.int32)
    cold = ids != jnp.repeat(hot, WAYS)[:, None]
    rounds = jnp.max(jnp.where(cold, rank, 0)) // SLOTS + 1
    my_hot = hot[y]
    my_ids = ids[y * WAYS + z]
    my_rank = rank[y * WAYS + z]
    codes = everyone[:, :, 2:].reshape(-1, row)[y * WAYS + z].reshape(-1, 2).astype(F32)
    shares = codes / jnp.sum(codes, axis=1, keepdims=True)
    own_hot = pair_ids == my_hot
    own_codes = gate_codes.astype(F32)
    own_shares = own_codes / jnp.sum(own_codes, axis=1, keepdims=True)
    hot_weight = jnp.sum(jnp.where(own_hot, own_shares, 0.0), axis=1)
    any_hot = jnp.any(own_hot, axis=1).astype(jnp.int32)
    hot_index = jnp.clip(jnp.cumsum(any_hot) - any_hot, 0, 1)
    numbers = jnp.arange(blocks, dtype=jnp.int32)
    pick = jnp.stack(
        [jnp.sum(numbers * any_hot * (hot_index == i).astype(jnp.int32)) for i in range(2)]
    )
    return my_ids, my_rank, shares, my_hot, rounds, hot_weight, hot_index, pick


def round_tables(info, turn, blocks):
    y, z, x, c = place()
    my_ids, my_rank, shares, my_hot = info
    visits = my_ids.shape[0]
    place_of = my_rank - turn * SLOTS
    usable = (my_ids != my_hot) & (place_of >= 0) & (place_of < SLOTS)
    slots = jnp.arange(WAYS * SLOTS, dtype=jnp.int32)
    expert = (slots // SLOTS) * (WAYS * CORES) + x * CORES + c
    hit = (
        (my_ids[None, :] == expert[:, None])
        & (place_of[None, :] == (slots % SLOTS)[:, None])
        & usable[None, :]
    )
    block = jnp.arange(visits, dtype=jnp.int32) // 2
    source = jnp.sum(jnp.where(hit, block[None, :], 0), axis=1)
    here = usable & ((my_ids // CORES) % WAYS == x)
    index = (my_ids % CORES) * (WAYS * SLOTS) + (my_ids // (WAYS * CORES)) * SLOTS + place_of
    index = jnp.where(here, index, 0)
    weight = jnp.where(here, shares.reshape(-1), 0.0)
    order = (x + jnp.arange(WAYS, dtype=jnp.int32)) % WAYS

    def mine(values):
        values = values.reshape(WAYS, CORES, blocks * 2)
        values = lax.dynamic_index_in_dim(values, c, 1, False)
        return jnp.take(values, order, axis=0).reshape(-1)

    return source, mine(index), mine(weight)


def body(
    hidden_in, attn_gain, w_qkv, head_gain, w_out, ffn_gain, w_gate, w_up, w_down, pair_ids, gate_codes
):
    tokens, width = hidden_in.shape
    blocks = tokens // ROWS
    groups = lax.axis_size("grp")
    my_ids, my_rank, shares, my_hot, rounds, hot_weight, hot_index, pick = routing(
        pair_ids, gate_codes
    )
    info = (my_ids, my_rank, shares, my_hot)
    is_mine = lax.axis_index("seq") == my_hot
    hot_weights = [
        lax.psum(jnp.where(is_mine, w[0], jnp.zeros_like(w[0])), "seq") for w in (w_gate, w_up, w_down)
    ]
    q, k, v, state = qkv(hidden_in, attn_gain[None], w_qkv)
    prior = prefix(state, groups)
    resid, ffn_in = attend(
        hidden_in, q, k, v, prior, head_gain[None], w_out, ffn_gain[None]
    )
    resid = resid.reshape(blocks, ROWS, width)
    ffn_in = ffn_in.reshape(blocks, ROWS, width)

    def turn_of(turn, base, hot_out, hot_weight):
        source, index, weight = round_tables(info, turn, blocks)
        arrived = dispatch(source, ffn_in)
        shape = arrived.shape
        result = experts(arrived.reshape(-1, width), w_gate[0], w_up[0], w_down[0], 512)
        return combine((index, weight, hot_index, hot_weight), result.reshape(shape), base, hot_out)

    hot_out = hot_experts(pick, ffn_in, *hot_weights)
    total = turn_of(0, resid, hot_out, hot_weight)

    def more(total):
        none = jnp.zeros_like(hot_weight)
        return lax.fori_loop(
            1, -(-LIMIT // SLOTS), lambda turn, t: turn_of(turn, t, hot_out, none), total
        )

    total = lax.cond(rounds > 1, more, lambda total: total, total)
    return total.reshape(tokens, width)


def solution(mesh):
    return jax.shard_map(
        body,
        mesh=mesh,
        in_specs=(
            P(("grp", "seq"), None), P(), P(), P(), P(), P(),
            P("seq", None, None), P("seq", None, None), P("seq", None, None),
            P(("grp", "seq"), None), P(("grp", "seq"), None),
        ),
        out_specs=P(("grp", "seq"), None),
        check_vma=False,
    )
```

```python
import functools

import jax
import jax.numpy as jnp
from jax import lax
from jax.experimental import pallas as pl
from jax.experimental.pallas import tpu as pltpu
from jax.sharding import PartitionSpec as P

HEADS = 8
HEAD_DIM = 128
ROWS = 128
EPS = 1e-06
WAYS = 4
CORES = 2
SLOTS = 2
SIDES = 2
PART = SIDES * SLOTS
CHUNKS = 8
STATE = 144
LIMIT = 8
LANES = 128
HOT = 15
MESH = pl.DeviceIdType.MESH
F32 = jnp.float32
BF16 = jnp.bfloat16
LIMIT_BYTES = 60 * 1024 * 1024


def place():
    seq = lax.axis_index("seq")
    return lax.axis_index("grp"), seq // (WAYS * CORES), (seq // CORES) % WAYS, seq % CORES


def remote(src, dst, send, recv, device):
    return pltpu.make_async_remote_copy(
        src_ref=src, dst_ref=dst, send_sem=send, recv_sem=recv, device_id=device, device_id_type=MESH
    )


def greet(devices):
    barrier = pltpu.get_barrier_semaphore()
    for device in devices:
        pl.semaphore_signal(barrier, inc=1, device_id=device, device_id_type=MESH)
    pl.semaphore_wait(barrier, len(devices))


def norm_rows(values, gain):
    return values * lax.rsqrt(jnp.mean(values * values, axis=-1, keepdims=True) + EPS) * gain


def dot_last(a, b):
    return lax.dot_general(a, b, (((1,), (1,)), ((), ())), preferred_element_type=F32)


def dot_first(a, b):
    return lax.dot_general(a, b, (((0,), (0,)), ((), ())), preferred_element_type=F32)


def lifted(values):
    return jnp.where(values > 0.0, values + 1.0, jnp.exp(jnp.minimum(values, 0.0))).astype(BF16)


def qkv_kernel(x_ref, gain_ref, wq_ref, wk_ref, wv_ref, q_ref, k_ref, v_ref, st_ref, normed):
    tokens = x_ref.shape[0]

    @pl.when(pl.program_id(0) == 0)
    def _():
        @pl.loop(0, tokens // ROWS)
        def _(i):
            rows = pl.ds(pl.multiple_of(i * ROWS, ROWS), ROWS)
            normed[rows, :] = norm_rows(x_ref[rows, :].astype(F32), gain_ref[...]).astype(BF16)

    q_ref[...] = lifted(jnp.dot(normed[...], wq_ref[...], preferred_element_type=F32))
    k_ref[...] = lifted(jnp.dot(normed[...], wk_ref[...], preferred_element_type=F32))
    v_ref[...] = jnp.dot(normed[...], wv_ref[...], preferred_element_type=F32).astype(BF16)
    for head in range(q_ref.shape[1] // HEAD_DIM):
        cols = slice(head * HEAD_DIM, (head + 1) * HEAD_DIM)
        keys = k_ref[:, cols]
        st_ref[head, :HEAD_DIM, :] = dot_first(v_ref[:, cols], keys)
        total = jnp.sum(keys.astype(F32), axis=0, keepdims=True)
        st_ref[head, HEAD_DIM:, :] = jnp.broadcast_to(total, (STATE - HEAD_DIM, HEAD_DIM))


def qkv(x, gain, w_qkv):
    tokens, width = x.shape
    step = 2 * HEAD_DIM
    steps = width // step
    column = pl.BlockSpec((tokens, step), lambda j: (0, j))
    return pl.pallas_call(
        qkv_kernel,
        grid=(steps,),
        out_shape=[jax.ShapeDtypeStruct((tokens, width), BF16)] * 3
        + [jax.ShapeDtypeStruct((width // HEAD_DIM, STATE, HEAD_DIM), F32)],
        in_specs=[
            pl.BlockSpec((tokens, width), lambda j: (0, 0)),
            pl.BlockSpec((1, width), lambda j: (0, 0)),
            pl.BlockSpec((width, step), lambda j: (0, j)),
            pl.BlockSpec((width, step), lambda j: (0, steps + j)),
            pl.BlockSpec((width, step), lambda j: (0, 2 * steps + j)),
        ],
        out_specs=[column] * 3 + [pl.BlockSpec((2, STATE, HEAD_DIM), lambda j: (j, 0, 0))],
        scratch_shapes=[pltpu.VMEM((tokens, width), BF16)],
        compiler_params=pltpu.CompilerParams(vmem_limit_bytes=LIMIT_BYTES),
        name="qkv",
    )(x, gain, w_qkv, w_qkv, w_qkv)


def prefix_kernel(
    groups, st_ref, out_ref, mine, sib, chips, xs, row_sum, zs, plane_sum, ys, back, heads_in, sib2,
    send, recv,
):
    y, z, x, c = place()
    lane = WAYS * CORES

    def at(yy, zz, xx, cc):
        return (yy, zz * lane + xx * CORES + cc)

    sibling = at(y, z, x, 1 - c)
    along_x = [at(y, z, (x + d) % WAYS, c) for d in range(1, WAYS)]
    along_z = [at(y, (z + d) % WAYS, x, c) for d in range(1, WAYS)]
    along_y = [at((y + d) % groups, z, x, c) for d in range(1, groups)]
    greet([sibling] + along_x + along_z + along_y)
    copies = []

    def go(src, dst, device):
        n = len(copies)
        copy = remote(src, dst, send.at[n], recv.at[n], device)
        copy.start()
        copies.append(copy)
        return copy

    mine[...] = st_ref[...].astype(BF16)
    swap = go(mine, sib, sibling)
    swap.wait_recv()
    base = c * WAYS
    for i in range(WAYS):
        chips[i] = (st_ref[base + i] + sib[base + i].astype(F32)).astype(BF16)
    xs[x] = chips[x]
    waits = [go(chips.at[(x + d) % WAYS], xs.at[x], along_x[d - 1]) for d in range(1, WAYS)]
    for copy in waits:
        copy.wait_recv()
    row_sum[...] = sum(xs[i].astype(F32) for i in range(WAYS)).astype(BF16)
    zs[z] = row_sum[...]
    waits = [go(row_sum, zs.at[z], along_z[d - 1]) for d in range(1, WAYS)]
    for copy in waits:
        copy.wait_recv()
    plane_sum[...] = sum(zs[i].astype(F32) for i in range(WAYS)).astype(BF16)
    waits = [go(plane_sum, ys.at[y], along_y[d - 1]) for d in range(1, groups)]
    total = jnp.zeros(row_sum.shape, F32)
    for i in range(WAYS):
        total = total + zs[i].astype(F32) * jnp.where(i < z, 1.0, 0.0)
    for copy in waits:
        copy.wait_recv()
    ys[y] = plane_sum[...]
    for i in range(groups):
        total = total + ys[i].astype(F32) * jnp.where(i < y, 1.0, 0.0)
    for i in range(WAYS):
        back[i] = total.astype(BF16)
        total = total + xs[i].astype(F32)
    heads_in[x] = back[x]
    waits = [go(back.at[(x + d) % WAYS], heads_in.at[x], along_x[d - 1]) for d in range(1, WAYS)]
    for copy in waits:
        copy.wait_recv()
    swap = go(heads_in, sib2, sibling)
    later = jnp.where(c == 1, 1.0, 0.0)
    for i in range(WAYS):
        mixed = heads_in[i].astype(F32) + sib[base + i].astype(F32) * later
        out_ref[base + i] = mixed.astype(BF16)
    swap.wait_recv()
    base = (1 - c) * WAYS
    for i in range(WAYS):
        mixed = sib2[i].astype(F32) + sib[base + i].astype(F32) * later
        out_ref[base + i] = mixed.astype(BF16)
    for copy in copies:
        copy.wait_send()


def prefix(state, groups):
    one = (STATE, HEAD_DIM)
    some = (WAYS,) + one
    count = 2 + 2 * (WAYS - 1) + (WAYS - 1) + groups - 1
    return pl.pallas_call(
        functools.partial(prefix_kernel, groups),
        out_shape=jax.ShapeDtypeStruct(state.shape, BF16),
        in_specs=[pl.BlockSpec(memory_space=pltpu.VMEM)],
        out_specs=pl.BlockSpec(memory_space=pltpu.VMEM),
        scratch_shapes=[
            pltpu.VMEM(state.shape, BF16),
            pltpu.VMEM(state.shape, BF16),
            pltpu.VMEM(some, BF16),
            pltpu.VMEM(some, BF16),
            pltpu.VMEM(one, BF16),
            pltpu.VMEM(some, BF16),
            pltpu.VMEM(one, BF16),
            pltpu.VMEM((groups,) + one, BF16),
            pltpu.VMEM(some, BF16),
            pltpu.VMEM(some, BF16),
            pltpu.VMEM(some, BF16),
            pltpu.SemaphoreType.DMA((count,)),
            pltpu.SemaphoreType.DMA((count,)),
        ],
        compiler_params=pltpu.CompilerParams(collective_id=0, has_side_effects=True),
        name="prefix",
    )(state)


def attend_kernel(
    x_ref, q_ref, k_ref, v_ref, prior_ref, hgain_ref, wout_ref, fgain_ref, resid_ref, ffn_ref, ratio
):
    tokens = x_ref.shape[0]
    tiles = tokens // ROWS
    causal = lax.broadcasted_iota(jnp.int32, (ROWS, ROWS), 0) >= lax.broadcasted_iota(
        jnp.int32, (ROWS, ROWS), 1
    )

    @pl.loop(0, HEADS)
    def _(head):
        cols = pl.ds(pl.multiple_of(head * HEAD_DIM, HEAD_DIM), HEAD_DIM)
        keys = k_ref[:, cols]
        wide = jnp.concatenate([v_ref[:, cols], jnp.ones((tokens, HEAD_DIM), BF16)], axis=1)
        prior = prior_ref[head]
        counts = jnp.broadcast_to(prior[HEAD_DIM : HEAD_DIM + 1, :], (HEAD_DIM, HEAD_DIM))
        carried = jnp.concatenate([prior[:HEAD_DIM, :], counts], axis=0)
        for tile in range(tiles):
            rows = slice(tile * ROWS, (tile + 1) * ROWS)
            query = q_ref[rows, cols]
            numer = dot_last(query, carried)
            scores = jnp.where(causal, dot_last(query, keys[rows, :]), 0.0).astype(BF16)
            numer = numer + jnp.dot(scores, wide[rows, :], preferred_element_type=F32)
            if tile > 0:
                scores = dot_last(query, keys[: tile * ROWS, :]).astype(BF16)
                numer = numer + jnp.dot(
                    scores, wide[: tile * ROWS, :], preferred_element_type=F32
                )
            ratio[rows, cols] = numer[:, :HEAD_DIM] / numer[:, HEAD_DIM:]

    half = tokens // 2
    for part in range(2):
        rows = slice(part * half, (part + 1) * half)
        attended = norm_rows(ratio[rows, :], hgain_ref[...]).astype(BF16)
        resid = x_ref[rows, :].astype(F32) + jnp.dot(
            attended, wout_ref[...], preferred_element_type=F32
        )
        resid = resid.astype(BF16)
        resid_ref[rows, :] = resid
        ffn_ref[rows, :] = norm_rows(resid.astype(F32), fgain_ref[...]).astype(BF16)


def attend(x, q, k, v, prior, head_gain, w_out, ffn_gain):
    tokens, width = x.shape
    return pl.pallas_call(
        attend_kernel,
        out_shape=[jax.ShapeDtypeStruct((tokens, width), BF16)] * 2,
        in_specs=[pl.BlockSpec(memory_space=pltpu.VMEM)] * 8,
        out_specs=[pl.BlockSpec(memory_space=pltpu.VMEM)] * 2,
        scratch_shapes=[pltpu.VMEM((tokens, width), F32)],
        compiler_params=pltpu.CompilerParams(vmem_limit_bytes=LIMIT_BYTES),
        name="attend",
    )(x, q, k, v, prior, head_gain, w_out, ffn_gain)


def tables(turn, ids, rank, shares, hot, out_int, out_real):
    y, z, x, c = place()
    half = x // 2
    other = (x + 2 * (x % 2) - 1 + WAYS) % WAYS
    span = LANES * 7 // 16
    lane = lax.broadcasted_iota(jnp.int32, (1, LANES), 1)
    local = lane - half * span
    near = (local >= 0) & (local < span)
    place_of = rank - turn * SLOTS
    usable = near & (ids >= 0) & (ids != hot) & (place_of >= 0) & (place_of < SLOTS)
    slot = lax.broadcasted_iota(jnp.int32, (16, LANES), 0)
    column = jnp.where(slot >= 8, other, x)
    expert = ((slot & 7) >> 1) * (WAYS * CORES) + column * CORES + c
    key = jnp.where(usable, ids * SLOTS + place_of, -1)
    hit = key == expert * SLOTS + (slot & 1)
    source = jnp.sum(jnp.where(hit, local >> 1, 0).astype(F32), axis=1, keepdims=True)
    out_int[0:16, :] = jnp.broadcast_to(source, (16, LANES)).astype(jnp.int32)
    here = (ids >> 1) & 3
    which = jnp.where(here == other, 1, 0)
    mine = usable & ((here == x) | (here == other))
    index = (ids & 1) * 16 + which * 8 + (ids >> 3) * SLOTS + place_of
    out_int[16:17, :] = jnp.where(mine, index, 0)
    out_real[0:1, :] = jnp.where(mine, shares, 0.0)


def learn_kernel(
    groups, blocks, pairs, codes, int_ref, real_ref, chip, chips, row, rows, peak, peaks, send, recv, sib
):
    y, z, x, c = place()
    lane_count = WAYS * CORES

    def at(yy, zz, xx, cc):
        return (yy, zz * lane_count + xx * CORES + cc)

    sibling = at(y, z, x, 1 - c)
    along_x = [at(y, z, (x + d) % WAYS, c) for d in range(1, WAYS)]
    along_z = [at(y, (z + d) % WAYS, x, c) for d in range(1, WAYS)]
    along_y = [at((y + d) % groups, z, x, c) for d in range(1, groups)]
    greet([sibling] + along_x + along_z + along_y)
    copies = []

    def go(src, dst, device):
        n = len(copies)
        copy = remote(src, dst, send.at[n], recv.at[n], device)
        copy.start()
        copies.append(copy)
        return copy

    visits = 2 * blocks
    lane = lax.broadcasted_iota(jnp.int32, (8, LANES), 1)
    sub = lax.broadcasted_iota(jnp.int32, (8, LANES), 0)
    base = (x * CORES + c) * visits
    info = jnp.zeros((8, LANES), jnp.int32)
    for b in range(blocks):
        both = codes[b, 0] + codes[b, 1]
        for j in range(2):
            here = lane == base + (2 * b + j)
            value = jnp.where(sub == 0, pairs[b, j] + 1, jnp.where(sub == 1, codes[b, j], both))
            info = jnp.where(here & (sub < 3), value, info)
    chip[...] = info
    go(chip, sib, sibling).wait_recv()
    chips[x] = info + sib[...]
    for copy in [go(chips.at[x], chips.at[x], device) for device in along_x]:
        copy.wait_recv()
    mine = chips[0] + chips[1] + chips[2] + chips[3]
    rows[z] = mine
    for copy in [go(rows.at[z], rows.at[z], device) for device in along_z]:
        copy.wait_recv()
    expert = lax.broadcasted_iota(jnp.int32, (WAYS * lane_count, LANES), 0)
    lanes = lax.broadcasted_iota(jnp.int32, (WAYS * lane_count, LANES), 1)
    total = jnp.zeros((WAYS * lane_count, 1), F32)
    most = jnp.zeros((WAYS * lane_count, 1), F32)
    for i in range(WAYS):
        there = (rows[i][0:1, :] - 1) == expert
        first = jnp.sum(jnp.where(there & (lanes < 4 * visits), 1.0, 0.0), axis=1, keepdims=True)
        second = jnp.sum(jnp.where(there & (lanes >= 4 * visits), 1.0, 0.0), axis=1, keepdims=True)
        total = total + first + second
        most = jnp.maximum(most, jnp.maximum(first, second))
    is_hot = total > HOT - 0.5
    hot = jnp.sum(jnp.where(is_hot, expert[:, 0:1].astype(F32), 0.0), axis=0, keepdims=True)
    most = jnp.max(jnp.where(is_hot, 0.0, most), axis=0, keepdims=True)
    peaks[y] = jnp.broadcast_to(most, (8, LANES))
    waits = [go(peaks.at[y], peaks.at[y], device) for device in along_y]
    hot = jnp.broadcast_to(hot, (1, LANES)).astype(jnp.int32)
    ids = mine[0:1, :] - 1
    wide = jnp.broadcast_to(ids, (LANES, LANES))
    tall = wide.T
    rank_lane = lax.broadcasted_iota(jnp.int32, (LANES, LANES), 1)
    rank_sub = lax.broadcasted_iota(jnp.int32, (LANES, LANES), 0)
    earlier = (wide == tall) & (rank_sub < rank_lane)
    halves = (rank_sub < 4 * visits) == (rank_lane < 4 * visits)
    rank = jnp.sum(jnp.where(earlier & halves, 1.0, 0.0), axis=0, keepdims=True).astype(jnp.int32)
    shares = mine[1:2, :].astype(F32) / jnp.maximum(mine[2:3, :], 1).astype(F32)
    int_ref[16:24, :] = jnp.zeros((8, LANES), jnp.int32)
    real_ref[...] = jnp.zeros((8, LANES), F32)
    tables(0, ids, rank, shares, hot, int_ref, real_ref)
    lane = lane[0:1, :]
    own = (lane >= base) & (lane < base + visits) & (ids == hot)
    own_rank = jnp.zeros((1, LANES), jnp.int32)
    seen = jnp.sum(jnp.where(own, 1.0, 0.0), axis=1, keepdims=True)
    first_lane = jnp.min(jnp.where(own, lane, 1000).astype(F32), axis=1, keepdims=True)
    last_lane = jnp.max(jnp.where(own, lane, -1).astype(F32), axis=1, keepdims=True)
    int_ref[17:18, :] = ids
    int_ref[18:19, :] = rank
    int_ref[19:20, :] = hot
    int_ref[20:21, :] = own_rank
    first_block = jnp.where(seen > 0.5, (first_lane.astype(jnp.int32) - base) >> 1, 0)
    last_block = (last_lane.astype(jnp.int32) - base) >> 1
    following = jnp.where(first_block + 1 >= blocks, 0, first_block + 1)
    second_block = jnp.where(seen > 1.5, last_block, following)
    int_ref[21:22, :] = jnp.where(lane == 0, first_block, second_block)
    first_share = jnp.sum(
        jnp.where(own & (lane.astype(F32) == first_lane), shares, 0.0), axis=1, keepdims=True
    )
    last_share = jnp.sum(
        jnp.where(own & (lane.astype(F32) == last_lane) & (seen > 1.5), shares, 0.0),
        axis=1,
        keepdims=True,
    )
    real_ref[1:2, :] = shares
    real_ref[2:3, :] = jnp.where(lane == 0, first_share, last_share)
    for copy in waits:
        copy.wait_recv()
    top = peaks[0]
    for i in range(1, groups):
        top = jnp.maximum(top, peaks[i])
    int_ref[22:23, :] = top[0:1, :].astype(jnp.int32)
    for copy in copies:
        copy.wait_send()


def learn(pair_ids, gate_codes, groups):
    blocks = pair_ids.shape[0]
    tile = (8, LANES)
    count = 1 + 2 * (WAYS - 1) + groups - 1
    return pl.pallas_call(
        functools.partial(learn_kernel, groups, blocks),
        out_shape=[
            jax.ShapeDtypeStruct((24, LANES), jnp.int32),
            jax.ShapeDtypeStruct(tile, F32),
        ],
        in_specs=[pl.BlockSpec(memory_space=pltpu.SMEM)] * 2,
        out_specs=[pl.BlockSpec(memory_space=pltpu.VMEM)] * 2,
        scratch_shapes=[
            pltpu.VMEM(tile, jnp.int32),
            pltpu.VMEM((WAYS,) + tile, jnp.int32),
            pltpu.VMEM(tile, jnp.int32),
            pltpu.VMEM((WAYS,) + tile, jnp.int32),
            pltpu.VMEM(tile, F32),
            pltpu.VMEM((groups,) + tile, F32),
            pltpu.SemaphoreType.DMA((count,)),
            pltpu.SemaphoreType.DMA((count,)),
            pltpu.VMEM(tile, jnp.int32),
        ],
        compiler_params=pltpu.CompilerParams(collective_id=3, has_side_effects=True),
        name="learn",
    )(pair_ids, gate_codes)


def moe_kernel(
    blocks, chunks, table, weight, f_ref, base_ref, wg_ref, wu_ref, wd_ref, out_ref, *rest
):
    gather, landed = rest[:chunks], rest[chunks : 2 * chunks]
    (
        hand, zs, relay, taken, made_rows, relay_back, hand_back, partial, final, local, send, recv
    ) = rest[2 * chunks :]
    depth = ROWS // chunks
    width = f_ref.shape[2]
    y, z, x, c = place()
    lane = WAYS * CORES
    parity = x % 2

    def at(zz, xx, cc):
        return (y, ((zz + WAYS) % WAYS) * lane + ((xx + WAYS) % WAYS) * CORES + cc)

    sibling = at(z, x, 1 - c)
    mate = at(z, x + 1 - 2 * parity, c)
    across = at(z, x + 2 * parity - 1, c)
    up, down = at(z + 1, x, c), at(z - 1, x, c)
    greet([sibling, mate, across, up, down])
    me = parity * CORES + c
    friend = (1 - parity) * CORES + c
    pending = []
    made = {}

    def go(k, n, src, dst, device):
        copy = remote(src, dst, send.at[k, n], recv.at[k, n], device)
        copy.start()
        pending.append(copy)
        made[k, n] = copy

    def keep(k, n, src, dst):
        copy = pltpu.make_async_copy(src, dst, local.at[k, n])
        copy.start()
        made[k, "keep", n] = copy

    def arrived(k, *numbers):
        for n in numbers:
            made[k, n].wait_recv()

    def step_of(row):
        return (row + WAYS) % WAYS

    def begin(k):
        own = f_ref.at[:, pl.ds(k * depth, depth), :]
        here = gather[k].at[pl.ds(me * blocks, blocks)]
        go(k, 0, own, here, mate)
        go(k, 1, own, here, sibling)
        keep(k, 0, own, here)

    def widen(k):
        arrived(k, 0)
        there = gather[k].at[pl.ds(friend * blocks, blocks)]
        go(k, 2, there, there, sibling)

    def select(k):
        made[k, "keep", 0].wait()
        arrived(k, 1, 2)
        for row in range(WAYS):
            for j in range(SLOTS):
                hand[k, row, j] = gather[k][table[8 + row * SLOTS + j, 0]]
        go(k, 3, hand.at[k], zs.at[k, :, 1], across)
        for row in range(WAYS):
            for j in range(SLOTS):
                zs[k, row, 0, j] = gather[k][table[row * SLOTS + j, 0]]

    def climb(k):
        arrived(k, 3)
        far = up if k % 2 == 0 else down
        go(k, 6, zs.at[k, step_of(z + 2)], relay.at[k], far)
        go(k, 4, zs.at[k, step_of(z + 1)], taken.at[k, z], up)
        go(k, 5, zs.at[k, step_of(z - 1)], taken.at[k, z], down)
        keep(k, 1, zs.at[k, z], taken.at[k, z])

    def forward(k):
        arrived(k, 6)
        origin = step_of(z - 1) if k % 2 == 0 else step_of(z + 1)
        go(k, 7, relay.at[k], taken.at[k, origin], up if k % 2 == 0 else down)

    def work(k):
        arrived(k, 4, 5, 7)
        made[k, "keep", 1].wait()
        rows = taken[k].reshape(WAYS * PART * depth, width)
        gate = jnp.dot(rows, wg_ref[...], preferred_element_type=F32)
        upper = jnp.dot(rows, wu_ref[...], preferred_element_type=F32)
        inner = (jax.nn.silu(gate) * upper).astype(BF16)
        result = jnp.dot(inner, wd_ref[...], preferred_element_type=F32).astype(BF16)
        made_rows[k] = result.reshape(WAYS, SIDES, SLOTS, depth, width)
        far = up if k % 2 == 0 else down
        go(k, 12, made_rows.at[k, step_of(z + 2)], relay_back.at[k], far)
        for n, d, device in ((8, 1, up), (10, -1, down)):
            target = step_of(z + d)
            go(k, n, made_rows.at[k, target, 0], landed[k].at[pl.ds(c * 16 + z * SLOTS, SLOTS)], device)
            go(k, n + 1, made_rows.at[k, target, 1], hand_back.at[k, pl.ds(z * SLOTS, SLOTS)], device)
        keep(k, 2, made_rows.at[k, z, 0], landed[k].at[pl.ds(c * 16 + z * SLOTS, SLOTS)])
        keep(k, 3, made_rows.at[k, z, 1], hand_back.at[k, pl.ds(z * SLOTS, SLOTS)])

    def forward_back(k):
        arrived(k, 12)
        origin = step_of(z - 1) if k % 2 == 0 else step_of(z + 1)
        device = up if k % 2 == 0 else down
        go(k, 13, relay_back.at[k, 0], landed[k].at[pl.ds(c * 16 + origin * SLOTS, SLOTS)], device)
        go(k, 14, relay_back.at[k, 1], hand_back.at[k, pl.ds(origin * SLOTS, SLOTS)], device)

    def give(k):
        arrived(k, 9, 11, 14)
        made[k, "keep", 3].wait()
        go(k, 15, hand_back.at[k], landed[k].at[pl.ds(c * 16 + 8, 8)], across)
        arrived(k, 8, 10, 13)
        made[k, "keep", 2].wait()
        there = landed[k].at[pl.ds(c * 16, 8)]
        go(k, 16, there, there, sibling)

    def mirror(k):
        arrived(k, 15)
        there = landed[k].at[pl.ds(c * 16 + 8, 8)]
        go(k, 17, there, there, sibling)

    def build(k):
        arrived(k, 16, 17)

        def one(start, offset):
            def run(b, carry):
                first = start + 2 * b
                total = landed[k][table[16, first]].astype(F32) * weight[0, first]
                total = total + landed[k][table[16, first + 1]].astype(F32) * weight[0, first + 1]
                partial[k, offset + b] = total.astype(BF16)
                return carry

            return run

        row = (x // 2) * 4 * 2 * blocks
        lax.fori_loop(0, blocks, one(row + friend * 2 * blocks, blocks), 0)
        go(k, 18, partial.at[k, pl.ds(blocks, blocks)], final.at[k], mate)
        lax.fori_loop(0, blocks, one(row + me * 2 * blocks, 0), 0)

    def finish(k):
        arrived(k, 18)
        rows = slice(k * depth, (k + 1) * depth)

        def run(b, carry):
            total = base_ref[b, rows, :].astype(F32) + partial[k, b].astype(F32)
            out_ref[b, rows, :] = (total + final[k, b].astype(F32)).astype(BF16)
            return carry

        lax.fori_loop(0, blocks, run, 0)

    stages = [widen, select, climb, forward, work, forward_back, give, mirror, build, finish]
    begin(0)
    begin(1)
    for step in range(chunks + len(stages) - 1):
        if step + 2 < chunks:
            begin(step + 2)
        for lag in reversed(range(len(stages))):
            if 0 <= step - lag < chunks:
                stages[lag](step - lag)
    for copy in pending:
        copy.wait_send()


def moe(table, weight, ffn_in, base, w_gate, w_up, w_down):
    blocks, rows, width = ffn_in.shape
    chunks = CHUNKS
    depth = rows // chunks
    pair = 2 * CORES * blocks
    whole = pl.BlockSpec(memory_space=pltpu.VMEM)
    return pl.pallas_call(
        functools.partial(moe_kernel, blocks, chunks),
        out_shape=jax.ShapeDtypeStruct(base.shape, BF16),
        in_specs=[pl.BlockSpec(memory_space=pltpu.SMEM)] * 2 + [whole] * 5,
        out_specs=whole,
        scratch_shapes=[pltpu.VMEM((pair, depth, width), BF16)] * chunks
        + [pltpu.VMEM((CORES * 16, depth, width), BF16)] * chunks
        + [
            pltpu.VMEM((chunks, WAYS, SLOTS, depth, width), BF16),
            pltpu.VMEM((chunks, WAYS, SIDES, SLOTS, depth, width), BF16),
            pltpu.VMEM((chunks, SIDES, SLOTS, depth, width), BF16),
            pltpu.VMEM((chunks, WAYS, SIDES, SLOTS, depth, width), BF16),
            pltpu.VMEM((chunks, WAYS, SIDES, SLOTS, depth, width), BF16),
            pltpu.VMEM((chunks, SIDES, SLOTS, depth, width), BF16),
            pltpu.VMEM((chunks, WAYS * SLOTS, depth, width), BF16),
            pltpu.VMEM((chunks, 2 * blocks, depth, width), BF16),
            pltpu.VMEM((chunks, blocks, depth, width), BF16),
            pltpu.SemaphoreType.DMA((chunks, 4)),
            pltpu.SemaphoreType.DMA((chunks, 19)),
            pltpu.SemaphoreType.DMA((chunks, 19)),
        ],
        compiler_params=pltpu.CompilerParams(
            collective_id=1, has_side_effects=True, vmem_limit_bytes=67043328
        ),
        name="moe",
    )(table, weight, ffn_in, base, w_gate, w_up, w_down)


def hot_kernel(pick, share, x_ref, gate_ref, up_ref, down_ref, total_ref, out_ref):
    rows = x_ref[0]
    gate = jnp.dot(rows, gate_ref[...], preferred_element_type=F32)
    upper = jnp.dot(rows, up_ref[...], preferred_element_type=F32)
    inner = (jax.nn.silu(gate) * upper).astype(BF16)
    result = jnp.dot(inner, down_ref[...], preferred_element_type=F32).astype(BF16)
    weight = share[pl.program_id(0)]
    out_ref[0] = (total_ref[0].astype(F32) + result.astype(F32) * weight).astype(BF16)


def add_hot(pick, share, ffn_in, w_gate, w_up, w_down, total):
    blocks, rows, width = ffn_in.shape
    hidden = w_gate.shape[1]
    block = pl.BlockSpec((1, rows, width), lambda i, pick, share: (pick[i], 0, 0))
    return pl.pallas_call(
        hot_kernel,
        grid_spec=pltpu.PrefetchScalarGridSpec(
            num_scalar_prefetch=2,
            grid=(2,),
            in_specs=[
                block,
                pl.BlockSpec((width, hidden), lambda i, pick, share: (0, 0)),
                pl.BlockSpec((width, hidden), lambda i, pick, share: (0, 0)),
                pl.BlockSpec((hidden, width), lambda i, pick, share: (0, 0)),
                block,
            ],
            out_specs=block,
        ),
        out_shape=jax.ShapeDtypeStruct(total.shape, BF16),
        input_output_aliases={6: 0},
        compiler_params=pltpu.CompilerParams(vmem_limit_bytes=LIMIT_BYTES),
        name="add_hot",
    )(pick, share, ffn_in, w_gate, w_up, w_down, total)


def tables_kernel(turn, int_ref, real_ref, out_int, out_real):
    out_int[...] = int_ref[...]
    out_real[...] = real_ref[...]
    tables(
        turn[0], int_ref[17:18, :], int_ref[18:19, :], real_ref[1:2, :], int_ref[19:20, :],
        out_int, out_real,
    )


def later_tables(turn, ints, reals):
    return pl.pallas_call(
        tables_kernel,
        out_shape=[
            jax.ShapeDtypeStruct(ints.shape, ints.dtype),
            jax.ShapeDtypeStruct(reals.shape, reals.dtype),
        ],
        in_specs=[pl.BlockSpec(memory_space=pltpu.SMEM)]
        + [pl.BlockSpec(memory_space=pltpu.VMEM)] * 2,
        out_specs=[pl.BlockSpec(memory_space=pltpu.VMEM)] * 2,
        name="later_tables",
    )(turn, ints, reals)


def body(
    hidden_in, attn_gain, w_qkv, head_gain, w_out, ffn_gain, w_gate, w_up, w_down, pair_ids, gate_codes
):
    tokens, width = hidden_in.shape
    blocks = tokens // ROWS
    groups = lax.axis_size("grp")
    ints, reals = learn(pair_ids, gate_codes, groups)
    is_mine = lax.axis_index("seq") == ints[19, 0]
    hot_weights = [
        lax.psum(jnp.where(is_mine, w[0], jnp.zeros_like(w[0])), "seq") for w in (w_gate, w_up, w_down)
    ]
    q, k, v, state = qkv(hidden_in, attn_gain[None], w_qkv)
    prior = prefix(state, groups)
    resid, ffn_in = attend(
        hidden_in, q, k, v, prior, head_gain[None], w_out, ffn_gain[None]
    )
    resid = resid.reshape(blocks, ROWS, width)
    ffn_in = ffn_in.reshape(blocks, ROWS, width)
    weights = (w_gate[0], w_up[0], w_down[0])
    total = moe(ints, reals, ffn_in, resid, *weights)

    def more(total):
        def one(turn, total):
            later_ints, later_reals = later_tables(turn[None], ints, reals)
            return moe(later_ints, later_reals, ffn_in, total, *weights)

        return lax.fori_loop(1, -(-LIMIT // SLOTS), one, total)

    total = lax.cond(ints[22, 0] > SLOTS, more, lambda total: total, total)
    total = add_hot(ints[21, :2], reals[2, :2], ffn_in, *hot_weights, total)
    return total.reshape(tokens, width)


def solution(mesh):
    return jax.shard_map(
        body,
        mesh=mesh,
        in_specs=(
            P(("grp", "seq"), None), P(), P(), P(), P(), P(),
            P("seq", None, None), P("seq", None, None), P("seq", None, None),
            P(("grp", "seq"), None), P(("grp", "seq"), None),
        ),
        out_specs=P(("grp", "seq"), None),
        check_vma=False,
    )
```

```python
import functools

import jax
import jax.numpy as jnp
from jax import lax
from jax.experimental import pallas as pl
from jax.experimental.pallas import tpu as pltpu
from jax.sharding import PartitionSpec as P

HEADS = 8
HEAD_DIM = 128
ROWS = 128
EPS = 1e-06
WAYS = 4
CORES = 2
SLOTS = 2
SIDES = 2
PART = SIDES * SLOTS
CHUNKS = 8
STATE = 144
LIMIT = 8
LANES = 128
HALF = 512
SLICE = 64
PIECE = 16
HOT = 15
MESH = pl.DeviceIdType.MESH
F32 = jnp.float32
BF16 = jnp.bfloat16
LIMIT_BYTES = 60 * 1024 * 1024


def place():
    seq = lax.axis_index("seq")
    return lax.axis_index("grp"), seq // (WAYS * CORES), (seq // CORES) % WAYS, seq % CORES


def remote(src, dst, send, recv, device):
    return pltpu.make_async_remote_copy(
        src_ref=src, dst_ref=dst, send_sem=send, recv_sem=recv, device_id=device, device_id_type=MESH
    )


def greet(devices):
    barrier = pltpu.get_barrier_semaphore()
    for device in devices:
        pl.semaphore_signal(barrier, inc=1, device_id=device, device_id_type=MESH)
    pl.semaphore_wait(barrier, len(devices))


def norm_rows(values, gain):
    return values * lax.rsqrt(jnp.mean(values * values, axis=-1, keepdims=True) + EPS) * gain


def dot_last(a, b):
    return lax.dot_general(a, b, (((1,), (1,)), ((), ())), preferred_element_type=F32)


def dot_first(a, b):
    return lax.dot_general(a, b, (((0,), (0,)), ((), ())), preferred_element_type=F32)


def lifted(values):
    return jnp.where(values > 0.0, values + 1.0, jnp.exp(jnp.minimum(values, 0.0))).astype(BF16)


def tables(turn, ids, rank, shares, hot, out_int, out_real):
    y, z, x, c = place()
    half = x // 2
    other = (x + 2 * (x % 2) - 1 + WAYS) % WAYS
    span = LANES * 7 // 16
    lane = lax.broadcasted_iota(jnp.int32, (1, LANES), 1)
    local = lane - half * span
    near = (local >= 0) & (local < span)
    place_of = rank - turn * SLOTS
    usable = near & (ids >= 0) & (ids != hot) & (place_of >= 0) & (place_of < SLOTS)
    slot = lax.broadcasted_iota(jnp.int32, (16, LANES), 0)
    column = jnp.where(slot >= 8, other, x)
    expert = ((slot & 7) >> 1) * (WAYS * CORES) + column * CORES + c
    key = jnp.where(usable, ids * SLOTS + place_of, -1)
    hit = key == expert * SLOTS + (slot & 1)
    source = jnp.sum(jnp.where(hit, local >> 1, 0).astype(F32), axis=1, keepdims=True)
    out_int[0:16, :] = jnp.broadcast_to(source, (16, LANES)).astype(jnp.int32)
    here = (ids >> 1) & 3
    which = jnp.where(here == other, 1, 0)
    mine = usable & ((here == x) | (here == other))
    index = (ids & 1) * 16 + which * 8 + (ids >> 3) * SLOTS + place_of
    out_int[16:17, :] = jnp.where(mine, index, 0)
    out_real[0:1, :] = jnp.where(mine, shares, 0.0)


def front_kernel(
    groups, blocks, pairs, codes, x_ref, again_ref, wqkv_ref, hgain_ref, wout_ref, fgain_ref,
    wg_ref, wu_ref, wd_ref, resid_ref, ffn_ref, int_ref, real_ref, hot_ref,
    normed, q, k, v, wcols, state, ratio, numer, denom,
    chip, chips, sib, rows, peak, peaks,
    mine, theirs, sums, xs, row_sum, zs, plane_sum, ys, back, heads_in, sib2,
    near, far, slices, halves_in, summed, pieces_in, loads, stay, send, recv,
):
    y, z, x, c = place()
    lane_count = WAYS * CORES
    tokens, width = x_ref.shape
    tiles = tokens // ROWS
    step = 2 * HEAD_DIM
    steps = width // step

    def at(yy, zz, xx, cc):
        return (yy, zz * lane_count + xx * CORES + cc)

    sibling = at(y, z, x, 1 - c)
    along_x = [at(y, z, (x + d) % WAYS, c) for d in range(1, WAYS)]
    along_z = [at(y, (z + d) % WAYS, x, c) for d in range(1, WAYS)]
    along_y = [at((y + d) % groups, z, x, c) for d in range(1, groups)]
    fetches = []
    for j in range(3 * steps):
        fetch = pltpu.make_async_copy(
            wqkv_ref.at[:, pl.ds(j * step, step)], wcols.at[j], loads.at[j]
        )
        fetch.start()
        fetches.append(fetch)
    greet([sibling] + along_x + along_z + along_y)
    copies = []

    def go(src, dst, device):
        n = len(copies)
        copy = remote(src, dst, send.at[n], recv.at[n], device)
        copy.start()
        copies.append(copy)
        return copy

    def arrive(waits):
        for copy in waits:
            copy.wait_recv()

    hidden = wg_ref.shape[1]
    offset = wd_ref.shape[0] - HALF
    lanes_of = (
        (wg_ref, HALF, pl.ds(0, hidden)),
        (wu_ref, HALF, pl.ds(hidden, hidden)),
        (wd_ref, offset, pl.ds(2 * hidden, width)),
    )
    ring = (
        (x, along_x[0], along_x[2], along_x[1]),
        (z, along_z[0], along_z[2], along_z[1]),
    )
    swapped = []
    for n, (source, jump, span) in enumerate(lanes_of):
        there = source.at[pl.ds(jump * (1 - c), HALF), :]
        swapped.append(go(there, far.at[:, span], sibling))
        local = pltpu.make_async_copy(
            source.at[pl.ds(jump * c, HALF), :], near.at[:, span], stay.at[n]
        )
        local.start()
        fetches.append(local)

    def start_reduce():
        waits = []
        for order, (spot, plus, minus, _) in enumerate(ring):
            top = order * (HALF // 2)

            def part(i, shift=0, size=SLICE):
                row = top + ((spot + i + WAYS) % WAYS) * SLICE + shift
                return near.at[pl.ds(row, size)]

            short = SLICE // 2
            waits.append(
                (
                    go(part(2, 0, short), halves_in.at[order, 0], plus),
                    go(part(2, short, short), halves_in.at[order, 1], minus),
                    go(part(1), slices.at[order, 0], plus),
                    go(part(-1), slices.at[order, 1], minus),
                )
            )
        return waits

    def relay_reduce(waits):
        short = SLICE // 2
        for order, (_, plus, minus, _) in enumerate(ring):
            arrive(waits[order][:2])
            waits[order] += (
                go(halves_in.at[order, 0], slices.at[order, 2, pl.ds(0, short)], plus),
                go(halves_in.at[order, 1], slices.at[order, 2, pl.ds(short, short)], minus),
            )

    def second_reduce(waits):
        later = []
        for order, (spot, _, _, _) in enumerate(ring):
            arrive(waits[order][2:])
            top = order * (HALF // 2) + spot * SLICE

            @pl.loop(0, SLICE // PIECE)
            def _(i):
                row = pl.multiple_of(i * PIECE, PIECE)
                base_rows = pl.ds(pl.multiple_of(top + row, PIECE), PIECE)
                row = pl.ds(row, PIECE)
                total = near[base_rows, :] + slices[order, 0, row, :]
                summed[order, row, :] = total + (slices[order, 1, row, :] + slices[order, 2, row, :])

            spot, plus, minus, opposite = ring[1 - order]
            for d, device in ((1, plus), (2, opposite), (3, minus)):
                piece = summed.at[order, pl.ds(((spot + d) % WAYS) * PIECE, PIECE)]
                later.append(go(piece, pieces_in.at[order, d - 1], device))
        return later

    def gather_pieces(waits):
        arrive(waits)
        later = []
        for order in range(2):
            spot, plus, minus, opposite = ring[1 - order]
            row = pl.ds(pl.multiple_of(spot * PIECE, PIECE), PIECE)
            total = summed[order, row, :] + pieces_in[order, 0]
            hot_ref[order, row, :] = total + (pieces_in[order, 1] + pieces_in[order, 2])
            for device in (plus, opposite, minus):
                later.append(go(hot_ref.at[order, row], hot_ref.at[order, row], device))
        return later

    visits = 2 * blocks
    lane = lax.broadcasted_iota(jnp.int32, (8, LANES), 1)
    sub = lax.broadcasted_iota(jnp.int32, (8, LANES), 0)
    first = (x * CORES + c) * visits
    info = jnp.zeros((8, LANES), jnp.int32)
    for b in range(blocks):
        both = codes[b, 0] + codes[b, 1]
        for j in range(2):
            here = lane == first + (2 * b + j)
            value = jnp.where(sub == 0, pairs[b, j] + 1, jnp.where(sub == 1, codes[b, j], both))
            info = jnp.where(here & (sub < 3), value, info)
    chip[...] = info
    waits = [go(chip, sib, sibling)]

    @pl.loop(0, tiles)
    def _(i):
        rows_i = pl.ds(pl.multiple_of(i * ROWS, ROWS), ROWS)
        normed[rows_i, :] = norm_rows(x_ref[rows_i, :].astype(F32), again_ref[...]).astype(BF16)

    arrive(waits)
    chips[x] = info + sib[...]
    waits = [go(chips.at[x], chips.at[x], device) for device in along_x]

    def project(j):
        for part in range(3):
            fetches[part * steps + j].wait()
        cols = slice(j * step, (j + 1) * step)
        q[:, cols] = lifted(jnp.dot(normed[...], wcols[j], preferred_element_type=F32))
        k[:, cols] = lifted(jnp.dot(normed[...], wcols[steps + j], preferred_element_type=F32))
        v[:, cols] = jnp.dot(
            normed[...], wcols[2 * steps + j], preferred_element_type=F32
        ).astype(BF16)
        for head in range(2 * j, 2 * j + 2):
            cols = slice(head * HEAD_DIM, (head + 1) * HEAD_DIM)
            keys = k[:, cols]
            total = jnp.sum(keys.astype(F32), axis=0, keepdims=True)
            total = jnp.broadcast_to(total, (STATE - HEAD_DIM, HEAD_DIM))
            outer = dot_first(v[:, cols], keys)
            state[head, :HEAD_DIM, :] = outer
            state[head, HEAD_DIM:, :] = total
            mine[head, :HEAD_DIM, :] = outer.astype(BF16)
            mine[head, HEAD_DIM:, :] = total.astype(BF16)

    project(0)
    arrive(waits)
    info_row = chips[0] + chips[1] + chips[2] + chips[3]
    rows[z] = info_row
    waits = [go(rows.at[z], rows.at[z], device) for device in along_z]
    project(1)
    arrive(waits)
    expert = lax.broadcasted_iota(jnp.int32, (WAYS * lane_count, LANES), 0)
    lanes = lax.broadcasted_iota(jnp.int32, (WAYS * lane_count, LANES), 1)
    counts = jnp.zeros((WAYS * lane_count, 1), F32)
    most = jnp.zeros((WAYS * lane_count, 1), F32)
    for i in range(WAYS):
        there = (rows[i][0:1, :] - 1) == expert
        low = jnp.sum(jnp.where(there & (lanes < 4 * visits), 1.0, 0.0), axis=1, keepdims=True)
        high = jnp.sum(jnp.where(there & (lanes >= 4 * visits), 1.0, 0.0), axis=1, keepdims=True)
        counts = counts + low + high
        most = jnp.maximum(most, jnp.maximum(low, high))
    is_hot = counts > HOT - 0.5
    hot = jnp.sum(jnp.where(is_hot, expert[:, 0:1].astype(F32), 0.0), axis=0, keepdims=True)
    most = jnp.max(jnp.where(is_hot, 0.0, most), axis=0, keepdims=True)
    peak[...] = jnp.broadcast_to(most, (8, LANES))
    peak_waits = [go(peak, peaks.at[y], device) for device in along_y]
    here = (hot == (z * lane_count + x * CORES + c).astype(F32)).astype(BF16)
    beside = (hot == (z * lane_count + x * CORES + 1 - c).astype(F32)).astype(BF16)
    project(2)
    arrive(swapped)
    for fetch in fetches[-3:]:
        fetch.wait()

    @pl.loop(0, HALF // PIECE)
    def _(i):
        row = pl.ds(pl.multiple_of(i * PIECE, PIECE), PIECE)
        near[row, :] = near[row, :] * here + far[row, :] * beside

    project(3)
    waits = [go(mine, theirs, sibling)]
    reduce_waits = start_reduce()
    hot = jnp.broadcast_to(hot, (1, LANES)).astype(jnp.int32)
    ids = info_row[0:1, :] - 1
    wide = jnp.broadcast_to(ids, (LANES, LANES))
    tall = wide.T
    rank_lane = lax.broadcasted_iota(jnp.int32, (LANES, LANES), 1)
    rank_sub = lax.broadcasted_iota(jnp.int32, (LANES, LANES), 0)
    earlier = (wide == tall) & (rank_sub < rank_lane)
    halves = (rank_sub < 4 * visits) == (rank_lane < 4 * visits)
    rank = jnp.sum(jnp.where(earlier & halves, 1.0, 0.0), axis=0, keepdims=True).astype(jnp.int32)
    shares = info_row[1:2, :].astype(F32) / jnp.maximum(info_row[2:3, :], 1).astype(F32)
    int_ref[16:24, :] = jnp.zeros((8, LANES), jnp.int32)
    real_ref[...] = jnp.zeros((8, LANES), F32)
    tables(0, ids, rank, shares, hot, int_ref, real_ref)
    lane = lane[0:1, :]
    own = (lane >= first) & (lane < first + visits) & (ids == hot)
    seen = jnp.sum(jnp.where(own, 1.0, 0.0), axis=1, keepdims=True)
    first_lane = jnp.min(jnp.where(own, lane, 1000).astype(F32), axis=1, keepdims=True)
    last_lane = jnp.max(jnp.where(own, lane, -1).astype(F32), axis=1, keepdims=True)
    int_ref[17:18, :] = ids
    int_ref[18:19, :] = rank
    int_ref[19:20, :] = hot
    first_block = jnp.where(seen > 0.5, (first_lane.astype(jnp.int32) - first) >> 1, 0)
    last_block = (last_lane.astype(jnp.int32) - first) >> 1
    following = jnp.where(first_block + 1 >= blocks, 0, first_block + 1)
    second_block = jnp.where(seen > 1.5, last_block, following)
    int_ref[21:22, :] = jnp.where(lane == 0, first_block, second_block)
    lane_real = lane.astype(F32)
    first_share = jnp.sum(
        jnp.where(own & (lane_real == first_lane), shares, 0.0), axis=1, keepdims=True
    )
    last_share = jnp.sum(
        jnp.where(own & (lane_real == last_lane) & (seen > 1.5), shares, 0.0), axis=1, keepdims=True
    )
    real_ref[1:2, :] = shares
    real_ref[2:3, :] = jnp.where(lane == 0, first_share, last_share)
    arrive(peak_waits)
    peaks[y] = peak[...]
    top = peaks[0]
    for i in range(1, groups):
        top = jnp.maximum(top, peaks[i])
    int_ref[22:23, :] = top[0:1, :].astype(jnp.int32)

    causal = lax.broadcasted_iota(jnp.int32, (ROWS, ROWS), 0) >= lax.broadcasted_iota(
        jnp.int32, (ROWS, ROWS), 1
    )

    def within(start, stop):
        @pl.loop(start, stop)
        def _(head):
            cols = pl.ds(pl.multiple_of(head * HEAD_DIM, HEAD_DIM), HEAD_DIM)
            keys = k[:, cols]
            both = jnp.concatenate([v[:, cols], jnp.ones((tokens, HEAD_DIM), BF16)], axis=1)
            for tile in range(tiles):
                part = slice(tile * ROWS, (tile + 1) * ROWS)
                query = q[part, cols]
                scores = jnp.where(causal, dot_last(query, keys[part, :]), 0.0).astype(BF16)
                total = jnp.dot(scores, both[part, :], preferred_element_type=F32)
                if tile > 0:
                    scores = dot_last(query, keys[: tile * ROWS, :]).astype(BF16)
                    total = total + jnp.dot(
                        scores, both[: tile * ROWS, :], preferred_element_type=F32
                    )
                numer[part, cols] = total[:, :HEAD_DIM]
                denom[part, cols] = total[:, HEAD_DIM:]

    within(0, 2)
    arrive(waits)
    base = c * WAYS
    for i in range(WAYS):
        sums[i] = (state[base + i] + theirs[base + i].astype(F32)).astype(BF16)
    xs[x] = sums[x]
    waits = [go(sums.at[(x + d) % WAYS], xs.at[x], along_x[d - 1]) for d in range(1, WAYS)]
    relay_reduce(reduce_waits)
    within(2, 4)
    arrive(waits)
    row_sum[...] = sum(xs[i].astype(F32) for i in range(WAYS)).astype(BF16)
    zs[z] = row_sum[...]
    waits = [go(row_sum, zs.at[z], along_z[d - 1]) for d in range(1, WAYS)]
    within(4, 6)
    arrive(waits)
    plane_sum[...] = sum(zs[i].astype(F32) for i in range(WAYS)).astype(BF16)
    waits = [go(plane_sum, ys.at[y], along_y[d - 1]) for d in range(1, groups)]
    total = jnp.zeros(row_sum.shape, F32)
    for i in range(WAYS):
        total = total + zs[i].astype(F32) * jnp.where(i < z, 1.0, 0.0)
    within(6, 7)
    arrive(waits)
    ys[y] = plane_sum[...]
    for i in range(groups):
        total = total + ys[i].astype(F32) * jnp.where(i < y, 1.0, 0.0)
    for i in range(WAYS):
        back[i] = total.astype(BF16)
        total = total + xs[i].astype(F32)
    heads_in[x] = back[x]
    waits = [go(back.at[(x + d) % WAYS], heads_in.at[x], along_x[d - 1]) for d in range(1, WAYS)]
    within(7, 8)
    reduce_waits = second_reduce(reduce_waits)
    arrive(waits)
    waits = [go(heads_in, sib2, sibling)]
    later = jnp.where(c == 1, 1.0, 0.0)

    def add_prior(first_head, source):
        @pl.loop(0, WAYS)
        def _(i):
            head = first_head + i
            prior = (source[i].astype(F32) + theirs[head].astype(F32) * later).astype(BF16)
            filled = jnp.broadcast_to(prior[HEAD_DIM : HEAD_DIM + 1, :], (HEAD_DIM, HEAD_DIM))
            carried = jnp.concatenate([prior[:HEAD_DIM, :], filled], axis=0)
            cols = pl.ds(pl.multiple_of(head * HEAD_DIM, HEAD_DIM), HEAD_DIM)
            total = dot_last(q[:, cols], carried)
            ratio[:, cols] = (numer[:, cols] + total[:, :HEAD_DIM]) / (
                denom[:, cols] + total[:, HEAD_DIM:]
            )

    add_prior(base, heads_in)
    reduce_waits = gather_pieces(reduce_waits)
    arrive(waits)
    add_prior((1 - c) * WAYS, sib2)
    half = tokens // 2
    for part in range(2):
        part_rows = slice(part * half, (part + 1) * half)
        attended = norm_rows(ratio[part_rows, :], hgain_ref[...]).astype(BF16)
        resid = x_ref[part_rows, :].astype(F32) + jnp.dot(
            attended, wout_ref[...], preferred_element_type=F32
        )
        resid = resid.astype(BF16)
        resid_ref[part_rows, :] = resid
        ffn_ref[part_rows, :] = norm_rows(resid.astype(F32), fgain_ref[...]).astype(BF16)
    arrive(reduce_waits)
    for copy in copies:
        copy.wait_send()


def front(
    x, attn_gain, w_qkv, head_gain, w_out, ffn_gain, w_gate, w_up, w_down, pair_ids, gate_codes, groups
):
    tokens, width = x.shape
    packed = 2 * w_gate.shape[1] + width
    blocks = pair_ids.shape[0]
    tile = (8, LANES)
    one = (STATE, HEAD_DIM)
    some = (WAYS,) + one
    every = (HEADS,) + one
    step = 2 * HEAD_DIM
    pieces = 3 * width // step
    count = 1 + 2 * (WAYS - 1) + groups - 1 + 2 + 3 * (WAYS - 1) + groups - 1
    count += 3 + 12 + 4 * (WAYS - 1)

    def wide(*shape):
        return pltpu.VMEM(shape + (packed,), BF16)

    smem = pl.BlockSpec(memory_space=pltpu.SMEM)
    vmem = pl.BlockSpec(memory_space=pltpu.VMEM)
    hbm = pl.BlockSpec(memory_space=pl.ANY)
    return pl.pallas_call(
        functools.partial(front_kernel, groups, blocks),
        out_shape=[jax.ShapeDtypeStruct((tokens, width), BF16)] * 2
        + [jax.ShapeDtypeStruct((24, LANES), jnp.int32), jax.ShapeDtypeStruct(tile, F32)]
        + [jax.ShapeDtypeStruct((2, SLICE, packed), BF16)],
        in_specs=[smem] * 2 + [vmem] * 2 + [hbm] + [vmem] * 3 + [hbm] * 3,
        out_specs=[vmem] * 5,
        scratch_shapes=[pltpu.VMEM((tokens, width), BF16)] * 4
        + [pltpu.VMEM((pieces, width, step), BF16), pltpu.VMEM(every, F32)]
        + [pltpu.VMEM((tokens, width), F32)] * 3
        + [
            pltpu.VMEM(tile, jnp.int32),
            pltpu.VMEM((WAYS,) + tile, jnp.int32),
            pltpu.VMEM(tile, jnp.int32),
            pltpu.VMEM((WAYS,) + tile, jnp.int32),
            pltpu.VMEM(tile, F32),
            pltpu.VMEM((groups,) + tile, F32),
            pltpu.VMEM(every, BF16),
            pltpu.VMEM(every, BF16),
            pltpu.VMEM(some, BF16),
            pltpu.VMEM(some, BF16),
            pltpu.VMEM(one, BF16),
            pltpu.VMEM(some, BF16),
            pltpu.VMEM(one, BF16),
            pltpu.VMEM((groups,) + one, BF16),
            pltpu.VMEM(some, BF16),
            pltpu.VMEM(some, BF16),
            pltpu.VMEM(some, BF16),
            wide(HALF),
            wide(HALF),
            wide(2, WAYS - 1, SLICE),
            wide(2, 2, SLICE // 2),
            wide(2, SLICE),
            wide(2, WAYS - 1, PIECE),
            pltpu.SemaphoreType.DMA((pieces,)),
            pltpu.SemaphoreType.DMA((3,)),
            pltpu.SemaphoreType.DMA((count,)),
            pltpu.SemaphoreType.DMA((count,)),
        ],
        compiler_params=pltpu.CompilerParams(
            collective_id=0, has_side_effects=True, vmem_limit_bytes=LIMIT_BYTES
        ),
        name="front",
    )(
        pair_ids, gate_codes, x, attn_gain, w_qkv, head_gain, w_out, ffn_gain, w_gate, w_up, w_down
    )


def moe_kernel(
    blocks, chunks, table, weight, f_ref, base_ref, wg_ref, wu_ref, wd_ref, slice_ref, out_ref,
    hot_ref, *rest
):
    gather, landed = rest[:chunks], rest[chunks : 2 * chunks]
    (
        hand, zs, relay, taken, made_rows, relay_back, hand_back, partial, final, local, send, recv,
        hot_local, hot_send, hot_recv,
    ) = rest[2 * chunks :]
    depth = ROWS // chunks
    width = f_ref.shape[2]
    y, z, x, c = place()
    lane = WAYS * CORES
    parity = x % 2

    def at(zz, xx, cc):
        return (y, ((zz + WAYS) % WAYS) * lane + ((xx + WAYS) % WAYS) * CORES + cc)

    sibling = at(z, x, 1 - c)
    mate = at(z, x + 1 - 2 * parity, c)
    across = at(z, x + 2 * parity - 1, c)
    up, down = at(z + 1, x, c), at(z - 1, x, c)
    greet([sibling, mate, across, up, down])
    me = parity * CORES + c
    friend = (1 - parity) * CORES + c
    pending = []
    made = {}

    def go(k, n, src, dst, device):
        copy = remote(src, dst, send.at[k, n], recv.at[k, n], device)
        copy.start()
        pending.append(copy)
        made[k, n] = copy

    def keep(k, n, src, dst):
        copy = pltpu.make_async_copy(src, dst, local.at[k, n])
        copy.start()
        made[k, "keep", n] = copy

    def arrived(k, *numbers):
        for n in numbers:
            made[k, n].wait_recv()

    def step_of(row):
        return (row + WAYS) % WAYS

    def begin(k):
        own = f_ref.at[:, pl.ds(k * depth, depth), :]
        here = gather[k].at[pl.ds(me * blocks, blocks)]
        go(k, 0, own, here, mate)
        go(k, 1, own, here, sibling)
        keep(k, 0, own, here)

    def widen(k):
        arrived(k, 0)
        there = gather[k].at[pl.ds(friend * blocks, blocks)]
        go(k, 2, there, there, sibling)

    def select(k):
        made[k, "keep", 0].wait()
        arrived(k, 1, 2)
        for row in range(WAYS):
            for j in range(SLOTS):
                hand[k, row, j] = gather[k][table[8 + row * SLOTS + j, 0]]
        go(k, 3, hand.at[k], zs.at[k, :, 1], across)
        for row in range(WAYS):
            for j in range(SLOTS):
                zs[k, row, 0, j] = gather[k][table[row * SLOTS + j, 0]]

    def climb(k):
        arrived(k, 3)
        go(k, 6, zs.at[k, step_of(z + 2), 0], relay.at[k, 0], up)
        go(k, 19, zs.at[k, step_of(z + 2), 1], relay.at[k, 1], down)
        go(k, 4, zs.at[k, step_of(z + 1)], taken.at[k, z], up)
        go(k, 5, zs.at[k, step_of(z - 1)], taken.at[k, z], down)
        keep(k, 1, zs.at[k, z], taken.at[k, z])

    def forward(k):
        arrived(k, 6)
        go(k, 7, relay.at[k, 0], taken.at[k, step_of(z - 1), 0], up)
        arrived(k, 19)
        go(k, 20, relay.at[k, 1], taken.at[k, step_of(z + 1), 1], down)

    def work(k):
        arrived(k, 4, 5, 7, 20)
        made[k, "keep", 1].wait()
        rows = taken[k].reshape(WAYS * PART * depth, width)
        gate = jnp.dot(rows, wg_ref[...], preferred_element_type=F32)
        upper = jnp.dot(rows, wu_ref[...], preferred_element_type=F32)
        inner = (jax.nn.silu(gate) * upper).astype(BF16)
        result = jnp.dot(inner, wd_ref[...], preferred_element_type=F32).astype(BF16)
        made_rows[k] = result.reshape(WAYS, SIDES, SLOTS, depth, width)
        go(k, 12, made_rows.at[k, step_of(z + 2), 0], relay_back.at[k, 0], up)
        go(k, 21, made_rows.at[k, step_of(z + 2), 1], relay_back.at[k, 1], down)
        for n, d, device in ((8, 1, up), (10, -1, down)):
            target = step_of(z + d)
            go(k, n, made_rows.at[k, target, 0], landed[k].at[pl.ds(c * 16 + z * SLOTS, SLOTS)], device)
            go(k, n + 1, made_rows.at[k, target, 1], hand_back.at[k, pl.ds(z * SLOTS, SLOTS)], device)
        keep(k, 2, made_rows.at[k, z, 0], landed[k].at[pl.ds(c * 16 + z * SLOTS, SLOTS)])
        keep(k, 3, made_rows.at[k, z, 1], hand_back.at[k, pl.ds(z * SLOTS, SLOTS)])

    def forward_back(k):
        arrived(k, 21)
        origin = step_of(z + 1)
        go(k, 14, relay_back.at[k, 1], hand_back.at[k, pl.ds(origin * SLOTS, SLOTS)], down)
        arrived(k, 12)
        origin = step_of(z - 1)
        go(k, 13, relay_back.at[k, 0], landed[k].at[pl.ds(c * 16 + origin * SLOTS, SLOTS)], up)

    def give(k):
        arrived(k, 9, 11, 14)
        made[k, "keep", 3].wait()
        go(k, 15, hand_back.at[k], landed[k].at[pl.ds(c * 16 + 8, 8)], across)
        arrived(k, 8, 10, 13)
        made[k, "keep", 2].wait()
        there = landed[k].at[pl.ds(c * 16, 8)]
        go(k, 16, there, there, sibling)

    def mirror(k):
        arrived(k, 15)
        there = landed[k].at[pl.ds(c * 16 + 8, 8)]
        go(k, 17, there, there, sibling)

    def build(k):
        arrived(k, 16, 17)

        def one(start, offset):
            def run(b, carry):
                first = start + 2 * b
                total = landed[k][table[16, first]].astype(F32) * weight[0, first]
                total = total + landed[k][table[16, first + 1]].astype(F32) * weight[0, first + 1]
                partial[k, offset + b] = total.astype(BF16)
                return carry

            return run

        row = (x // 2) * 4 * 2 * blocks
        lax.fori_loop(0, blocks, one(row + friend * 2 * blocks, blocks), 0)
        go(k, 18, partial.at[k, pl.ds(blocks, blocks)], final.at[k], mate)
        lax.fori_loop(0, blocks, one(row + me * 2 * blocks, 0), 0)

    def finish(k):
        arrived(k, 18)
        rows = slice(k * depth, (k + 1) * depth)

        def run(b, carry):
            total = base_ref[b, rows, :].astype(F32) + partial[k, b].astype(F32)
            out_ref[b, rows, :] = (total + final[k, b].astype(F32)).astype(BF16)
            return carry

        lax.fori_loop(0, blocks, run, 0)

    right, left = at(z, x + 1, c), at(z, x - 1, c)
    ring = ((x, right, left), (z, up, down))
    hot_made = {}

    def hot_go(n, src, dst, device):
        copy = remote(src, dst, hot_send.at[n], hot_recv.at[n], device)
        copy.start()
        pending.append(copy)
        hot_made[n] = copy

    def hot_rows(order, spot, shift=0, size=SLICE):
        row = order * (HALF // 2) + ((spot + WAYS) % WAYS) * SLICE + shift
        return hot_ref.at[c, pl.ds(row, size)]

    def hot_begin():
        for order, (spot, plus, minus) in enumerate(ring):
            there = hot_rows(order, spot)
            hot_go(8 * order, slice_ref.at[order], there, plus)
            hot_go(8 * order + 1, slice_ref.at[order], there, minus)
            hot_go(8 * order + 2, slice_ref.at[order], there, sibling)
            copy = pltpu.make_async_copy(slice_ref.at[order], there, hot_local.at[order])
            copy.start()
            hot_made["keep", order] = copy

    def hot_relay():
        short = SLICE // 2
        for order, (spot, plus, minus) in enumerate(ring):
            hot_made[8 * order].wait_recv()
            there = hot_rows(order, spot - 1, 0, short)
            hot_go(8 * order + 3, there, there, plus)
            there = hot_rows(order, spot - 1)
            hot_go(8 * order + 4, there, there, sibling)
            hot_made[8 * order + 1].wait_recv()
            there = hot_rows(order, spot + 1, short, short)
            hot_go(8 * order + 5, there, there, minus)
            there = hot_rows(order, spot + 1)
            hot_go(8 * order + 6, there, there, sibling)

    def hot_end():
        for order, (spot, plus, minus) in enumerate(ring):
            hot_made[8 * order + 3].wait_recv()
            hot_made[8 * order + 5].wait_recv()
            there = hot_rows(order, spot + 2)
            hot_go(8 * order + 7, there, there, sibling)
            hot_made["keep", order].wait()
            for n in (2, 4, 6):
                hot_made[8 * order + n].wait_recv()

    stages = [widen, select, climb, forward, work, forward_back, give, mirror, build, finish]
    begin(0)
    begin(1)
    for step in range(chunks + len(stages) - 1):
        if step + 2 < chunks:
            begin(step + 2)
        for lag in reversed(range(len(stages))):
            if 0 <= step - lag < chunks:
                stages[lag](step - lag)
        if step == chunks + 3:
            hot_begin()
        if step == chunks + 6:
            hot_relay()
    hot_end()
    for order in range(2):
        hot_made[8 * order + 7].wait_recv()
    for copy in pending:
        copy.wait_send()


def moe(table, weight, ffn_in, base, w_gate, w_up, w_down, hot_slices):
    blocks, rows, width = ffn_in.shape
    packed = hot_slices.shape[2]
    hbm = pl.BlockSpec(memory_space=pl.ANY)
    chunks = CHUNKS
    depth = rows // chunks
    pair = 2 * CORES * blocks
    whole = pl.BlockSpec(memory_space=pltpu.VMEM)
    return pl.pallas_call(
        functools.partial(moe_kernel, blocks, chunks),
        out_shape=[
            jax.ShapeDtypeStruct(base.shape, BF16),
            jax.ShapeDtypeStruct((CORES, HALF, packed), BF16),
        ],
        in_specs=[pl.BlockSpec(memory_space=pltpu.SMEM)] * 2 + [whole] * 6,
        out_specs=[whole, hbm],
        scratch_shapes=[pltpu.VMEM((pair, depth, width), BF16)] * chunks
        + [pltpu.VMEM((CORES * 16, depth, width), BF16)] * chunks
        + [
            pltpu.VMEM((chunks, WAYS, SLOTS, depth, width), BF16),
            pltpu.VMEM((chunks, WAYS, SIDES, SLOTS, depth, width), BF16),
            pltpu.VMEM((chunks, SIDES, SLOTS, depth, width), BF16),
            pltpu.VMEM((chunks, WAYS, SIDES, SLOTS, depth, width), BF16),
            pltpu.VMEM((chunks, WAYS, SIDES, SLOTS, depth, width), BF16),
            pltpu.VMEM((chunks, SIDES, SLOTS, depth, width), BF16),
            pltpu.VMEM((chunks, WAYS * SLOTS, depth, width), BF16),
            pltpu.VMEM((chunks, 2 * blocks, depth, width), BF16),
            pltpu.VMEM((chunks, blocks, depth, width), BF16),
            pltpu.SemaphoreType.DMA((chunks, 4)),
            pltpu.SemaphoreType.DMA((chunks, 22)),
            pltpu.SemaphoreType.DMA((chunks, 22)),
            pltpu.SemaphoreType.DMA((2,)),
            pltpu.SemaphoreType.DMA((16,)),
            pltpu.SemaphoreType.DMA((16,)),
        ],
        compiler_params=pltpu.CompilerParams(
            collective_id=1, has_side_effects=True, vmem_limit_bytes=67043328
        ),
        name="moe",
    )(table, weight, ffn_in, base, w_gate, w_up, w_down, hot_slices)


def hot_kernel(hidden, pick, share, x_ref, low_ref, high_ref, total_ref, out_ref):
    block = pl.program_id(0)
    width = x_ref.shape[2]
    is_first = block == pick[21, 0]
    is_second = block == pick[21, 1]

    @pl.when(is_first | is_second)
    def _():
        low, high = x_ref[0][:, :HALF], x_ref[0][:, HALF:]

        def both(start):
            cols = slice(start, start + hidden)
            return jnp.dot(low, low_ref[0, :, cols], preferred_element_type=F32) + jnp.dot(
                high, high_ref[0, :, cols], preferred_element_type=F32
            )

        inner = (jax.nn.silu(both(0)) * both(hidden)).astype(BF16)
        cols = slice(2 * hidden, 2 * hidden + width)
        result = jnp.dot(inner[:, :HALF], low_ref[0, :, cols], preferred_element_type=F32)
        result = result + jnp.dot(
            inner[:, HALF:], high_ref[0, 2 * HALF - hidden :, cols], preferred_element_type=F32
        )
        weight = jnp.where(is_first, share[2, 0], share[2, 1])
        result = result.astype(BF16).astype(F32) * weight
        out_ref[0] = (total_ref[0].astype(F32) + result).astype(BF16)

    @pl.when(jnp.logical_not(is_first | is_second))
    def _():
        out_ref[...] = total_ref[...]


def add_hot(pick, share, ffn_in, hot, total):
    blocks, rows, width = ffn_in.shape
    packed = hot.shape[2]
    hidden = (packed - width) // 2
    block = pl.BlockSpec((1, rows, width), lambda i, pick, share: (i, 0, 0))
    return pl.pallas_call(
        functools.partial(hot_kernel, hidden),
        grid_spec=pltpu.PrefetchScalarGridSpec(
            num_scalar_prefetch=2,
            grid=(blocks,),
            in_specs=[
                block,
                pl.BlockSpec((1, HALF, packed), lambda i, pick, share: (0, 0, 0)),
                pl.BlockSpec((1, HALF, packed), lambda i, pick, share: (1, 0, 0)),
                block,
            ],
            out_specs=block,
        ),
        out_shape=jax.ShapeDtypeStruct(total.shape, BF16),
        compiler_params=pltpu.CompilerParams(vmem_limit_bytes=LIMIT_BYTES),
        name="add_hot",
    )(pick, share, ffn_in, hot, hot, total)


def tables_kernel(turn, int_ref, real_ref, out_int, out_real):
    out_int[...] = int_ref[...]
    out_real[...] = real_ref[...]
    tables(
        turn[0], int_ref[17:18, :], int_ref[18:19, :], real_ref[1:2, :], int_ref[19:20, :],
        out_int, out_real,
    )


def later_tables(turn, ints, reals):
    return pl.pallas_call(
        tables_kernel,
        out_shape=[
            jax.ShapeDtypeStruct(ints.shape, ints.dtype),
            jax.ShapeDtypeStruct(reals.shape, reals.dtype),
        ],
        in_specs=[pl.BlockSpec(memory_space=pltpu.SMEM)]
        + [pl.BlockSpec(memory_space=pltpu.VMEM)] * 2,
        out_specs=[pl.BlockSpec(memory_space=pltpu.VMEM)] * 2,
        name="later_tables",
    )(turn, ints, reals)


def body(
    hidden_in, attn_gain, w_qkv, head_gain, w_out, ffn_gain, w_gate, w_up, w_down, pair_ids, gate_codes
):
    tokens, width = hidden_in.shape
    blocks = tokens // ROWS
    groups = lax.axis_size("grp")
    weights = (w_gate[0], w_up[0], w_down[0])
    resid, ffn_in, ints, reals, hot_slices = front(
        hidden_in, attn_gain[None], w_qkv, head_gain[None], w_out, ffn_gain[None], *weights, pair_ids,
        gate_codes, groups,
    )
    resid = resid.reshape(blocks, ROWS, width)
    ffn_in = ffn_in.reshape(blocks, ROWS, width)
    total, hot = moe(ints, reals, ffn_in, resid, *weights, hot_slices)

    def more(total):
        def one(turn, total):
            later_ints, later_reals = later_tables(turn[None], ints, reals)
            return moe(later_ints, later_reals, ffn_in, total, *weights, hot_slices)[0]

        return lax.fori_loop(1, -(-LIMIT // SLOTS), one, total)

    total = lax.cond(ints[22, 0] > SLOTS, more, lambda total: total, total)
    total = add_hot(ints, reals, ffn_in, hot, total)
    return total.reshape(tokens, width)


def solution(mesh):
    return jax.shard_map(
        body,
        mesh=mesh,
        in_specs=(
            P(("grp", "seq"), None), P(), P(), P(), P(), P(),
            P("seq", None, None), P("seq", None, None), P("seq", None, None),
            P(("grp", "seq"), None), P(("grp", "seq"), None),
        ),
        out_specs=P(("grp", "seq"), None),
        check_vma=False,
    )
```

```python
import functools

import jax
import jax.numpy as jnp
from jax import lax
from jax.experimental import pallas as pl
from jax.experimental.pallas import tpu as pltpu
from jax.sharding import PartitionSpec as P

HEADS = 8
HEAD_DIM = 128
ROWS = 128
EPS = 1e-06
WAYS = 4
CORES = 2
SLOTS = 2
SIDES = 2
PART = SIDES * SLOTS
CHUNKS = 8
STATE = 144
LIMIT = 8
LANES = 128
HALF = 512
SLICE = 64
PIECE = 16
HOT = 15
MESH = pl.DeviceIdType.MESH
F32 = jnp.float32
BF16 = jnp.bfloat16
LIMIT_BYTES = 60 * 1024 * 1024


def place():
    seq = lax.axis_index("seq")
    return lax.axis_index("grp"), seq // (WAYS * CORES), (seq // CORES) % WAYS, seq % CORES


def remote(src, dst, send, recv, device):
    return pltpu.make_async_remote_copy(
        src_ref=src, dst_ref=dst, send_sem=send, recv_sem=recv, device_id=device, device_id_type=MESH
    )


def greet(devices):
    barrier = pltpu.get_barrier_semaphore()
    for device in devices:
        pl.semaphore_signal(barrier, inc=1, device_id=device, device_id_type=MESH)
    pl.semaphore_wait(barrier, len(devices))


def norm_rows(values, gain):
    return values * lax.rsqrt(jnp.mean(values * values, axis=-1, keepdims=True) + EPS) * gain


def dot_last(a, b):
    return lax.dot_general(a, b, (((1,), (1,)), ((), ())), preferred_element_type=F32)


def dot_first(a, b):
    return lax.dot_general(a, b, (((0,), (0,)), ((), ())), preferred_element_type=F32)


def lifted(values):
    return jnp.where(values > 0.0, values + 1.0, jnp.exp(jnp.minimum(values, 0.0))).astype(BF16)


def tables(turn, ids, rank, shares, hot, out_int, out_real):
    y, z, x, c = place()
    half = x // 2
    other = (x + 2 * (x % 2) - 1 + WAYS) % WAYS
    span = LANES * 7 // 16
    lane = lax.broadcasted_iota(jnp.int32, (1, LANES), 1)
    local = lane - half * span
    near = (local >= 0) & (local < span)
    place_of = rank - turn * SLOTS
    usable = near & (ids >= 0) & (ids != hot) & (place_of >= 0) & (place_of < SLOTS)
    slot = lax.broadcasted_iota(jnp.int32, (16, LANES), 0)
    column = jnp.where(slot >= 8, other, x)
    expert = ((slot & 7) >> 1) * (WAYS * CORES) + column * CORES + c
    key = jnp.where(usable, ids * SLOTS + place_of, -1)
    hit = key == expert * SLOTS + (slot & 1)
    source = jnp.sum(jnp.where(hit, local >> 1, 0).astype(F32), axis=1, keepdims=True)
    out_int[0:16, :] = jnp.broadcast_to(source, (16, LANES)).astype(jnp.int32)
    here = (ids >> 1) & 3
    which = jnp.where(here == other, 1, 0)
    mine = usable & ((here == x) | (here == other))
    index = (ids & 1) * 16 + which * 8 + (ids >> 3) * SLOTS + place_of
    out_int[16:17, :] = jnp.where(mine, index, 0)
    out_real[0:1, :] = jnp.where(mine, shares, 0.0)


def front_kernel(
    groups, blocks, pairs, codes, x_ref, again_ref, wqkv_ref, hgain_ref, wout_ref, fgain_ref,
    wg_ref, wu_ref, wd_ref, resid_ref, ffn_ref, int_ref, real_ref, hot_ref,
    normed, q, k, v, wcols, state, ratio, numer, denom,
    chip, chips, sib, rows, peak, peaks,
    mine, theirs, sums, xs, row_sum, zs, plane_sum, ys, back, heads_in, sib2,
    near, far, slices, halves_in, summed, pieces_in, loads, stay, send, recv,
):
    y, z, x, c = place()
    lane_count = WAYS * CORES
    tokens, width = x_ref.shape
    tiles = tokens // ROWS
    step = 2 * HEAD_DIM
    steps = width // step

    def at(yy, zz, xx, cc):
        return (yy, zz * lane_count + xx * CORES + cc)

    sibling = at(y, z, x, 1 - c)
    along_x = [at(y, z, (x + d) % WAYS, c) for d in range(1, WAYS)]
    along_z = [at(y, (z + d) % WAYS, x, c) for d in range(1, WAYS)]
    along_y = [at((y + d) % groups, z, x, c) for d in range(1, groups)]
    fetches = []
    for j in range(3 * steps):
        fetch = pltpu.make_async_copy(
            wqkv_ref.at[:, pl.ds(j * step, step)], wcols.at[j], loads.at[j]
        )
        fetch.start()
        fetches.append(fetch)
    greet([sibling] + along_x + along_z + along_y)
    copies = []

    def go(src, dst, device):
        n = len(copies)
        copy = remote(src, dst, send.at[n], recv.at[n], device)
        copy.start()
        copies.append(copy)
        return copy

    def arrive(waits):
        for copy in waits:
            copy.wait_recv()

    hidden = wg_ref.shape[1]
    offset = wd_ref.shape[0] - HALF
    lanes_of = (
        (wg_ref, HALF, pl.ds(0, hidden)),
        (wu_ref, HALF, pl.ds(hidden, hidden)),
        (wd_ref, offset, pl.ds(2 * hidden, width)),
    )
    ring = (
        (x, along_x[0], along_x[2], along_x[1]),
        (z, along_z[0], along_z[2], along_z[1]),
    )
    swapped = []
    for n, (source, jump, span) in enumerate(lanes_of):
        there = source.at[pl.ds(jump * (1 - c), HALF), :]
        swapped.append(go(there, far.at[:, span], sibling))
        local = pltpu.make_async_copy(
            source.at[pl.ds(jump * c, HALF), :], near.at[:, span], stay.at[n]
        )
        local.start()
        fetches.append(local)

    def start_reduce(far_half):
        waits = []
        for order, (spot, plus, minus, _) in enumerate(ring):
            top = order * (HALF // 2)

            def part(i, shift=0, size=SLICE):
                row = top + ((spot + i + WAYS) % WAYS) * SLICE + shift
                return near.at[pl.ds(row, size)]

            short = SLICE // 2
            if far_half:
                waits.append(
                    (
                        go(part(2, 0, short), halves_in.at[order, 0], plus),
                        go(part(2, short, short), halves_in.at[order, 1], minus),
                    )
                )
            else:
                waits.append(
                    (
                        go(part(1), slices.at[order, 0], plus),
                        go(part(-1), slices.at[order, 1], minus),
                    )
                )
        return waits

    def relay_reduce(waits):
        short = SLICE // 2
        for order, (_, plus, minus, _) in enumerate(ring):
            arrive(waits[order])
            waits[order] = (
                go(halves_in.at[order, 0], slices.at[order, 2, pl.ds(0, short)], plus),
                go(halves_in.at[order, 1], slices.at[order, 2, pl.ds(short, short)], minus),
            )

    def second_reduce(waits):
        later = []
        for order, (spot, _, _, _) in enumerate(ring):
            arrive(waits[order])
            top = order * (HALF // 2) + spot * SLICE

            @pl.loop(0, SLICE // PIECE)
            def _(i):
                row = pl.multiple_of(i * PIECE, PIECE)
                base_rows = pl.ds(pl.multiple_of(top + row, PIECE), PIECE)
                row = pl.ds(row, PIECE)
                total = near[base_rows, :] + slices[order, 0, row, :]
                summed[order, row, :] = total + (slices[order, 1, row, :] + slices[order, 2, row, :])

            spot, plus, minus, opposite = ring[1 - order]
            for d, device in ((1, plus), (2, opposite), (3, minus)):
                piece = summed.at[order, pl.ds(((spot + d) % WAYS) * PIECE, PIECE)]
                later.append(go(piece, pieces_in.at[order, d - 1], device))
        return later

    def gather_pieces(waits):
        arrive(waits)
        later = []
        for order in range(2):
            spot, plus, minus, opposite = ring[1 - order]
            row = pl.ds(pl.multiple_of(spot * PIECE, PIECE), PIECE)
            total = summed[order, row, :] + pieces_in[order, 0]
            hot_ref[order, row, :] = total + (pieces_in[order, 1] + pieces_in[order, 2])
            for device in (plus, opposite, minus):
                later.append(go(hot_ref.at[order, row], hot_ref.at[order, row], device))
        return later

    visits = 2 * blocks
    lane = lax.broadcasted_iota(jnp.int32, (8, LANES), 1)
    sub = lax.broadcasted_iota(jnp.int32, (8, LANES), 0)
    first = (x * CORES + c) * visits
    info = jnp.zeros((8, LANES), jnp.int32)
    for b in range(blocks):
        both = codes[b, 0] + codes[b, 1]
        for j in range(2):
            here = lane == first + (2 * b + j)
            value = jnp.where(sub == 0, pairs[b, j] + 1, jnp.where(sub == 1, codes[b, j], both))
            info = jnp.where(here & (sub < 3), value, info)
    chip[...] = info
    waits = [go(chip, sib, sibling)]

    @pl.loop(0, tiles)
    def _(i):
        rows_i = pl.ds(pl.multiple_of(i * ROWS, ROWS), ROWS)
        normed[rows_i, :] = norm_rows(x_ref[rows_i, :].astype(F32), again_ref[...]).astype(BF16)

    arrive(waits)
    chips[x] = info + sib[...]
    waits = [go(chips.at[x], chips.at[x], device) for device in along_x]

    def project(j):
        for part in range(3):
            fetches[part * steps + j].wait()
        cols = slice(j * step, (j + 1) * step)
        q[:, cols] = lifted(jnp.dot(normed[...], wcols[j], preferred_element_type=F32))
        k[:, cols] = lifted(jnp.dot(normed[...], wcols[steps + j], preferred_element_type=F32))
        v[:, cols] = jnp.dot(
            normed[...], wcols[2 * steps + j], preferred_element_type=F32
        ).astype(BF16)
        for head in range(2 * j, 2 * j + 2):
            cols = slice(head * HEAD_DIM, (head + 1) * HEAD_DIM)
            keys = k[:, cols]
            total = jnp.sum(keys.astype(F32), axis=0, keepdims=True)
            total = jnp.broadcast_to(total, (STATE - HEAD_DIM, HEAD_DIM))
            outer = dot_first(v[:, cols], keys)
            state[head, :HEAD_DIM, :] = outer
            state[head, HEAD_DIM:, :] = total
            mine[head, :HEAD_DIM, :] = outer.astype(BF16)
            mine[head, HEAD_DIM:, :] = total.astype(BF16)

    project(0)
    arrive(waits)
    info_row = chips[0] + chips[1] + chips[2] + chips[3]
    rows[z] = info_row
    waits = [go(rows.at[z], rows.at[z], device) for device in along_z]
    project(1)
    arrive(waits)
    expert = lax.broadcasted_iota(jnp.int32, (WAYS * lane_count, LANES), 0)
    lanes = lax.broadcasted_iota(jnp.int32, (WAYS * lane_count, LANES), 1)
    counts = jnp.zeros((WAYS * lane_count, 1), F32)
    most = jnp.zeros((WAYS * lane_count, 1), F32)
    for i in range(WAYS):
        there = (rows[i][0:1, :] - 1) == expert
        low = jnp.sum(jnp.where(there & (lanes < 4 * visits), 1.0, 0.0), axis=1, keepdims=True)
        high = jnp.sum(jnp.where(there & (lanes >= 4 * visits), 1.0, 0.0), axis=1, keepdims=True)
        counts = counts + low + high
        most = jnp.maximum(most, jnp.maximum(low, high))
    is_hot = counts > HOT - 0.5
    hot = jnp.sum(jnp.where(is_hot, expert[:, 0:1].astype(F32), 0.0), axis=0, keepdims=True)
    most = jnp.max(jnp.where(is_hot, 0.0, most), axis=0, keepdims=True)
    peak[...] = jnp.broadcast_to(most, (8, LANES))
    peak_waits = [go(peak, peaks.at[y], device) for device in along_y]
    here = (hot == (z * lane_count + x * CORES + c).astype(F32)).astype(BF16)
    beside = (hot == (z * lane_count + x * CORES + 1 - c).astype(F32)).astype(BF16)
    project(2)
    arrive(swapped)
    for fetch in fetches[-3:]:
        fetch.wait()

    @pl.loop(0, HALF // PIECE)
    def _(i):
        row = pl.ds(pl.multiple_of(i * PIECE, PIECE), PIECE)
        near[row, :] = near[row, :] * here + far[row, :] * beside

    reduce_waits = start_reduce(False)
    project(3)
    waits = [go(mine, theirs, sibling)]
    hot = jnp.broadcast_to(hot, (1, LANES)).astype(jnp.int32)
    ids = info_row[0:1, :] - 1
    wide = jnp.broadcast_to(ids, (LANES, LANES))
    tall = wide.T
    rank_lane = lax.broadcasted_iota(jnp.int32, (LANES, LANES), 1)
    rank_sub = lax.broadcasted_iota(jnp.int32, (LANES, LANES), 0)
    earlier = (wide == tall) & (rank_sub < rank_lane)
    halves = (rank_sub < 4 * visits) == (rank_lane < 4 * visits)
    rank = jnp.sum(jnp.where(earlier & halves, 1.0, 0.0), axis=0, keepdims=True).astype(jnp.int32)
    shares = info_row[1:2, :].astype(F32) / jnp.maximum(info_row[2:3, :], 1).astype(F32)
    int_ref[16:24, :] = jnp.zeros((8, LANES), jnp.int32)
    real_ref[...] = jnp.zeros((8, LANES), F32)
    tables(0, ids, rank, shares, hot, int_ref, real_ref)
    lane = lane[0:1, :]
    own = (lane >= first) & (lane < first + visits) & (ids == hot)
    seen = jnp.sum(jnp.where(own, 1.0, 0.0), axis=1, keepdims=True)
    first_lane = jnp.min(jnp.where(own, lane, 1000).astype(F32), axis=1, keepdims=True)
    last_lane = jnp.max(jnp.where(own, lane, -1).astype(F32), axis=1, keepdims=True)
    int_ref[17:18, :] = ids
    int_ref[18:19, :] = rank
    int_ref[19:20, :] = hot
    first_block = jnp.where(seen > 0.5, (first_lane.astype(jnp.int32) - first) >> 1, 0)
    last_block = (last_lane.astype(jnp.int32) - first) >> 1
    following = jnp.where(first_block + 1 >= blocks, 0, first_block + 1)
    second_block = jnp.where(seen > 1.5, last_block, following)
    int_ref[21:22, :] = jnp.where(lane == 0, first_block, second_block)
    lane_real = lane.astype(F32)
    first_share = jnp.sum(
        jnp.where(own & (lane_real == first_lane), shares, 0.0), axis=1, keepdims=True
    )
    last_share = jnp.sum(
        jnp.where(own & (lane_real == last_lane) & (seen > 1.5), shares, 0.0), axis=1, keepdims=True
    )
    real_ref[1:2, :] = shares
    real_ref[2:3, :] = jnp.where(lane == 0, first_share, last_share)
    arrive(peak_waits)
    peaks[y] = peak[...]
    top = peaks[0]
    for i in range(1, groups):
        top = jnp.maximum(top, peaks[i])
    int_ref[22:23, :] = top[0:1, :].astype(jnp.int32)

    causal = lax.broadcasted_iota(jnp.int32, (ROWS, ROWS), 0) >= lax.broadcasted_iota(
        jnp.int32, (ROWS, ROWS), 1
    )

    def within(start, stop):
        @pl.loop(start, stop)
        def _(head):
            cols = pl.ds(pl.multiple_of(head * HEAD_DIM, HEAD_DIM), HEAD_DIM)
            keys = k[:, cols]
            both = jnp.concatenate([v[:, cols], jnp.ones((tokens, HEAD_DIM), BF16)], axis=1)
            for tile in range(tiles):
                part = slice(tile * ROWS, (tile + 1) * ROWS)
                query = q[part, cols]
                scores = jnp.where(causal, dot_last(query, keys[part, :]), 0.0).astype(BF16)
                total = jnp.dot(scores, both[part, :], preferred_element_type=F32)
                if tile > 0:
                    scores = dot_last(query, keys[: tile * ROWS, :]).astype(BF16)
                    total = total + jnp.dot(
                        scores, both[: tile * ROWS, :], preferred_element_type=F32
                    )
                numer[part, cols] = total[:, :HEAD_DIM]
                denom[part, cols] = total[:, HEAD_DIM:]

    within(0, 2)
    arrive(waits)
    base = c * WAYS
    for i in range(WAYS):
        sums[i] = (state[base + i] + theirs[base + i].astype(F32)).astype(BF16)
    xs[x] = sums[x]
    waits = [go(sums.at[(x + d) % WAYS], xs.at[x], along_x[d - 1]) for d in range(1, WAYS)]
    far_waits = start_reduce(True)
    within(2, 4)
    arrive(waits)
    row_sum[...] = sum(xs[i].astype(F32) for i in range(WAYS)).astype(BF16)
    zs[z] = row_sum[...]
    waits = [go(row_sum, zs.at[z], along_z[d - 1]) for d in range(1, WAYS)]
    relay_reduce(far_waits)
    within(4, 6)
    arrive(waits)
    plane_sum[...] = sum(zs[i].astype(F32) for i in range(WAYS)).astype(BF16)
    waits = [go(plane_sum, ys.at[y], along_y[d - 1]) for d in range(1, groups)]
    total = jnp.zeros(row_sum.shape, F32)
    for i in range(WAYS):
        total = total + zs[i].astype(F32) * jnp.where(i < z, 1.0, 0.0)
    within(6, 7)
    arrive(waits)
    ys[y] = plane_sum[...]
    for i in range(groups):
        total = total + ys[i].astype(F32) * jnp.where(i < y, 1.0, 0.0)
    for i in range(WAYS):
        back[i] = total.astype(BF16)
        total = total + xs[i].astype(F32)
    heads_in[x] = back[x]
    waits = [go(back.at[(x + d) % WAYS], heads_in.at[x], along_x[d - 1]) for d in range(1, WAYS)]
    within(7, 8)
    reduce_waits = second_reduce([a + b for a, b in zip(reduce_waits, far_waits)])
    arrive(waits)
    waits = [go(heads_in, sib2, sibling)]
    later = jnp.where(c == 1, 1.0, 0.0)

    def add_prior(first_head, source):
        @pl.loop(0, WAYS)
        def _(i):
            head = first_head + i
            prior = (source[i].astype(F32) + theirs[head].astype(F32) * later).astype(BF16)
            filled = jnp.broadcast_to(prior[HEAD_DIM : HEAD_DIM + 1, :], (HEAD_DIM, HEAD_DIM))
            carried = jnp.concatenate([prior[:HEAD_DIM, :], filled], axis=0)
            cols = pl.ds(pl.multiple_of(head * HEAD_DIM, HEAD_DIM), HEAD_DIM)
            total = dot_last(q[:, cols], carried)
            ratio[:, cols] = (numer[:, cols] + total[:, :HEAD_DIM]) / (
                denom[:, cols] + total[:, HEAD_DIM:]
            )

    add_prior(base, heads_in)
    reduce_waits = gather_pieces(reduce_waits)
    arrive(waits)
    add_prior((1 - c) * WAYS, sib2)
    half = tokens // 2
    for part in range(2):
        part_rows = slice(part * half, (part + 1) * half)
        attended = norm_rows(ratio[part_rows, :], hgain_ref[...]).astype(BF16)
        resid = x_ref[part_rows, :].astype(F32) + jnp.dot(
            attended, wout_ref[...], preferred_element_type=F32
        )
        resid = resid.astype(BF16)
        resid_ref[part_rows, :] = resid
        ffn_ref[part_rows, :] = norm_rows(resid.astype(F32), fgain_ref[...]).astype(BF16)
    arrive(reduce_waits)
    for copy in copies:
        copy.wait_send()


def front(
    x, attn_gain, w_qkv, head_gain, w_out, ffn_gain, w_gate, w_up, w_down, pair_ids, gate_codes, groups
):
    tokens, width = x.shape
    packed = 2 * w_gate.shape[1] + width
    blocks = pair_ids.shape[0]
    tile = (8, LANES)
    one = (STATE, HEAD_DIM)
    some = (WAYS,) + one
    every = (HEADS,) + one
    step = 2 * HEAD_DIM
    pieces = 3 * width // step
    count = 1 + 2 * (WAYS - 1) + groups - 1 + 2 + 3 * (WAYS - 1) + groups - 1
    count += 3 + 12 + 4 * (WAYS - 1)

    def wide(*shape):
        return pltpu.VMEM(shape + (packed,), BF16)

    smem = pl.BlockSpec(memory_space=pltpu.SMEM)
    vmem = pl.BlockSpec(memory_space=pltpu.VMEM)
    hbm = pl.BlockSpec(memory_space=pl.ANY)
    return pl.pallas_call(
        functools.partial(front_kernel, groups, blocks),
        out_shape=[jax.ShapeDtypeStruct((tokens, width), BF16)] * 2
        + [jax.ShapeDtypeStruct((24, LANES), jnp.int32), jax.ShapeDtypeStruct(tile, F32)]
        + [jax.ShapeDtypeStruct((2, SLICE, packed), BF16)],
        in_specs=[smem] * 2 + [vmem] * 2 + [hbm] + [vmem] * 3 + [hbm] * 3,
        out_specs=[vmem] * 5,
        scratch_shapes=[pltpu.VMEM((tokens, width), BF16)] * 4
        + [pltpu.VMEM((pieces, width, step), BF16), pltpu.VMEM(every, F32)]
        + [pltpu.VMEM((tokens, width), F32)] * 3
        + [
            pltpu.VMEM(tile, jnp.int32),
            pltpu.VMEM((WAYS,) + tile, jnp.int32),
            pltpu.VMEM(tile, jnp.int32),
            pltpu.VMEM((WAYS,) + tile, jnp.int32),
            pltpu.VMEM(tile, F32),
            pltpu.VMEM((groups,) + tile, F32),
            pltpu.VMEM(every, BF16),
            pltpu.VMEM(every, BF16),
            pltpu.VMEM(some, BF16),
            pltpu.VMEM(some, BF16),
            pltpu.VMEM(one, BF16),
            pltpu.VMEM(some, BF16),
            pltpu.VMEM(one, BF16),
            pltpu.VMEM((groups,) + one, BF16),
            pltpu.VMEM(some, BF16),
            pltpu.VMEM(some, BF16),
            pltpu.VMEM(some, BF16),
            wide(HALF),
            wide(HALF),
            wide(2, WAYS - 1, SLICE),
            wide(2, 2, SLICE // 2),
            wide(2, SLICE),
            wide(2, WAYS - 1, PIECE),
            pltpu.SemaphoreType.DMA((pieces,)),
            pltpu.SemaphoreType.DMA((3,)),
            pltpu.SemaphoreType.DMA((count,)),
            pltpu.SemaphoreType.DMA((count,)),
        ],
        compiler_params=pltpu.CompilerParams(
            collective_id=0, has_side_effects=True, vmem_limit_bytes=LIMIT_BYTES
        ),
        name="front",
    )(
        pair_ids, gate_codes, x, attn_gain, w_qkv, head_gain, w_out, ffn_gain, w_gate, w_up, w_down
    )


def moe_kernel(
    blocks, chunks, table, weight, f_ref, base_ref, wg_ref, wu_ref, wd_ref, slice_ref, out_ref,
    *rest
):
    gather, landed = rest[:chunks], rest[chunks : 2 * chunks]
    (
        hand, zs, relay, taken, made_rows, relay_back, hand_back, partial, final, local, send, recv,
        hotw, hot_inner, hot_out, hot_local, hot_send, hot_recv,
    ) = rest[2 * chunks :]
    depth = ROWS // chunks
    width = f_ref.shape[2]
    y, z, x, c = place()
    lane = WAYS * CORES
    parity = x % 2

    def at(zz, xx, cc):
        return (y, ((zz + WAYS) % WAYS) * lane + ((xx + WAYS) % WAYS) * CORES + cc)

    sibling = at(z, x, 1 - c)
    mate = at(z, x + 1 - 2 * parity, c)
    across = at(z, x + 2 * parity - 1, c)
    up, down = at(z + 1, x, c), at(z - 1, x, c)
    greet([sibling, mate, across, up, down])
    me = parity * CORES + c
    friend = (1 - parity) * CORES + c
    pending = []
    made = {}

    def go(k, n, src, dst, device):
        copy = remote(src, dst, send.at[k, n], recv.at[k, n], device)
        copy.start()
        pending.append(copy)
        made[k, n] = copy

    def keep(k, n, src, dst):
        copy = pltpu.make_async_copy(src, dst, local.at[k, n])
        copy.start()
        made[k, "keep", n] = copy

    def arrived(k, *numbers):
        for n in numbers:
            made[k, n].wait_recv()

    def step_of(row):
        return (row + WAYS) % WAYS

    def begin(k):
        own = f_ref.at[:, pl.ds(k * depth, depth), :]
        here = gather[k].at[pl.ds(me * blocks, blocks)]
        go(k, 0, own, here, mate)
        go(k, 1, own, here, sibling)
        keep(k, 0, own, here)

    def widen(k):
        arrived(k, 0)
        there = gather[k].at[pl.ds(friend * blocks, blocks)]
        go(k, 2, there, there, sibling)

    def select(k):
        made[k, "keep", 0].wait()
        arrived(k, 1, 2)
        for row in range(WAYS):
            for j in range(SLOTS):
                hand[k, row, j] = gather[k][table[8 + row * SLOTS + j, 0]]
        go(k, 3, hand.at[k], zs.at[k, :, 1], across)
        for row in range(WAYS):
            for j in range(SLOTS):
                zs[k, row, 0, j] = gather[k][table[row * SLOTS + j, 0]]

    def climb(k):
        arrived(k, 3)
        go(k, 6, zs.at[k, step_of(z + 2), 0], relay.at[k, 0], up)
        go(k, 19, zs.at[k, step_of(z + 2), 1], relay.at[k, 1], down)
        go(k, 4, zs.at[k, step_of(z + 1)], taken.at[k, z], up)
        go(k, 5, zs.at[k, step_of(z - 1)], taken.at[k, z], down)
        keep(k, 1, zs.at[k, z], taken.at[k, z])

    def forward(k):
        arrived(k, 6)
        go(k, 7, relay.at[k, 0], taken.at[k, step_of(z - 1), 0], up)
        arrived(k, 19)
        go(k, 20, relay.at[k, 1], taken.at[k, step_of(z + 1), 1], down)

    def work(k):
        arrived(k, 4, 5, 7, 20)
        made[k, "keep", 1].wait()
        rows = taken[k].reshape(WAYS * PART * depth, width)
        gate = jnp.dot(rows, wg_ref[...], preferred_element_type=F32)
        upper = jnp.dot(rows, wu_ref[...], preferred_element_type=F32)
        inner = (jax.nn.silu(gate) * upper).astype(BF16)
        result = jnp.dot(inner, wd_ref[...], preferred_element_type=F32).astype(BF16)
        made_rows[k] = result.reshape(WAYS, SIDES, SLOTS, depth, width)
        go(k, 12, made_rows.at[k, step_of(z + 2), 0], relay_back.at[k, 0], up)
        go(k, 21, made_rows.at[k, step_of(z + 2), 1], relay_back.at[k, 1], down)
        for n, d, device in ((8, 1, up), (10, -1, down)):
            target = step_of(z + d)
            go(k, n, made_rows.at[k, target, 0], landed[k].at[pl.ds(c * 16 + z * SLOTS, SLOTS)], device)
            go(k, n + 1, made_rows.at[k, target, 1], hand_back.at[k, pl.ds(z * SLOTS, SLOTS)], device)
        keep(k, 2, made_rows.at[k, z, 0], landed[k].at[pl.ds(c * 16 + z * SLOTS, SLOTS)])
        keep(k, 3, made_rows.at[k, z, 1], hand_back.at[k, pl.ds(z * SLOTS, SLOTS)])

    def forward_back(k):
        arrived(k, 21)
        origin = step_of(z + 1)
        go(k, 14, relay_back.at[k, 1], hand_back.at[k, pl.ds(origin * SLOTS, SLOTS)], down)
        arrived(k, 12)
        origin = step_of(z - 1)
        go(k, 13, relay_back.at[k, 0], landed[k].at[pl.ds(c * 16 + origin * SLOTS, SLOTS)], up)

    def give(k):
        arrived(k, 9, 11, 14)
        made[k, "keep", 3].wait()
        go(k, 15, hand_back.at[k], landed[k].at[pl.ds(c * 16 + 8, 8)], across)
        arrived(k, 8, 10, 13)
        made[k, "keep", 2].wait()
        there = landed[k].at[pl.ds(c * 16, 8)]
        go(k, 16, there, there, sibling)

    def mirror(k):
        arrived(k, 15)
        there = landed[k].at[pl.ds(c * 16 + 8, 8)]
        go(k, 17, there, there, sibling)

    def build(k):
        arrived(k, 16, 17)

        def one(start, offset):
            def run(b, carry):
                first = start + 2 * b
                total = landed[k][table[16, first]].astype(F32) * weight[0, first]
                total = total + landed[k][table[16, first + 1]].astype(F32) * weight[0, first + 1]
                partial[k, offset + b] = total.astype(BF16)
                return carry

            return run

        row = (x // 2) * 4 * 2 * blocks
        lax.fori_loop(0, blocks, one(row + friend * 2 * blocks, blocks), 0)
        go(k, 18, partial.at[k, pl.ds(blocks, blocks)], final.at[k], mate)
        lax.fori_loop(0, blocks, one(row + me * 2 * blocks, 0), 0)

    def finish(k):
        arrived(k, 18)
        rows = slice(k * depth, (k + 1) * depth)

        def run(b, carry):
            total = base_ref[b, rows, :].astype(F32) + partial[k, b].astype(F32)
            total = total + final[k, b].astype(F32)
            for i in range(2):
                share = jnp.where(table[21, i] == b, weight[2, i], 0.0)
                total = total + hot_out[i, rows, :].astype(F32) * share
            out_ref[b, rows, :] = total.astype(BF16)
            return carry

        lax.fori_loop(0, blocks, run, 0)

    right, left = at(z, x + 1, c), at(z, x - 1, c)
    ring = ((x, right, left), (z, up, down))
    hot_made = {}

    def hot_go(n, src, dst, device):
        copy = remote(src, dst, hot_send.at[n], hot_recv.at[n], device)
        copy.start()
        pending.append(copy)
        hot_made[n] = copy

    short = SLICE // 2

    def hot_rows(order, spot, shift=0, size=SLICE):
        row = order * (HALF // 2) + ((spot + WAYS) % WAYS) * SLICE + shift
        return hotw.at[c, pl.ds(row, size)]

    def hot_begin(order, part):
        spot, plus, minus = ring[order]
        shift = part * short
        piece = slice_ref.at[order, pl.ds(shift, short)]
        there = hot_rows(order, spot, shift, short)
        base = 16 * order + 8 * part
        hot_go(base, piece, there, plus)
        hot_go(base + 1, piece, there, minus)
        hot_go(base + 2, piece, there, sibling)
        copy = pltpu.make_async_copy(piece, there, hot_local.at[2 * order + part])
        copy.start()
        hot_made["keep", order, part] = copy

    def hot_relay(order, part):
        spot, plus, minus = ring[order]
        base = 16 * order + 8 * part
        shift = part * short
        for n, neighbour in ((0, spot - 1), (1, spot + 1)):
            hot_made[base + n].wait_recv()
            there = hot_rows(order, neighbour, shift, short)
            if n == part:
                hot_go(base + 3, there, there, plus if n == 0 else minus)
            hot_go(base + 4 + n, there, there, sibling)

    def hot_last(order, part):
        spot = ring[order][0]
        base = 16 * order + 8 * part
        hot_made[base + 3].wait_recv()
        there = hot_rows(order, spot + 2, part * short, short)
        hot_go(base + 6, there, there, sibling)

    def hot_ready():
        for order in range(2):
            for part in range(2):
                hot_made["keep", order, part].wait()
                for n in (2, 4, 5, 6):
                    hot_made[16 * order + 8 * part + n].wait_recv()

    hidden = wg_ref.shape[1]
    def hot_first():
        rows = jnp.concatenate([f_ref[table[21, 0]], f_ref[table[21, 1]]], axis=0)
        low, high = rows[:, :HALF], rows[:, HALF:]

        def both(start):
            cols = slice(start, start + hidden)
            return jnp.dot(low, hotw[0, :, cols], preferred_element_type=F32) + jnp.dot(
                high, hotw[1, :, cols], preferred_element_type=F32
            )

        hot_inner[...] = (jax.nn.silu(both(0)) * both(hidden)).astype(BF16)

    def hot_second():
        cols = slice(2 * hidden, 2 * hidden + width)
        result = jnp.dot(hot_inner[:, :HALF], hotw[0, :, cols], preferred_element_type=F32)
        result = result + jnp.dot(
            hot_inner[:, HALF:], hotw[1, 2 * HALF - hidden :, cols], preferred_element_type=F32
        )
        hot_out[...] = result.astype(BF16).reshape(2, ROWS, width)

    stages = [widen, select, climb, forward, work, forward_back, give, mirror, build]
    begin(0)
    begin(1)
    hot_begin(1, 0)
    hot_begin(1, 1)
    extras = {
        2: ((hot_relay, 1, 0), (hot_begin, 0, 0)),
        3: ((hot_relay, 1, 1),),
        4: ((hot_last, 1, 0), (hot_relay, 0, 0)),
        5: ((hot_last, 1, 1), (hot_begin, 0, 1)),
        7: ((hot_last, 0, 0), (hot_relay, 0, 1)),
        9: ((hot_last, 0, 1),),
        chunks + 3: ((hot_ready,), (hot_first,)),
        chunks + 4: ((hot_second,),),
    }
    lag_of = len(stages)
    done = 0
    for step in range(chunks + lag_of):
        if step + 2 < chunks:
            begin(step + 2)
        for lag in reversed(range(lag_of)):
            if 0 <= step - lag < chunks:
                stages[lag](step - lag)
        for extra in extras.get(step, ()):
            extra[0](*extra[1:])
        if step > chunks + 4:
            while done <= min(step - lag_of, chunks - 1):
                finish(done)
                done += 1
    for copy in pending:
        copy.wait_send()


def moe(table, weight, ffn_in, base, w_gate, w_up, w_down, hot_slices):
    blocks, rows, width = ffn_in.shape
    packed = hot_slices.shape[2]
    chunks = CHUNKS
    depth = rows // chunks
    pair = 2 * CORES * blocks
    whole = pl.BlockSpec(memory_space=pltpu.VMEM)
    return pl.pallas_call(
        functools.partial(moe_kernel, blocks, chunks),
        out_shape=jax.ShapeDtypeStruct(base.shape, BF16),
        in_specs=[pl.BlockSpec(memory_space=pltpu.SMEM)] * 2 + [whole] * 6,
        out_specs=whole,
        scratch_shapes=[pltpu.VMEM((pair, depth, width), BF16)] * chunks
        + [pltpu.VMEM((CORES * 16, depth, width), BF16)] * chunks
        + [
            pltpu.VMEM((chunks, WAYS, SLOTS, depth, width), BF16),
            pltpu.VMEM((chunks, WAYS, SIDES, SLOTS, depth, width), BF16),
            pltpu.VMEM((chunks, SIDES, SLOTS, depth, width), BF16),
            pltpu.VMEM((chunks, WAYS, SIDES, SLOTS, depth, width), BF16),
            pltpu.VMEM((chunks, WAYS, SIDES, SLOTS, depth, width), BF16),
            pltpu.VMEM((chunks, SIDES, SLOTS, depth, width), BF16),
            pltpu.VMEM((chunks, WAYS * SLOTS, depth, width), BF16),
            pltpu.VMEM((chunks, 2 * blocks, depth, width), BF16),
            pltpu.VMEM((chunks, blocks, depth, width), BF16),
            pltpu.SemaphoreType.DMA((chunks, 4)),
            pltpu.SemaphoreType.DMA((chunks, 22)),
            pltpu.SemaphoreType.DMA((chunks, 22)),
            pltpu.VMEM((CORES, HALF, packed), BF16),
            pltpu.VMEM((2 * rows, w_gate.shape[1]), BF16),
            pltpu.VMEM((2, rows, width), BF16),
            pltpu.SemaphoreType.DMA((4,)),
            pltpu.SemaphoreType.DMA((32,)),
            pltpu.SemaphoreType.DMA((32,)),
        ],
        compiler_params=pltpu.CompilerParams(
            collective_id=1, has_side_effects=True, vmem_limit_bytes=67043328
        ),
        name="moe",
    )(table, weight, ffn_in, base, w_gate, w_up, w_down, hot_slices)


def tables_kernel(turn, int_ref, real_ref, out_int, out_real):
    out_int[...] = int_ref[...]
    out_real[...] = real_ref[...]
    out_real[2:3, :] = jnp.zeros((1, LANES), F32)
    tables(
        turn[0], int_ref[17:18, :], int_ref[18:19, :], real_ref[1:2, :], int_ref[19:20, :],
        out_int, out_real,
    )


def later_tables(turn, ints, reals):
    return pl.pallas_call(
        tables_kernel,
        out_shape=[
            jax.ShapeDtypeStruct(ints.shape, ints.dtype),
            jax.ShapeDtypeStruct(reals.shape, reals.dtype),
        ],
        in_specs=[pl.BlockSpec(memory_space=pltpu.SMEM)]
        + [pl.BlockSpec(memory_space=pltpu.VMEM)] * 2,
        out_specs=[pl.BlockSpec(memory_space=pltpu.VMEM)] * 2,
        name="later_tables",
    )(turn, ints, reals)


def body(
    hidden_in, attn_gain, w_qkv, head_gain, w_out, ffn_gain, w_gate, w_up, w_down, pair_ids, gate_codes
):
    tokens, width = hidden_in.shape
    blocks = tokens // ROWS
    groups = lax.axis_size("grp")
    weights = (w_gate[0], w_up[0], w_down[0])
    resid, ffn_in, ints, reals, hot_slices = front(
        hidden_in, attn_gain[None], w_qkv, head_gain[None], w_out, ffn_gain[None], *weights, pair_ids,
        gate_codes, groups,
    )
    resid = resid.reshape(blocks, ROWS, width)
    ffn_in = ffn_in.reshape(blocks, ROWS, width)

    def unfinished(carry):
        return carry[0] * SLOTS < carry[1][22, 0]

    def one(carry):
        turn, ints, reals, total = carry
        total = moe(ints, reals, ffn_in, total, *weights, hot_slices)
        turn = turn + 1
        ints, reals = lax.cond(
            turn * SLOTS < ints[22, 0],
            lambda pair: tuple(later_tables(turn[None], *pair)),
            lambda pair: pair,
            (ints, reals),
        )
        return turn, ints, reals, total

    total = lax.while_loop(unfinished, one, (jnp.int32(0), ints, reals, resid))[3]
    return total.reshape(tokens, width)


def solution(mesh):
    return jax.shard_map(
        body,
        mesh=mesh,
        in_specs=(
            P(("grp", "seq"), None), P(), P(), P(), P(), P(),
            P("seq", None, None), P("seq", None, None), P("seq", None, None),
            P(("grp", "seq"), None), P(("grp", "seq"), None),
        ),
        out_specs=P(("grp", "seq"), None),
        check_vma=False,
    )
```

```python
import functools

import jax
import jax.numpy as jnp
from jax import lax
from jax.experimental import pallas as pl
from jax.experimental.pallas import tpu as pltpu
from jax.sharding import PartitionSpec as P

HEADS = 8
HEAD_DIM = 128
ROWS = 128
EPS = 1e-06
WAYS = 4
CORES = 2
SLOTS = 2
SIDES = 2
PART = SIDES * SLOTS
CHUNKS = 8
STATE = 144
LIMIT = 8
LANES = 128
HALF = 512
TILE = 256
SLICE = 64
PIECE = 16
HOT = 15
MESH = pl.DeviceIdType.MESH
F32 = jnp.float32
BF16 = jnp.bfloat16
LIMIT_BYTES = 60 * 1024 * 1024


def place():
    seq = lax.axis_index("seq")
    return lax.axis_index("grp"), seq // (WAYS * CORES), (seq // CORES) % WAYS, seq % CORES


def remote(src, dst, send, recv, device):
    return pltpu.make_async_remote_copy(
        src_ref=src, dst_ref=dst, send_sem=send, recv_sem=recv, device_id=device, device_id_type=MESH
    )


def greet(devices):
    barrier = pltpu.get_barrier_semaphore()
    for device in devices:
        pl.semaphore_signal(barrier, inc=1, device_id=device, device_id_type=MESH)
    pl.semaphore_wait(barrier, len(devices))


def norm_rows(values, gain):
    return values * lax.rsqrt(jnp.mean(values * values, axis=-1, keepdims=True) + EPS) * gain


def dot_last(a, b):
    return lax.dot_general(a, b, (((1,), (1,)), ((), ())), preferred_element_type=F32)


def dot_first(a, b):
    return lax.dot_general(a, b, (((0,), (0,)), ((), ())), preferred_element_type=F32)


def lifted(values):
    return jnp.where(values > 0.0, values + 1.0, jnp.exp(jnp.minimum(values, 0.0))).astype(BF16)


def tables(turn, ids, rank, shares, hot, out_int, out_real):
    y, z, x, c = place()
    half = x // 2
    other = (x + 2 * (x % 2) - 1 + WAYS) % WAYS
    span = LANES * 7 // 16
    lane = lax.broadcasted_iota(jnp.int32, (1, LANES), 1)
    local = lane - half * span
    near = (local >= 0) & (local < span)
    place_of = rank - turn * SLOTS
    usable = near & (ids >= 0) & (ids != hot) & (place_of >= 0) & (place_of < SLOTS)
    slot = lax.broadcasted_iota(jnp.int32, (16, LANES), 0)
    column = jnp.where(slot >= 8, other, x)
    expert = ((slot & 7) >> 1) * (WAYS * CORES) + column * CORES + c
    key = jnp.where(usable, ids * SLOTS + place_of, -1)
    hit = key == expert * SLOTS + (slot & 1)
    source = jnp.sum(jnp.where(hit, local >> 1, 0).astype(F32), axis=1, keepdims=True)
    out_int[0:16, :] = jnp.broadcast_to(source, (16, LANES)).astype(jnp.int32)
    here = (ids >> 1) & 3
    which = jnp.where(here == other, 1, 0)
    mine = usable & ((here == x) | (here == other))
    index = (ids & 1) * 16 + which * 8 + (ids >> 3) * SLOTS + place_of
    out_int[16:17, :] = jnp.where(mine, index, 0)
    out_real[0:1, :] = jnp.where(mine, shares, 0.0)


def front_kernel(
    groups, blocks, pairs, codes, x_ref, again_ref, wqkv_ref, hgain_ref, wout_ref, fgain_ref,
    wg_ref, wu_ref, wd_ref, resid_ref, ffn_ref, int_ref, real_ref, hot_ref,
    normed, q, k, v, wcols, state, ratio, numer, denom,
    chip, chips, sib, rows, peak, peaks,
    mine, theirs, sums, xs, row_sum, zs, plane_sum, ys, back, heads_in, sib2,
    near, far, slices, halves_in, summed, pieces_in, loads, stay, send, recv,
):
    y, z, x, c = place()
    lane_count = WAYS * CORES
    tokens, width = x_ref.shape
    tiles = tokens // ROWS
    step = 2 * HEAD_DIM
    steps = width // step
    half = tokens // 2

    def at(yy, zz, xx, cc):
        return (yy, zz * lane_count + xx * CORES + cc)

    sibling = at(y, z, x, 1 - c)
    along_x = [at(y, z, (x + d) % WAYS, c) for d in range(1, WAYS)]
    along_z = [at(y, (z + d) % WAYS, x, c) for d in range(1, WAYS)]
    along_y = [at((y + d) % groups, z, x, c) for d in range(1, groups)]
    fetches = []
    for j in range(3 * steps):
        fetch = pltpu.make_async_copy(
            wqkv_ref.at[:, pl.ds(j * step, step)], wcols.at[j], loads.at[j]
        )
        fetch.start()
        fetches.append(fetch)
    greet([sibling] + along_x + along_z + along_y)
    copies = []

    def go(src, dst, device):
        n = len(copies)
        copy = remote(src, dst, send.at[n], recv.at[n], device)
        copy.start()
        copies.append(copy)
        return copy

    def arrive(waits):
        for copy in waits:
            copy.wait_recv()

    hidden = wg_ref.shape[1]
    offset = wd_ref.shape[0] - HALF
    lanes_of = (
        (wg_ref, HALF, pl.ds(0, hidden)),
        (wu_ref, HALF, pl.ds(hidden, hidden)),
        (wd_ref, offset, pl.ds(2 * hidden, width)),
    )
    ring = (
        (x, along_x[0], along_x[2], along_x[1]),
        (z, along_z[0], along_z[2], along_z[1]),
    )
    swapped = []
    for n, (source, jump, span) in enumerate(lanes_of):
        there = source.at[pl.ds(jump * (1 - c), HALF), :]
        swapped.append(go(there, far.at[:, span], sibling))
        local = pltpu.make_async_copy(
            source.at[pl.ds(jump * c, HALF), :], near.at[:, span], stay.at[n]
        )
        local.start()
        fetches.append(local)

    def start_reduce(far_half):
        waits = []
        for order, (spot, plus, minus, _) in enumerate(ring):
            top = order * (HALF // 2)

            def part(i, shift=0, size=SLICE):
                row = top + ((spot + i + WAYS) % WAYS) * SLICE + shift
                return near.at[pl.ds(row, size)]

            short = SLICE // 2
            if far_half:
                waits.append(
                    (
                        go(part(2, 0, short), halves_in.at[order, 0], plus),
                        go(part(2, short, short), halves_in.at[order, 1], minus),
                    )
                )
            else:
                waits.append(
                    (
                        go(part(1), slices.at[order, 0], plus),
                        go(part(-1), slices.at[order, 1], minus),
                    )
                )
        return waits

    def relay_reduce(waits):
        short = SLICE // 2
        for order, (_, plus, minus, _) in enumerate(ring):
            arrive(waits[order])
            waits[order] = (
                go(halves_in.at[order, 0], slices.at[order, 2, pl.ds(0, short)], plus),
                go(halves_in.at[order, 1], slices.at[order, 2, pl.ds(short, short)], minus),
            )

    def second_reduce(waits):
        later = []
        for order, (spot, _, _, _) in enumerate(ring):
            arrive(waits[order])
            top = order * (HALF // 2) + spot * SLICE

            @pl.loop(0, SLICE // PIECE)
            def _(i):
                row = pl.multiple_of(i * PIECE, PIECE)
                base_rows = pl.ds(pl.multiple_of(top + row, PIECE), PIECE)
                row = pl.ds(row, PIECE)
                total = near[base_rows, :] + slices[order, 0, row, :]
                summed[order, row, :] = total + (slices[order, 1, row, :] + slices[order, 2, row, :])

            spot, plus, minus, opposite = ring[1 - order]
            for d, device in ((1, plus), (2, opposite), (3, minus)):
                piece = summed.at[order, pl.ds(((spot + d) % WAYS) * PIECE, PIECE)]
                later.append(go(piece, pieces_in.at[order, d - 1], device))
        return later

    def gather_pieces(waits):
        arrive(waits)
        later = []
        for order in range(2):
            spot, plus, minus, opposite = ring[1 - order]
            row = pl.ds(pl.multiple_of(spot * PIECE, PIECE), PIECE)
            total = summed[order, row, :] + pieces_in[order, 0]
            hot_ref[order, row, :] = total + (pieces_in[order, 1] + pieces_in[order, 2])
            for device in (plus, opposite, minus):
                later.append(go(hot_ref.at[order, row], hot_ref.at[order, row], device))
        return later

    visits = 2 * blocks
    lane = lax.broadcasted_iota(jnp.int32, (8, LANES), 1)
    sub = lax.broadcasted_iota(jnp.int32, (8, LANES), 0)
    first = (x * CORES + c) * visits
    info = jnp.zeros((8, LANES), jnp.int32)
    for b in range(blocks):
        code = codes[:, b : b + 1]
        pair = pairs[:, b : b + 1] + 1
        both = code[0:1, :] + code[1:2, :]
        for j in range(2):
            here = lane == first + (2 * b + j)
            value = jnp.where(
                sub == 0, pair[j : j + 1, :], jnp.where(sub == 1, code[j : j + 1, :], both)
            )
            info = jnp.where(here & (sub < 3), value, info)
    chip[...] = info
    waits = [go(chip, sib, sibling)]

    @pl.loop(0, tiles)
    def _(i):
        rows_i = pl.ds(pl.multiple_of(i * ROWS, ROWS), ROWS)
        normed[rows_i, :] = norm_rows(x_ref[rows_i, :].astype(F32), again_ref[...]).astype(BF16)

    arrive(waits)
    chips[x] = info + sib[...]
    waits = [go(chips.at[x], chips.at[x], device) for device in along_x]

    def project(j):
        for part in range(3):
            fetches[part * steps + j].wait()
        cols = slice(j * step, (j + 1) * step)

        @pl.loop(0, 2)
        def _(i):
            part = pl.ds(pl.multiple_of(i * half, PIECE), half)
            rows_in = normed[part, :]
            q[part, cols] = lifted(jnp.dot(rows_in, wcols[j], preferred_element_type=F32))
            k[part, cols] = lifted(jnp.dot(rows_in, wcols[steps + j], preferred_element_type=F32))
            v[part, cols] = jnp.dot(
                rows_in, wcols[2 * steps + j], preferred_element_type=F32
            ).astype(BF16)

        for head in range(2 * j, 2 * j + 2):
            cols = slice(head * HEAD_DIM, (head + 1) * HEAD_DIM)
            keys = k[:, cols]
            total = jnp.sum(keys.astype(F32), axis=0, keepdims=True)
            total = jnp.broadcast_to(total, (STATE - HEAD_DIM, HEAD_DIM))
            outer = dot_first(v[:, cols], keys)
            state[head, :HEAD_DIM, :] = outer
            state[head, HEAD_DIM:, :] = total
            mine[head, :HEAD_DIM, :] = outer.astype(BF16)
            mine[head, HEAD_DIM:, :] = total.astype(BF16)

    project(0)
    arrive(waits)
    info_row = chips[0] + chips[1] + chips[2] + chips[3]
    rows[z] = info_row
    waits = [go(rows.at[z], rows.at[z], device) for device in along_z]
    project(1)
    arrive(waits)
    expert = lax.broadcasted_iota(jnp.int32, (WAYS * lane_count, LANES), 0)
    lanes = lax.broadcasted_iota(jnp.int32, (WAYS * lane_count, LANES), 1)
    counts = jnp.zeros((WAYS * lane_count, 1), F32)
    most = jnp.zeros((WAYS * lane_count, 1), F32)
    for i in range(WAYS):
        there = (rows[i][0:1, :] - 1) == expert
        low = jnp.sum(jnp.where(there & (lanes < 4 * visits), 1.0, 0.0), axis=1, keepdims=True)
        high = jnp.sum(jnp.where(there & (lanes >= 4 * visits), 1.0, 0.0), axis=1, keepdims=True)
        counts = counts + low + high
        most = jnp.maximum(most, jnp.maximum(low, high))
    is_hot = counts > HOT - 0.5
    hot = jnp.sum(jnp.where(is_hot, expert[:, 0:1].astype(F32), 0.0), axis=0, keepdims=True)
    most = jnp.max(jnp.where(is_hot, 0.0, most), axis=0, keepdims=True)
    peak[...] = jnp.broadcast_to(most, (8, LANES))
    peak_waits = [go(peak, peaks.at[y], device) for device in along_y]
    here = (hot == (z * lane_count + x * CORES + c).astype(F32)).astype(BF16)
    beside = (hot == (z * lane_count + x * CORES + 1 - c).astype(F32)).astype(BF16)
    project(2)
    arrive(swapped)
    for fetch in fetches[-3:]:
        fetch.wait()

    @pl.loop(0, HALF // PIECE)
    def _(i):
        row = pl.ds(pl.multiple_of(i * PIECE, PIECE), PIECE)
        near[row, :] = near[row, :] * here + far[row, :] * beside

    reduce_waits = start_reduce(False)
    project(3)
    waits = [go(mine, theirs, sibling)]
    hot = jnp.broadcast_to(hot, (1, LANES)).astype(jnp.int32)
    ids = info_row[0:1, :] - 1
    wide = jnp.broadcast_to(ids, (LANES, LANES))
    tall = wide.T
    rank_lane = lax.broadcasted_iota(jnp.int32, (LANES, LANES), 1)
    rank_sub = lax.broadcasted_iota(jnp.int32, (LANES, LANES), 0)
    earlier = (wide == tall) & (rank_sub < rank_lane)
    halves = (rank_sub < 4 * visits) == (rank_lane < 4 * visits)
    rank = jnp.sum(jnp.where(earlier & halves, 1.0, 0.0), axis=0, keepdims=True).astype(jnp.int32)
    shares = info_row[1:2, :].astype(F32) / jnp.maximum(info_row[2:3, :], 1).astype(F32)
    int_ref[16:24, :] = jnp.zeros((8, LANES), jnp.int32)
    real_ref[...] = jnp.zeros((8, LANES), F32)
    tables(0, ids, rank, shares, hot, int_ref, real_ref)
    lane = lane[0:1, :]
    own = (lane >= first) & (lane < first + visits) & (ids == hot)
    seen = jnp.sum(jnp.where(own, 1.0, 0.0), axis=1, keepdims=True)
    first_lane = jnp.min(jnp.where(own, lane, 1000).astype(F32), axis=1, keepdims=True)
    last_lane = jnp.max(jnp.where(own, lane, -1).astype(F32), axis=1, keepdims=True)
    int_ref[17:18, :] = ids
    int_ref[18:19, :] = rank
    int_ref[19:20, :] = hot
    first_block = jnp.where(seen > 0.5, (first_lane.astype(jnp.int32) - first) >> 1, 0)
    last_block = (last_lane.astype(jnp.int32) - first) >> 1
    following = jnp.where(first_block + 1 >= blocks, 0, first_block + 1)
    second_block = jnp.where(seen > 1.5, last_block, following)
    int_ref[21:22, :] = jnp.where(lane == 0, first_block, second_block)
    lane_real = lane.astype(F32)
    first_share = jnp.sum(
        jnp.where(own & (lane_real == first_lane), shares, 0.0), axis=1, keepdims=True
    )
    last_share = jnp.sum(
        jnp.where(own & (lane_real == last_lane) & (seen > 1.5), shares, 0.0), axis=1, keepdims=True
    )
    real_ref[1:2, :] = shares
    real_ref[2:3, :] = jnp.where(lane == 0, first_share, last_share)
    arrive(peak_waits)
    peaks[y] = peak[...]
    top = peaks[0]
    for i in range(1, groups):
        top = jnp.maximum(top, peaks[i])
    int_ref[22:23, :] = top[0:1, :].astype(jnp.int32)

    causal = lax.broadcasted_iota(jnp.int32, (ROWS, ROWS), 0) >= lax.broadcasted_iota(
        jnp.int32, (ROWS, ROWS), 1
    )

    def within(start, stop):
        @pl.loop(start, stop)
        def _(head):
            cols = pl.ds(pl.multiple_of(head * HEAD_DIM, HEAD_DIM), HEAD_DIM)
            keys = k[:, cols]
            both = jnp.concatenate([v[:, cols], jnp.ones((tokens, HEAD_DIM), BF16)], axis=1)
            for tile in range(tiles):
                part = slice(tile * ROWS, (tile + 1) * ROWS)
                query = q[part, cols]
                scores = jnp.where(causal, dot_last(query, keys[part, :]), 0.0).astype(BF16)
                total = jnp.dot(scores, both[part, :], preferred_element_type=F32)
                if tile > 0:
                    scores = dot_last(query, keys[: tile * ROWS, :]).astype(BF16)
                    total = total + jnp.dot(
                        scores, both[: tile * ROWS, :], preferred_element_type=F32
                    )
                numer[part, cols] = total[:, :HEAD_DIM]
                denom[part, cols] = total[:, HEAD_DIM:]

    within(0, 2)
    arrive(waits)
    base = c * WAYS
    for i in range(WAYS):
        sums[i] = (state[base + i] + theirs[base + i].astype(F32)).astype(BF16)
    xs[x] = sums[x]
    waits = [go(sums.at[(x + d) % WAYS], xs.at[x], along_x[d - 1]) for d in range(1, WAYS)]
    far_waits = start_reduce(True)
    within(2, 4)
    arrive(waits)
    row_sum[...] = sum(xs[i].astype(F32) for i in range(WAYS)).astype(BF16)
    zs[z] = row_sum[...]
    waits = [go(row_sum, zs.at[z], along_z[d - 1]) for d in range(1, WAYS)]
    relay_reduce(far_waits)
    within(4, 6)
    arrive(waits)
    plane_sum[...] = sum(zs[i].astype(F32) for i in range(WAYS)).astype(BF16)
    waits = [go(plane_sum, ys.at[y], along_y[d - 1]) for d in range(1, groups)]
    total = jnp.zeros(row_sum.shape, F32)
    for i in range(WAYS):
        total = total + zs[i].astype(F32) * jnp.where(i < z, 1.0, 0.0)
    within(6, 7)
    arrive(waits)
    ys[y] = plane_sum[...]
    for i in range(groups):
        total = total + ys[i].astype(F32) * jnp.where(i < y, 1.0, 0.0)
    for i in range(WAYS):
        back[i] = total.astype(BF16)
        total = total + xs[i].astype(F32)
    heads_in[x] = back[x]
    waits = [go(back.at[(x + d) % WAYS], heads_in.at[x], along_x[d - 1]) for d in range(1, WAYS)]
    within(7, 8)
    reduce_waits = second_reduce([a + b for a, b in zip(reduce_waits, far_waits)])
    arrive(waits)
    waits = [go(heads_in, sib2, sibling)]
    later = jnp.where(c == 1, 1.0, 0.0)

    def add_prior(first_head, source):
        @pl.loop(0, WAYS)
        def _(i):
            head = first_head + i
            prior = (source[i].astype(F32) + theirs[head].astype(F32) * later).astype(BF16)
            filled = jnp.broadcast_to(prior[HEAD_DIM : HEAD_DIM + 1, :], (HEAD_DIM, HEAD_DIM))
            carried = jnp.concatenate([prior[:HEAD_DIM, :], filled], axis=0)
            cols = pl.ds(pl.multiple_of(head * HEAD_DIM, HEAD_DIM), HEAD_DIM)
            total = dot_last(q[:, cols], carried)
            ratio[:, cols] = (numer[:, cols] + total[:, :HEAD_DIM]) / (
                denom[:, cols] + total[:, HEAD_DIM:]
            )

    add_prior(base, heads_in)
    reduce_waits = gather_pieces(reduce_waits)
    arrive(waits)
    add_prior((1 - c) * WAYS, sib2)

    @pl.loop(0, 2)
    def _(part):
        part_rows = pl.ds(pl.multiple_of(part * half, PIECE), half)
        attended = norm_rows(ratio[part_rows, :], hgain_ref[...]).astype(BF16)
        resid = x_ref[part_rows, :].astype(F32) + jnp.dot(
            attended, wout_ref[...], preferred_element_type=F32
        )
        resid = resid.astype(BF16)
        resid_ref[part_rows, :] = resid
        ffn_ref[part_rows, :] = norm_rows(resid.astype(F32), fgain_ref[...]).astype(BF16)
    arrive(reduce_waits)
    for copy in copies:
        copy.wait_send()


def front(
    x, attn_gain, w_qkv, head_gain, w_out, ffn_gain, w_gate, w_up, w_down, pair_ids, gate_codes, groups
):
    tokens, width = x.shape
    packed = 2 * w_gate.shape[1] + width
    blocks = pair_ids.shape[1]
    tile = (8, LANES)
    one = (STATE, HEAD_DIM)
    some = (WAYS,) + one
    every = (HEADS,) + one
    step = 2 * HEAD_DIM
    pieces = 3 * width // step
    count = 1 + 2 * (WAYS - 1) + groups - 1 + 2 + 3 * (WAYS - 1) + groups - 1
    count += 3 + 12 + 4 * (WAYS - 1)

    def wide(*shape):
        return pltpu.VMEM(shape + (packed,), BF16)

    vmem = pl.BlockSpec(memory_space=pltpu.VMEM)
    hbm = pl.BlockSpec(memory_space=pl.ANY)
    return pl.pallas_call(
        functools.partial(front_kernel, groups, blocks),
        out_shape=[jax.ShapeDtypeStruct((tokens, width), BF16)] * 2
        + [jax.ShapeDtypeStruct((24, LANES), jnp.int32), jax.ShapeDtypeStruct(tile, F32)]
        + [jax.ShapeDtypeStruct((2, SLICE, packed), BF16)],
        in_specs=[vmem] * 4 + [hbm] + [vmem] * 3 + [hbm] * 3,
        out_specs=[vmem] * 5,
        scratch_shapes=[pltpu.VMEM((tokens, width), BF16)] * 4
        + [pltpu.VMEM((pieces, width, step), BF16), pltpu.VMEM(every, F32)]
        + [pltpu.VMEM((tokens, width), F32)] * 3
        + [
            pltpu.VMEM(tile, jnp.int32),
            pltpu.VMEM((WAYS,) + tile, jnp.int32),
            pltpu.VMEM(tile, jnp.int32),
            pltpu.VMEM((WAYS,) + tile, jnp.int32),
            pltpu.VMEM(tile, F32),
            pltpu.VMEM((groups,) + tile, F32),
            pltpu.VMEM(every, BF16),
            pltpu.VMEM(every, BF16),
            pltpu.VMEM(some, BF16),
            pltpu.VMEM(some, BF16),
            pltpu.VMEM(one, BF16),
            pltpu.VMEM(some, BF16),
            pltpu.VMEM(one, BF16),
            pltpu.VMEM((groups,) + one, BF16),
            pltpu.VMEM(some, BF16),
            pltpu.VMEM(some, BF16),
            pltpu.VMEM(some, BF16),
            wide(HALF),
            wide(HALF),
            wide(2, WAYS - 1, SLICE),
            wide(2, 2, SLICE // 2),
            wide(2, SLICE),
            wide(2, WAYS - 1, PIECE),
            pltpu.SemaphoreType.DMA((pieces,)),
            pltpu.SemaphoreType.DMA((3,)),
            pltpu.SemaphoreType.DMA((count,)),
            pltpu.SemaphoreType.DMA((count,)),
        ],
        compiler_params=pltpu.CompilerParams(
            collective_id=0, has_side_effects=True, vmem_limit_bytes=LIMIT_BYTES
        ),
        name="front",
    )(
        pair_ids, gate_codes, x, attn_gain, w_qkv, head_gain, w_out, ffn_gain, w_gate, w_up, w_down
    )


def moe_kernel(
    blocks, chunks, table, weight, f_ref, base_ref, wg_ref, wu_ref, wd_ref, slice_ref, out_ref,
    *rest
):
    gather, landed = rest[:chunks], rest[chunks : 2 * chunks]
    (
        hand, zs, relay, taken, made_rows, relay_back, hand_back, partial, final, local, send, recv,
        inside, hotw, hot_inner, hot_out, hot_local, hot_send, hot_recv,
    ) = rest[2 * chunks :]
    depth = ROWS // chunks
    width = f_ref.shape[2]
    hidden = wg_ref.shape[1]
    y, z, x, c = place()
    lane = WAYS * CORES
    parity = x % 2

    def at(zz, xx, cc):
        return (y, ((zz + WAYS) % WAYS) * lane + ((xx + WAYS) % WAYS) * CORES + cc)

    sibling = at(z, x, 1 - c)
    mate = at(z, x + 1 - 2 * parity, c)
    across = at(z, x + 2 * parity - 1, c)
    up, down = at(z + 1, x, c), at(z - 1, x, c)
    greet([sibling, mate, across, up, down])
    me = parity * CORES + c
    friend = (1 - parity) * CORES + c
    pending = []
    made = {}

    def go(k, n, src, dst, device):
        copy = remote(src, dst, send.at[k, n], recv.at[k, n], device)
        copy.start()
        pending.append(copy)
        made[k, n] = copy

    def keep(k, n, src, dst):
        copy = pltpu.make_async_copy(src, dst, local.at[k, n])
        copy.start()
        made[k, "keep", n] = copy

    def arrived(k, *numbers):
        for n in numbers:
            made[k, n].wait_recv()

    def step_of(row):
        return (row + WAYS) % WAYS

    def begin(k):
        own = f_ref.at[:, pl.ds(k * depth, depth), :]
        here = gather[k].at[pl.ds(me * blocks, blocks)]
        go(k, 0, own, here, mate)
        go(k, 1, own, here, sibling)
        keep(k, 0, own, here)

    def widen(k):
        arrived(k, 0)
        there = gather[k].at[pl.ds(friend * blocks, blocks)]
        go(k, 2, there, there, sibling)

    def select(k):
        made[k, "keep", 0].wait()
        arrived(k, 1, 2)
        for row in range(WAYS):
            for j in range(SLOTS):
                hand[k, row, j] = gather[k][table[8 + row * SLOTS + j, 0]]
        go(k, 3, hand.at[k], zs.at[k, :, 1], across)
        for row in range(WAYS):
            for j in range(SLOTS):
                zs[k, row, 0, j] = gather[k][table[row * SLOTS + j, 0]]

    def climb(k):
        arrived(k, 3)
        go(k, 6, zs.at[k, step_of(z + 2), 0], relay.at[k, 0], up)
        go(k, 19, zs.at[k, step_of(z + 2), 1], relay.at[k, 1], down)
        go(k, 4, zs.at[k, step_of(z + 1)], taken.at[k, z], up)
        go(k, 5, zs.at[k, step_of(z - 1)], taken.at[k, z], down)
        keep(k, 1, zs.at[k, z], taken.at[k, z])

    def forward(k):
        arrived(k, 6)
        go(k, 7, relay.at[k, 0], taken.at[k, step_of(z - 1), 0], up)
        arrived(k, 19)
        go(k, 20, relay.at[k, 1], taken.at[k, step_of(z + 1), 1], down)

    def work(k):
        arrived(k, 4, 5, 7, 20)
        made[k, "keep", 1].wait()
        def rise(cols):
            rows = taken[k].reshape(WAYS * PART * depth, width)
            gate = jnp.dot(rows, wg_ref[:, cols], preferred_element_type=F32)
            upper = jnp.dot(rows, wu_ref[:, cols], preferred_element_type=F32)
            inside[:, cols] = (jax.nn.silu(gate) * upper).astype(BF16)

        @pl.loop(0, hidden // TILE)
        def _(i):
            rise(pl.ds(pl.multiple_of(i * TILE, TILE), TILE))

        if hidden % TILE:
            rise(slice(hidden - hidden % TILE, hidden))

        @pl.loop(0, width // TILE)
        def _(i):
            cols = pl.ds(pl.multiple_of(i * TILE, TILE), TILE)
            result = jnp.dot(inside[...], wd_ref[:, cols], preferred_element_type=F32)
            made_rows[k, :, :, :, :, cols] = result.astype(BF16).reshape(
                WAYS, SIDES, SLOTS, depth, TILE
            )

        go(k, 12, made_rows.at[k, step_of(z + 2), 0], relay_back.at[k, 0], up)
        go(k, 21, made_rows.at[k, step_of(z + 2), 1], relay_back.at[k, 1], down)
        for n, d, device in ((8, 1, up), (10, -1, down)):
            target = step_of(z + d)
            go(k, n, made_rows.at[k, target, 0], landed[k].at[pl.ds(c * 16 + z * SLOTS, SLOTS)], device)
            go(k, n + 1, made_rows.at[k, target, 1], hand_back.at[k, pl.ds(z * SLOTS, SLOTS)], device)
        keep(k, 2, made_rows.at[k, z, 0], landed[k].at[pl.ds(c * 16 + z * SLOTS, SLOTS)])
        keep(k, 3, made_rows.at[k, z, 1], hand_back.at[k, pl.ds(z * SLOTS, SLOTS)])

    def forward_back(k):
        arrived(k, 21)
        origin = step_of(z + 1)
        go(k, 14, relay_back.at[k, 1], hand_back.at[k, pl.ds(origin * SLOTS, SLOTS)], down)
        arrived(k, 12)
        origin = step_of(z - 1)
        go(k, 13, relay_back.at[k, 0], landed[k].at[pl.ds(c * 16 + origin * SLOTS, SLOTS)], up)

    def give(k):
        arrived(k, 9, 11, 14)
        made[k, "keep", 3].wait()
        go(k, 15, hand_back.at[k], landed[k].at[pl.ds(c * 16 + 8, 8)], across)
        arrived(k, 8, 10, 13)
        made[k, "keep", 2].wait()
        there = landed[k].at[pl.ds(c * 16, 8)]
        go(k, 16, there, there, sibling)

    def mirror(k):
        arrived(k, 15)
        there = landed[k].at[pl.ds(c * 16 + 8, 8)]
        go(k, 17, there, there, sibling)

    def build(k):
        arrived(k, 16, 17)

        def one(start, offset):
            def run(b, carry):
                first = start + 2 * b
                total = landed[k][table[16, first]].astype(F32) * weight[0, first]
                total = total + landed[k][table[16, first + 1]].astype(F32) * weight[0, first + 1]
                partial[k, offset + b] = total.astype(BF16)
                return carry

            return run

        row = (x // 2) * 4 * 2 * blocks
        lax.fori_loop(0, blocks, one(row + friend * 2 * blocks, blocks), 0)
        go(k, 18, partial.at[k, pl.ds(blocks, blocks)], final.at[k], mate)
        lax.fori_loop(0, blocks, one(row + me * 2 * blocks, 0), 0)

    def finish(k):
        arrived(k, 18)
        rows = slice(k * depth, (k + 1) * depth)

        def run(b, carry):
            total = base_ref[b, rows, :].astype(F32) + partial[k, b].astype(F32)
            total = total + final[k, b].astype(F32)
            for i in range(2):
                share = jnp.where(table[21, i] == b, weight[2, i], 0.0)
                total = total + hot_out[i, rows, :].astype(F32) * share
            out_ref[b, rows, :] = total.astype(BF16)
            return carry

        lax.fori_loop(0, blocks, run, 0)

    right, left = at(z, x + 1, c), at(z, x - 1, c)
    ring = ((x, right, left), (z, up, down))
    hot_made = {}

    def hot_go(n, src, dst, device):
        copy = remote(src, dst, hot_send.at[n], hot_recv.at[n], device)
        copy.start()
        pending.append(copy)
        hot_made[n] = copy

    short = SLICE // 2

    def hot_rows(order, spot, shift=0, size=SLICE):
        row = order * (HALF // 2) + ((spot + WAYS) % WAYS) * SLICE + shift
        return hotw.at[c, pl.ds(row, size)]

    def hot_begin(order, part):
        spot, plus, minus = ring[order]
        shift = part * short
        piece = slice_ref.at[order, pl.ds(shift, short)]
        there = hot_rows(order, spot, shift, short)
        base = 16 * order + 8 * part
        hot_go(base, piece, there, plus)
        hot_go(base + 1, piece, there, minus)
        hot_go(base + 2, piece, there, sibling)
        copy = pltpu.make_async_copy(piece, there, hot_local.at[2 * order + part])
        copy.start()
        hot_made["keep", order, part] = copy

    def hot_relay(order, part):
        spot, plus, minus = ring[order]
        base = 16 * order + 8 * part
        shift = part * short
        for n, neighbour in ((0, spot - 1), (1, spot + 1)):
            hot_made[base + n].wait_recv()
            there = hot_rows(order, neighbour, shift, short)
            if n == part:
                hot_go(base + 3, there, there, plus if n == 0 else minus)
            hot_go(base + 4 + n, there, there, sibling)

    def hot_last(order, part):
        spot = ring[order][0]
        base = 16 * order + 8 * part
        hot_made[base + 3].wait_recv()
        there = hot_rows(order, spot + 2, part * short, short)
        hot_go(base + 6, there, there, sibling)

    def hot_ready():
        for order in range(2):
            for part in range(2):
                hot_made["keep", order, part].wait()
                for n in (2, 4, 5, 6):
                    hot_made[16 * order + 8 * part + n].wait_recv()

    def hot_first():
        def rise(start):
            rows = jnp.concatenate([f_ref[table[21, 0]], f_ref[table[21, 1]]], axis=0)
            low, high = rows[:, :HALF], rows[:, HALF:]

            def both(cols):
                return jnp.dot(low, hotw[0, :, cols], preferred_element_type=F32) + jnp.dot(
                    high, hotw[1, :, cols], preferred_element_type=F32
                )

            gate = both(pl.ds(start, HEAD_DIM))
            upper = both(pl.ds(pl.multiple_of(start + hidden, HEAD_DIM), HEAD_DIM))
            hot_inner[:, pl.ds(start, HEAD_DIM)] = (jax.nn.silu(gate) * upper).astype(BF16)

        @pl.loop(0, hidden // HEAD_DIM)
        def _(i):
            rise(pl.multiple_of(i * HEAD_DIM, HEAD_DIM))

    def hot_second():
        @pl.loop(0, width // TILE)
        def _(i):
            start = pl.multiple_of(i * TILE, TILE)
            cols = pl.ds(pl.multiple_of(2 * hidden + start, TILE), TILE)
            result = jnp.dot(hot_inner[:, :HALF], hotw[0, :, cols], preferred_element_type=F32)
            result = result + jnp.dot(
                hot_inner[:, HALF:], hotw[1, 2 * HALF - hidden :, cols], preferred_element_type=F32
            )
            hot_out[:, :, pl.ds(start, TILE)] = result.astype(BF16).reshape(2, ROWS, TILE)

    stages = [widen, select, climb, forward, work, forward_back, give, mirror, build]
    begin(0)
    begin(1)
    hot_begin(1, 0)
    hot_begin(1, 1)
    extras = {
        2: ((hot_relay, 1, 0), (hot_begin, 0, 0)),
        3: ((hot_relay, 1, 1),),
        4: ((hot_last, 1, 0), (hot_relay, 0, 0)),
        5: ((hot_last, 1, 1), (hot_begin, 0, 1)),
        7: ((hot_last, 0, 0), (hot_relay, 0, 1)),
        9: ((hot_last, 0, 1),),
        chunks + 3: ((hot_ready,), (hot_first,)),
        chunks + 4: ((hot_second,),),
    }
    lag_of = len(stages)
    done = 0
    for step in range(chunks + lag_of):
        if step + 2 < chunks:
            begin(step + 2)
        for lag in reversed(range(lag_of)):
            if 0 <= step - lag < chunks:
                stages[lag](step - lag)
        for extra in extras.get(step, ()):
            extra[0](*extra[1:])
        if step > chunks + 4:
            while done <= min(step - lag_of, chunks - 1):
                finish(done)
                done += 1
    for copy in pending:
        copy.wait_send()


def moe(table, weight, ffn_in, base, w_gate, w_up, w_down, hot_slices):
    blocks, rows, width = ffn_in.shape
    packed = hot_slices.shape[2]
    chunks = CHUNKS
    depth = rows // chunks
    pair = 2 * CORES * blocks
    whole = pl.BlockSpec(memory_space=pltpu.VMEM)
    return pl.pallas_call(
        functools.partial(moe_kernel, blocks, chunks),
        out_shape=jax.ShapeDtypeStruct(base.shape, BF16),
        in_specs=[pl.BlockSpec(memory_space=pltpu.SMEM)] * 2 + [whole] * 6,
        out_specs=whole,
        scratch_shapes=[pltpu.VMEM((pair, depth, width), BF16)] * chunks
        + [pltpu.VMEM((CORES * 16, depth, width), BF16)] * chunks
        + [
            pltpu.VMEM((chunks, WAYS, SLOTS, depth, width), BF16),
            pltpu.VMEM((chunks, WAYS, SIDES, SLOTS, depth, width), BF16),
            pltpu.VMEM((chunks, SIDES, SLOTS, depth, width), BF16),
            pltpu.VMEM((chunks, WAYS, SIDES, SLOTS, depth, width), BF16),
            pltpu.VMEM((chunks, WAYS, SIDES, SLOTS, depth, width), BF16),
            pltpu.VMEM((chunks, SIDES, SLOTS, depth, width), BF16),
            pltpu.VMEM((chunks, WAYS * SLOTS, depth, width), BF16),
            pltpu.VMEM((chunks, 2 * blocks, depth, width), BF16),
            pltpu.VMEM((chunks, blocks, depth, width), BF16),
            pltpu.SemaphoreType.DMA((chunks, 4)),
            pltpu.SemaphoreType.DMA((chunks, 22)),
            pltpu.SemaphoreType.DMA((chunks, 22)),
            pltpu.VMEM((WAYS * PART * depth, w_gate.shape[1]), BF16),
            pltpu.VMEM((CORES, HALF, packed), BF16),
            pltpu.VMEM((2 * rows, w_gate.shape[1]), BF16),
            pltpu.VMEM((2, rows, width), BF16),
            pltpu.SemaphoreType.DMA((4,)),
            pltpu.SemaphoreType.DMA((32,)),
            pltpu.SemaphoreType.DMA((32,)),
        ],
        compiler_params=pltpu.CompilerParams(
            collective_id=1, has_side_effects=True, vmem_limit_bytes=67043328
        ),
        name="moe",
    )(table, weight, ffn_in, base, w_gate, w_up, w_down, hot_slices)


def tables_kernel(turn, int_ref, real_ref, out_int, out_real):
    out_int[...] = int_ref[...]
    out_real[...] = real_ref[...]
    out_real[2:3, :] = jnp.zeros((1, LANES), F32)
    tables(
        turn[0], int_ref[17:18, :], int_ref[18:19, :], real_ref[1:2, :], int_ref[19:20, :],
        out_int, out_real,
    )


def later_tables(turn, ints, reals):
    return pl.pallas_call(
        tables_kernel,
        out_shape=[
            jax.ShapeDtypeStruct(ints.shape, ints.dtype),
            jax.ShapeDtypeStruct(reals.shape, reals.dtype),
        ],
        in_specs=[pl.BlockSpec(memory_space=pltpu.SMEM)]
        + [pl.BlockSpec(memory_space=pltpu.VMEM)] * 2,
        out_specs=[pl.BlockSpec(memory_space=pltpu.VMEM)] * 2,
        name="later_tables",
    )(turn, ints, reals)


def body(
    hidden_in, attn_gain, w_qkv, head_gain, w_out, ffn_gain, w_gate, w_up, w_down, pair_ids, gate_codes
):
    tokens, width = hidden_in.shape
    blocks = tokens // ROWS
    groups = lax.axis_size("grp")
    weights = (w_gate[0], w_up[0], w_down[0])
    resid, ffn_in, ints, reals, hot_slices = front(
        hidden_in, attn_gain[None], w_qkv, head_gain[None], w_out, ffn_gain[None], *weights, pair_ids.T,
        gate_codes.T, groups,
    )
    resid = resid.reshape(blocks, ROWS, width)
    ffn_in = ffn_in.reshape(blocks, ROWS, width)

    total = moe(ints, reals, ffn_in, resid, *weights, hot_slices)

    def more(total):
        def one(turn, total):
            later_ints, later_reals = later_tables(turn[None], ints, reals)
            return moe(later_ints, later_reals, ffn_in, total, *weights, hot_slices)

        return lax.fori_loop(1, -(-LIMIT // SLOTS), one, total)

    total = lax.cond(ints[22, 0] > SLOTS, more, lambda total: total, total)
    return total.reshape(tokens, width)


def solution(mesh):
    return jax.shard_map(
        body,
        mesh=mesh,
        in_specs=(
            P(("grp", "seq"), None), P(), P(), P(), P(), P(),
            P("seq", None, None), P("seq", None, None), P("seq", None, None),
            P(("grp", "seq"), None), P(("grp", "seq"), None),
        ),
        out_specs=P(("grp", "seq"), None),
        check_vma=False,
    )
```

```python
import functools

import jax
import jax.numpy as jnp
from jax import lax
from jax.experimental import pallas as pl
from jax.experimental.pallas import tpu as pltpu
from jax.sharding import PartitionSpec as P

HEADS = 8
HEAD_DIM = 128
ROWS = 128
EPS = 1e-06
WAYS = 4
CORES = 2
SLOTS = 2
SIDES = 2
PART = SIDES * SLOTS
CHUNKS = 8
STATE = 144
LIMIT = 8
LANES = 128
HALF = 512
TILE = 256
SLICE = 64
PIECE = 16
HOT = 15
MESH = pl.DeviceIdType.MESH
F32 = jnp.float32
BF16 = jnp.bfloat16
LIMIT_BYTES = 60 * 1024 * 1024


def place():
    seq = lax.axis_index("seq")
    return lax.axis_index("grp"), seq // (WAYS * CORES), (seq // CORES) % WAYS, seq % CORES


def remote(src, dst, send, recv, device):
    return pltpu.make_async_remote_copy(
        src_ref=src, dst_ref=dst, send_sem=send, recv_sem=recv, device_id=device, device_id_type=MESH
    )


def greet(devices):
    barrier = pltpu.get_barrier_semaphore()
    for device in devices:
        pl.semaphore_signal(barrier, inc=1, device_id=device, device_id_type=MESH)
    pl.semaphore_wait(barrier, len(devices))


def norm_rows(values, gain):
    return values * lax.rsqrt(jnp.mean(values * values, axis=-1, keepdims=True) + EPS) * gain


def dot_last(a, b):
    return lax.dot_general(a, b, (((1,), (1,)), ((), ())), preferred_element_type=F32)


def dot_first(a, b):
    return lax.dot_general(a, b, (((0,), (0,)), ((), ())), preferred_element_type=F32)


def lifted(values):
    return jnp.where(values > 0.0, values + 1.0, jnp.exp(jnp.minimum(values, 0.0))).astype(BF16)


def tables(turn, ids, rank, shares, hot, out_int, out_real):
    y, z, x, c = place()
    half = x // 2
    other = (x + 2 * (x % 2) - 1 + WAYS) % WAYS
    span = LANES * 7 // 16
    lane = lax.broadcasted_iota(jnp.int32, (1, LANES), 1)
    local = lane - half * span
    near = (local >= 0) & (local < span)
    place_of = rank - turn * SLOTS
    usable = near & (ids >= 0) & (ids != hot) & (place_of >= 0) & (place_of < SLOTS)
    slot = lax.broadcasted_iota(jnp.int32, (16, LANES), 0)
    column = jnp.where(slot >= 8, other, x)
    expert = ((slot & 7) >> 1) * (WAYS * CORES) + column * CORES + c
    key = jnp.where(usable, ids * SLOTS + place_of, -1)
    hit = key == expert * SLOTS + (slot & 1)
    source = jnp.sum(jnp.where(hit, local >> 1, 0).astype(F32), axis=1, keepdims=True)
    out_int[0:16, :] = jnp.broadcast_to(source, (16, LANES)).astype(jnp.int32)
    here = (ids >> 1) & 3
    which = jnp.where(here == other, 1, 0)
    mine = usable & ((here == x) | (here == other))
    index = (ids & 1) * 16 + which * 8 + (ids >> 3) * SLOTS + place_of
    out_int[16:17, :] = jnp.where(mine, index, 0)
    out_real[0:1, :] = jnp.where(mine, shares, 0.0)


def front_kernel(
    groups, blocks, pairs, codes, x_ref, again_ref, wqkv_ref, hgain_ref, wout_ref, fgain_ref,
    wg_ref, wu_ref, wd_ref, resid_ref, ffn_ref, int_ref, real_ref, hot_ref,
    normed, q, k, v, wcols, state, ratio, numer, denom,
    chip, chips, sib, rows, peak, peaks,
    mine, theirs, sums, xs, row_sum, zs, plane_sum, ys, back, heads_in, sib2,
    near, far, slices, halves_in, summed, pieces_in, loads, stay, send, recv,
):
    y, z, x, c = place()
    lane_count = WAYS * CORES
    tokens, width = x_ref.shape
    tiles = tokens // ROWS
    step = 2 * HEAD_DIM
    steps = width // step
    half = tokens // 2

    def at(yy, zz, xx, cc):
        return (yy, zz * lane_count + xx * CORES + cc)

    sibling = at(y, z, x, 1 - c)
    along_x = [at(y, z, (x + d) % WAYS, c) for d in range(1, WAYS)]
    along_z = [at(y, (z + d) % WAYS, x, c) for d in range(1, WAYS)]
    along_y = [at((y + d) % groups, z, x, c) for d in range(1, groups)]
    fetches = []
    for j in range(3 * steps):
        fetch = pltpu.make_async_copy(
            wqkv_ref.at[:, pl.ds(j * step, step)], wcols.at[j], loads.at[j]
        )
        fetch.start()
        fetches.append(fetch)
    greet([sibling] + along_x + along_z + along_y)
    copies = []

    def go(src, dst, device):
        n = len(copies)
        copy = remote(src, dst, send.at[n], recv.at[n], device)
        copy.start()
        copies.append(copy)
        return copy

    def arrive(waits):
        for copy in waits:
            copy.wait_recv()

    hidden = wg_ref.shape[1]
    offset = wd_ref.shape[0] - HALF
    lanes_of = (
        (wg_ref, HALF, pl.ds(0, hidden)),
        (wu_ref, HALF, pl.ds(hidden, hidden)),
        (wd_ref, offset, pl.ds(2 * hidden, width)),
    )
    ring = (
        (x, along_x[0], along_x[2], along_x[1]),
        (z, along_z[0], along_z[2], along_z[1]),
    )
    swapped = []
    for n, (source, jump, span) in enumerate(lanes_of):
        there = source.at[pl.ds(jump * (1 - c), HALF), :]
        swapped.append(go(there, far.at[:, span], sibling))
        local = pltpu.make_async_copy(
            source.at[pl.ds(jump * c, HALF), :], near.at[:, span], stay.at[n]
        )
        local.start()
        fetches.append(local)

    short = SLICE // 2
    held = {}

    def part_of(order, i, shift=0, size=SLICE):
        row = order * (HALF // 2) + ((ring[order][0] + i + WAYS) % WAYS) * SLICE + shift
        return near.at[pl.ds(row, size)]

    def send_near(order):
        _, plus, minus, _ = ring[order]
        held[order, 0] = go(part_of(order, 1), slices.at[order, 0], plus)
        held[order, 1] = go(part_of(order, -1), slices.at[order, 1], minus)

    def send_far(order):
        _, plus, minus, _ = ring[order]
        held[order, 2] = go(part_of(order, 2, 0, short), halves_in.at[order, 0], plus)
        held[order, 3] = go(part_of(order, 2, short, short), halves_in.at[order, 1], minus)

    def relay_far(order):
        _, plus, minus, _ = ring[order]
        arrive([held[order, 2], held[order, 3]])
        first_half, second_half = slices.at[order, 2, pl.ds(0, short)], slices.at[order, 2, pl.ds(short, short)]
        held[order, 4] = go(halves_in.at[order, 0], first_half, plus)
        held[order, 5] = go(halves_in.at[order, 1], second_half, minus)

    def second_reduce(order):
        arrive([held[order, n] for n in (0, 1, 4, 5)])
        top = order * (HALF // 2) + ring[order][0] * SLICE

        @pl.loop(0, SLICE // PIECE)
        def _(i):
            row = pl.multiple_of(i * PIECE, PIECE)
            base_rows = pl.ds(pl.multiple_of(top + row, PIECE), PIECE)
            row = pl.ds(row, PIECE)
            total = near[base_rows, :] + slices[order, 0, row, :]
            summed[order, row, :] = total + (slices[order, 1, row, :] + slices[order, 2, row, :])

        spot, plus, minus, opposite = ring[1 - order]
        held[order, "pieces"] = [
            go(
                summed.at[order, pl.ds(((spot + d) % WAYS) * PIECE, PIECE)],
                pieces_in.at[order, d - 1],
                device,
            )
            for d, device in ((2, opposite), (1, plus), (3, minus))
        ]

    def gather_pieces(order):
        arrive(held[order, "pieces"])
        spot, plus, minus, opposite = ring[1 - order]
        row = pl.ds(pl.multiple_of(spot * PIECE, PIECE), PIECE)
        total = summed[order, row, :] + pieces_in[order, 0]
        hot_ref[order, row, :] = total + (pieces_in[order, 1] + pieces_in[order, 2])
        return [
            go(hot_ref.at[order, row], hot_ref.at[order, row], device)
            for device in (opposite, plus, minus)
        ]

    visits = 2 * blocks
    lane = lax.broadcasted_iota(jnp.int32, (8, LANES), 1)
    sub = lax.broadcasted_iota(jnp.int32, (8, LANES), 0)
    first = (x * CORES + c) * visits
    info = jnp.zeros((8, LANES), jnp.int32)
    for b in range(blocks):
        code = codes[:, b : b + 1]
        pair = pairs[:, b : b + 1] + 1
        both = code[0:1, :] + code[1:2, :]
        for j in range(2):
            here = lane == first + (2 * b + j)
            value = jnp.where(
                sub == 0, pair[j : j + 1, :], jnp.where(sub == 1, code[j : j + 1, :], both)
            )
            info = jnp.where(here & (sub < 3), value, info)
    chip[...] = info
    waits = [go(chip, sib, sibling)]

    @pl.loop(0, tiles)
    def _(i):
        rows_i = pl.ds(pl.multiple_of(i * ROWS, ROWS), ROWS)
        normed[rows_i, :] = norm_rows(x_ref[rows_i, :].astype(F32), again_ref[...]).astype(BF16)

    arrive(waits)
    chips[x] = info + sib[...]
    waits = [go(chips.at[x], chips.at[x], device) for device in along_x]

    def project_query(j):
        fetches[j].wait()
        cols = slice(j * step, (j + 1) * step)

        @pl.loop(0, 2)
        def _(i):
            part = pl.ds(pl.multiple_of(i * half, PIECE), half)
            q[part, cols] = lifted(jnp.dot(normed[part, :], wcols[j], preferred_element_type=F32))

    def project(j):
        for part in range(1, 3):
            fetches[part * steps + j].wait()
        cols = slice(j * step, (j + 1) * step)

        @pl.loop(0, 2)
        def _(i):
            part = pl.ds(pl.multiple_of(i * half, PIECE), half)
            rows_in = normed[part, :]
            k[part, cols] = lifted(jnp.dot(rows_in, wcols[steps + j], preferred_element_type=F32))
            v[part, cols] = jnp.dot(
                rows_in, wcols[2 * steps + j], preferred_element_type=F32
            ).astype(BF16)

        for head in range(2 * j, 2 * j + 2):
            cols = slice(head * HEAD_DIM, (head + 1) * HEAD_DIM)
            keys = k[:, cols]
            total = jnp.sum(keys.astype(F32), axis=0, keepdims=True)
            total = jnp.broadcast_to(total, (STATE - HEAD_DIM, HEAD_DIM))
            outer = dot_first(v[:, cols], keys)
            state[head, :HEAD_DIM, :] = outer
            state[head, HEAD_DIM:, :] = total
            mine[head, :HEAD_DIM, :] = outer.astype(BF16)
            mine[head, HEAD_DIM:, :] = total.astype(BF16)

    project(0)
    arrive(waits)
    info_row = chips[0] + chips[1] + chips[2] + chips[3]
    rows[z] = info_row
    waits = [go(rows.at[z], rows.at[z], device) for device in along_z]
    project(1)
    arrive(waits)
    expert = lax.broadcasted_iota(jnp.int32, (WAYS * lane_count, LANES), 0)
    lanes = lax.broadcasted_iota(jnp.int32, (WAYS * lane_count, LANES), 1)
    counts = jnp.zeros((WAYS * lane_count, 1), F32)
    most = jnp.zeros((WAYS * lane_count, 1), F32)
    for i in range(WAYS):
        there = (rows[i][0:1, :] - 1) == expert
        low = jnp.sum(jnp.where(there & (lanes < 4 * visits), 1.0, 0.0), axis=1, keepdims=True)
        high = jnp.sum(jnp.where(there & (lanes >= 4 * visits), 1.0, 0.0), axis=1, keepdims=True)
        counts = counts + low + high
        most = jnp.maximum(most, jnp.maximum(low, high))
    is_hot = counts > HOT - 0.5
    hot = jnp.sum(jnp.where(is_hot, expert[:, 0:1].astype(F32), 0.0), axis=0, keepdims=True)
    most = jnp.max(jnp.where(is_hot, 0.0, most), axis=0, keepdims=True)
    peak[...] = jnp.broadcast_to(most, (8, LANES))
    peak_waits = [go(peak, peaks.at[y], device) for device in along_y]
    here = (hot == (z * lane_count + x * CORES + c).astype(F32)).astype(BF16)
    beside = (hot == (z * lane_count + x * CORES + 1 - c).astype(F32)).astype(BF16)
    project(2)
    arrive(swapped)
    for fetch in fetches[-3:]:
        fetch.wait()

    @pl.loop(0, HALF // PIECE)
    def _(i):
        row = pl.ds(pl.multiple_of(i * PIECE, PIECE), PIECE)
        near[row, :] = near[row, :] * here + far[row, :] * beside

    send_near(1)
    project(3)
    waits = [go(mine, theirs, sibling)]
    project_query(0)
    project_query(1)
    hot = jnp.broadcast_to(hot, (1, LANES)).astype(jnp.int32)
    ids = info_row[0:1, :] - 1
    wide = jnp.broadcast_to(ids, (LANES, LANES))
    tall = wide.T
    rank_lane = lax.broadcasted_iota(jnp.int32, (LANES, LANES), 1)
    rank_sub = lax.broadcasted_iota(jnp.int32, (LANES, LANES), 0)
    earlier = (wide == tall) & (rank_sub < rank_lane)
    halves = (rank_sub < 4 * visits) == (rank_lane < 4 * visits)
    rank = jnp.sum(jnp.where(earlier & halves, 1.0, 0.0), axis=0, keepdims=True).astype(jnp.int32)
    shares = info_row[1:2, :].astype(F32) / jnp.maximum(info_row[2:3, :], 1).astype(F32)
    int_ref[16:24, :] = jnp.zeros((8, LANES), jnp.int32)
    real_ref[...] = jnp.zeros((8, LANES), F32)
    tables(0, ids, rank, shares, hot, int_ref, real_ref)
    lane = lane[0:1, :]
    own = (lane >= first) & (lane < first + visits) & (ids == hot)
    seen = jnp.sum(jnp.where(own, 1.0, 0.0), axis=1, keepdims=True)
    first_lane = jnp.min(jnp.where(own, lane, 1000).astype(F32), axis=1, keepdims=True)
    last_lane = jnp.max(jnp.where(own, lane, -1).astype(F32), axis=1, keepdims=True)
    int_ref[17:18, :] = ids
    int_ref[18:19, :] = rank
    int_ref[19:20, :] = hot
    first_block = jnp.where(seen > 0.5, (first_lane.astype(jnp.int32) - first) >> 1, 0)
    last_block = (last_lane.astype(jnp.int32) - first) >> 1
    following = jnp.where(first_block + 1 >= blocks, 0, first_block + 1)
    second_block = jnp.where(seen > 1.5, last_block, following)
    int_ref[21:22, :] = jnp.where(lane == 0, first_block, second_block)
    lane_real = lane.astype(F32)
    first_share = jnp.sum(
        jnp.where(own & (lane_real == first_lane), shares, 0.0), axis=1, keepdims=True
    )
    last_share = jnp.sum(
        jnp.where(own & (lane_real == last_lane) & (seen > 1.5), shares, 0.0), axis=1, keepdims=True
    )
    real_ref[1:2, :] = shares
    real_ref[2:3, :] = jnp.where(lane == 0, first_share, last_share)
    arrive(peak_waits)
    peaks[y] = peak[...]
    top = peaks[0]
    for i in range(1, groups):
        top = jnp.maximum(top, peaks[i])
    int_ref[22:23, :] = top[0:1, :].astype(jnp.int32)

    causal = lax.broadcasted_iota(jnp.int32, (ROWS, ROWS), 0) >= lax.broadcasted_iota(
        jnp.int32, (ROWS, ROWS), 1
    )

    def within(start, stop):
        @pl.loop(start, stop)
        def _(head):
            cols = pl.ds(pl.multiple_of(head * HEAD_DIM, HEAD_DIM), HEAD_DIM)
            keys = k[:, cols]
            both = jnp.concatenate([v[:, cols], jnp.ones((tokens, HEAD_DIM), BF16)], axis=1)
            for tile in range(tiles):
                part = slice(tile * ROWS, (tile + 1) * ROWS)
                query = q[part, cols]
                scores = jnp.where(causal, dot_last(query, keys[part, :]), 0.0).astype(BF16)
                total = jnp.dot(scores, both[part, :], preferred_element_type=F32)
                if tile > 0:
                    scores = dot_last(query, keys[: tile * ROWS, :]).astype(BF16)
                    total = total + jnp.dot(
                        scores, both[: tile * ROWS, :], preferred_element_type=F32
                    )
                numer[part, cols] = total[:, :HEAD_DIM]
                denom[part, cols] = total[:, HEAD_DIM:]

    arrive(waits)
    base = c * WAYS
    for i in range(WAYS):
        sums[i] = (state[base + i] + theirs[base + i].astype(F32)).astype(BF16)
    xs[x] = sums[x]
    waits = [go(sums.at[(x + d) % WAYS], xs.at[x], along_x[d - 1]) for d in range(1, WAYS)]
    send_near(0)
    project_query(2)
    project_query(3)
    arrive(waits)
    row_sum[...] = sum(xs[i].astype(F32) for i in range(WAYS)).astype(BF16)
    zs[z] = row_sum[...]
    waits = [go(row_sum, zs.at[z], along_z[d - 1]) for d in range(1, WAYS)]
    send_far(1)
    within(0, 3)
    arrive(waits)
    plane_sum[...] = sum(zs[i].astype(F32) for i in range(WAYS)).astype(BF16)
    waits = [go(plane_sum, ys.at[y], along_y[d - 1]) for d in range(1, groups)]
    total = jnp.zeros(row_sum.shape, F32)
    for i in range(WAYS):
        total = total + zs[i].astype(F32) * jnp.where(i < z, 1.0, 0.0)
    within(3, 6)
    relay_far(1)
    arrive(waits)
    ys[y] = plane_sum[...]
    for i in range(groups):
        total = total + ys[i].astype(F32) * jnp.where(i < y, 1.0, 0.0)
    for i in range(WAYS):
        back[i] = total.astype(BF16)
        total = total + xs[i].astype(F32)
    heads_in[x] = back[x]
    waits = [go(back.at[(x + d) % WAYS], heads_in.at[x], along_x[d - 1]) for d in range(1, WAYS)]
    send_far(0)
    within(6, 8)
    arrive(waits)
    waits = [go(heads_in, sib2, sibling)]
    later = jnp.where(c == 1, 1.0, 0.0)

    def add_prior(first_head, source):
        @pl.loop(0, WAYS)
        def _(i):
            head = first_head + i
            prior = (source[i].astype(F32) + theirs[head].astype(F32) * later).astype(BF16)
            filled = jnp.broadcast_to(prior[HEAD_DIM : HEAD_DIM + 1, :], (HEAD_DIM, HEAD_DIM))
            carried = jnp.concatenate([prior[:HEAD_DIM, :], filled], axis=0)
            cols = pl.ds(pl.multiple_of(head * HEAD_DIM, HEAD_DIM), HEAD_DIM)
            total = dot_last(q[:, cols], carried)
            ratio[:, cols] = (numer[:, cols] + total[:, :HEAD_DIM]) / (
                denom[:, cols] + total[:, HEAD_DIM:]
            )

    second_reduce(1)
    add_prior(base, heads_in)
    relay_far(0)
    arrive(waits)
    add_prior((1 - c) * WAYS, sib2)
    reduce_waits = gather_pieces(1)
    second_reduce(0)

    @pl.loop(0, 2)
    def _(part):
        part_rows = pl.ds(pl.multiple_of(part * half, PIECE), half)
        attended = norm_rows(ratio[part_rows, :], hgain_ref[...]).astype(BF16)
        resid = x_ref[part_rows, :].astype(F32) + jnp.dot(
            attended, wout_ref[...], preferred_element_type=F32
        )
        resid = resid.astype(BF16)
        resid_ref[part_rows, :] = resid
        ffn_ref[part_rows, :] = norm_rows(resid.astype(F32), fgain_ref[...]).astype(BF16)
    arrive(reduce_waits + gather_pieces(0))
    for copy in copies:
        copy.wait_send()


def front(
    x, attn_gain, w_qkv, head_gain, w_out, ffn_gain, w_gate, w_up, w_down, pair_ids, gate_codes, groups
):
    tokens, width = x.shape
    packed = 2 * w_gate.shape[1] + width
    blocks = pair_ids.shape[1]
    tile = (8, LANES)
    one = (STATE, HEAD_DIM)
    some = (WAYS,) + one
    every = (HEADS,) + one
    step = 2 * HEAD_DIM
    pieces = 3 * width // step
    count = 1 + 2 * (WAYS - 1) + groups - 1 + 2 + 3 * (WAYS - 1) + groups - 1
    count += 3 + 12 + 4 * (WAYS - 1)

    def wide(*shape):
        return pltpu.VMEM(shape + (packed,), BF16)

    vmem = pl.BlockSpec(memory_space=pltpu.VMEM)
    hbm = pl.BlockSpec(memory_space=pl.ANY)
    return pl.pallas_call(
        functools.partial(front_kernel, groups, blocks),
        out_shape=[jax.ShapeDtypeStruct((tokens, width), BF16)] * 2
        + [jax.ShapeDtypeStruct((24, LANES), jnp.int32), jax.ShapeDtypeStruct(tile, F32)]
        + [jax.ShapeDtypeStruct((2, SLICE, packed), BF16)],
        in_specs=[vmem] * 4 + [hbm] + [vmem] * 3 + [hbm] * 3,
        out_specs=[vmem] * 5,
        scratch_shapes=[pltpu.VMEM((tokens, width), BF16)] * 4
        + [pltpu.VMEM((pieces, width, step), BF16), pltpu.VMEM(every, F32)]
        + [pltpu.VMEM((tokens, width), F32)] * 3
        + [
            pltpu.VMEM(tile, jnp.int32),
            pltpu.VMEM((WAYS,) + tile, jnp.int32),
            pltpu.VMEM(tile, jnp.int32),
            pltpu.VMEM((WAYS,) + tile, jnp.int32),
            pltpu.VMEM(tile, F32),
            pltpu.VMEM((groups,) + tile, F32),
            pltpu.VMEM(every, BF16),
            pltpu.VMEM(every, BF16),
            pltpu.VMEM(some, BF16),
            pltpu.VMEM(some, BF16),
            pltpu.VMEM(one, BF16),
            pltpu.VMEM(some, BF16),
            pltpu.VMEM(one, BF16),
            pltpu.VMEM((groups,) + one, BF16),
            pltpu.VMEM(some, BF16),
            pltpu.VMEM(some, BF16),
            pltpu.VMEM(some, BF16),
            wide(HALF),
            wide(HALF),
            wide(2, WAYS - 1, SLICE),
            wide(2, 2, SLICE // 2),
            wide(2, SLICE),
            wide(2, WAYS - 1, PIECE),
            pltpu.SemaphoreType.DMA((pieces,)),
            pltpu.SemaphoreType.DMA((3,)),
            pltpu.SemaphoreType.DMA((count,)),
            pltpu.SemaphoreType.DMA((count,)),
        ],
        compiler_params=pltpu.CompilerParams(
            collective_id=0, has_side_effects=True, vmem_limit_bytes=LIMIT_BYTES
        ),
        name="front",
    )(
        pair_ids, gate_codes, x, attn_gain, w_qkv, head_gain, w_out, ffn_gain, w_gate, w_up, w_down
    )


def moe_kernel(
    blocks, chunks, table, weight, f_ref, base_hbm, wg_hbm, wu_hbm, wd_hbm, slice_ref, out_ref,
    *rest
):
    gather, landed = rest[:chunks], rest[chunks : 2 * chunks]
    (
        hand, zs, relay, taken, made_rows, relay_back, hand_back, partial, final, local, send, recv,
        base_ref, wg_ref, wu_ref, wd_ref, fetch_sem, inside, hotw, hot_inner, hot_out, hot_local, hot_send, hot_recv,
    ) = rest[2 * chunks :]
    depth = ROWS // chunks
    width = f_ref.shape[2]
    hidden = wg_ref.shape[1]
    y, z, x, c = place()
    lane = WAYS * CORES
    parity = x % 2

    def at(zz, xx, cc):
        return (y, ((zz + WAYS) % WAYS) * lane + ((xx + WAYS) % WAYS) * CORES + cc)

    sibling = at(z, x, 1 - c)
    mate = at(z, x + 1 - 2 * parity, c)
    across = at(z, x + 2 * parity - 1, c)
    up, down = at(z + 1, x, c), at(z - 1, x, c)
    fetched = []
    for n, (source, place_in) in enumerate(
        ((wg_hbm, wg_ref), (wu_hbm, wu_ref), (wd_hbm, wd_ref), (base_hbm, base_ref))
    ):
        fetch = pltpu.make_async_copy(source, place_in, fetch_sem.at[n])
        fetch.start()
        fetched.append(fetch)
    greet([sibling, mate, across, up, down])
    me = parity * CORES + c
    friend = (1 - parity) * CORES + c
    pending = []
    made = {}

    def go(k, n, src, dst, device):
        copy = remote(src, dst, send.at[k, n], recv.at[k, n], device)
        copy.start()
        pending.append(copy)
        made[k, n] = copy

    def keep(k, n, src, dst):
        copy = pltpu.make_async_copy(src, dst, local.at[k, n])
        copy.start()
        made[k, "keep", n] = copy

    def arrived(k, *numbers):
        for n in numbers:
            made[k, n].wait_recv()

    def step_of(row):
        return (row + WAYS) % WAYS

    def begin(k):
        own = f_ref.at[:, pl.ds(k * depth, depth), :]
        here = gather[k].at[pl.ds(me * blocks, blocks)]
        go(k, 0, own, here, mate)
        go(k, 1, own, here, sibling)
        keep(k, 0, own, here)

    def widen(k):
        arrived(k, 0)
        there = gather[k].at[pl.ds(friend * blocks, blocks)]
        go(k, 2, there, there, sibling)

    def select(k):
        made[k, "keep", 0].wait()
        arrived(k, 1, 2)
        for row in range(WAYS):
            for j in range(SLOTS):
                hand[k, row, j] = gather[k][table[8 + row * SLOTS + j, 0]]
        go(k, 3, hand.at[k], zs.at[k, :, 1], across)
        for row in range(WAYS):
            for j in range(SLOTS):
                zs[k, row, 0, j] = gather[k][table[row * SLOTS + j, 0]]

    def climb(k):
        arrived(k, 3)
        go(k, 6, zs.at[k, step_of(z + 2), 0], relay.at[k, 0], up)
        go(k, 19, zs.at[k, step_of(z + 2), 1], relay.at[k, 1], down)
        go(k, 4, zs.at[k, step_of(z + 1)], taken.at[k, z], up)
        go(k, 5, zs.at[k, step_of(z - 1)], taken.at[k, z], down)
        keep(k, 1, zs.at[k, z], taken.at[k, z])

    def forward(k):
        arrived(k, 6)
        go(k, 7, relay.at[k, 0], taken.at[k, step_of(z - 1), 0], up)
        arrived(k, 19)
        go(k, 20, relay.at[k, 1], taken.at[k, step_of(z + 1), 1], down)

    def work(k):
        if k == 0:
            for fetch in fetched:
                fetch.wait()
        arrived(k, 4, 5, 7, 20)
        made[k, "keep", 1].wait()
        def rise(cols):
            rows = taken[k].reshape(WAYS * PART * depth, width)
            gate = jnp.dot(rows, wg_ref[:, cols], preferred_element_type=F32)
            upper = jnp.dot(rows, wu_ref[:, cols], preferred_element_type=F32)
            inside[:, cols] = (jax.nn.silu(gate) * upper).astype(BF16)

        @pl.loop(0, hidden // TILE)
        def _(i):
            rise(pl.ds(pl.multiple_of(i * TILE, TILE), TILE))

        if hidden % TILE:
            rise(slice(hidden - hidden % TILE, hidden))

        @pl.loop(0, width // TILE)
        def _(i):
            cols = pl.ds(pl.multiple_of(i * TILE, TILE), TILE)
            result = jnp.dot(inside[...], wd_ref[:, cols], preferred_element_type=F32)
            made_rows[k, :, :, :, :, cols] = result.astype(BF16).reshape(
                WAYS, SIDES, SLOTS, depth, TILE
            )

        go(k, 12, made_rows.at[k, step_of(z + 2), 0], relay_back.at[k, 0], up)
        go(k, 21, made_rows.at[k, step_of(z + 2), 1], relay_back.at[k, 1], down)
        for n, d, device in ((8, 1, up), (10, -1, down)):
            target = step_of(z + d)
            go(k, n, made_rows.at[k, target, 0], landed[k].at[pl.ds(c * 16 + z * SLOTS, SLOTS)], device)
            go(k, n + 1, made_rows.at[k, target, 1], hand_back.at[k, pl.ds(z * SLOTS, SLOTS)], device)
        keep(k, 2, made_rows.at[k, z, 0], landed[k].at[pl.ds(c * 16 + z * SLOTS, SLOTS)])
        keep(k, 3, made_rows.at[k, z, 1], hand_back.at[k, pl.ds(z * SLOTS, SLOTS)])

    def forward_back(k):
        arrived(k, 21)
        origin = step_of(z + 1)
        go(k, 14, relay_back.at[k, 1], hand_back.at[k, pl.ds(origin * SLOTS, SLOTS)], down)
        arrived(k, 12)
        origin = step_of(z - 1)
        go(k, 13, relay_back.at[k, 0], landed[k].at[pl.ds(c * 16 + origin * SLOTS, SLOTS)], up)

    def give(k):
        arrived(k, 9, 11, 14)
        made[k, "keep", 3].wait()
        go(k, 15, hand_back.at[k], landed[k].at[pl.ds(c * 16 + 8, 8)], across)
        arrived(k, 8, 10, 13)
        made[k, "keep", 2].wait()
        there = landed[k].at[pl.ds(c * 16, 8)]
        go(k, 16, there, there, sibling)

    def mirror(k):
        arrived(k, 15)
        there = landed[k].at[pl.ds(c * 16 + 8, 8)]
        go(k, 17, there, there, sibling)

    def build(k):
        arrived(k, 16, 17)

        def one(start, offset):
            def run(b, carry):
                first = start + 2 * b
                total = landed[k][table[16, first]].astype(F32) * weight[0, first]
                total = total + landed[k][table[16, first + 1]].astype(F32) * weight[0, first + 1]
                partial[k, offset + b] = total.astype(BF16)
                return carry

            return run

        row = (x // 2) * 4 * 2 * blocks
        lax.fori_loop(0, blocks, one(row + friend * 2 * blocks, blocks), 0)
        go(k, 18, partial.at[k, pl.ds(blocks, blocks)], final.at[k], mate)
        lax.fori_loop(0, blocks, one(row + me * 2 * blocks, 0), 0)

    def finish(k):
        arrived(k, 18)
        rows = slice(k * depth, (k + 1) * depth)

        def run(b, carry):
            total = base_ref[b, rows, :].astype(F32) + partial[k, b].astype(F32)
            total = total + final[k, b].astype(F32)
            for i in range(2):
                share = jnp.where(table[21, i] == b, weight[2, i], 0.0)
                total = total + hot_out[i, rows, :].astype(F32) * share
            out_ref[b, rows, :] = total.astype(BF16)
            return carry

        lax.fori_loop(0, blocks, run, 0)

    right, left = at(z, x + 1, c), at(z, x - 1, c)
    ring = ((x, right, left), (z, up, down))
    hot_made = {}

    def hot_go(n, src, dst, device):
        copy = remote(src, dst, hot_send.at[n], hot_recv.at[n], device)
        copy.start()
        pending.append(copy)
        hot_made[n] = copy

    short = SLICE // 2

    def hot_rows(order, spot, shift=0, size=SLICE):
        row = order * (HALF // 2) + ((spot + WAYS) % WAYS) * SLICE + shift
        return hotw.at[c, pl.ds(row, size)]

    def hot_begin(order, part):
        spot, plus, minus = ring[order]
        shift = part * short
        piece = slice_ref.at[order, pl.ds(shift, short)]
        there = hot_rows(order, spot, shift, short)
        base = 16 * order + 8 * part
        hot_go(base, piece, there, plus)
        hot_go(base + 1, piece, there, minus)
        hot_go(base + 2, piece, there, sibling)
        copy = pltpu.make_async_copy(piece, there, hot_local.at[2 * order + part])
        copy.start()
        hot_made["keep", order, part] = copy

    def hot_relay(order, part):
        spot, plus, minus = ring[order]
        base = 16 * order + 8 * part
        shift = part * short
        for n, neighbour in ((0, spot - 1), (1, spot + 1)):
            hot_made[base + n].wait_recv()
            there = hot_rows(order, neighbour, shift, short)
            if n == part:
                hot_go(base + 3, there, there, plus if n == 0 else minus)
            hot_go(base + 4 + n, there, there, sibling)

    def hot_last(order, part):
        spot = ring[order][0]
        base = 16 * order + 8 * part
        hot_made[base + 3].wait_recv()
        there = hot_rows(order, spot + 2, part * short, short)
        hot_go(base + 6, there, there, sibling)

    def hot_ready():
        for order in range(2):
            for part in range(2):
                hot_made["keep", order, part].wait()
                for n in (2, 4, 5, 6):
                    hot_made[16 * order + 8 * part + n].wait_recv()

    def hot_first():
        def rise(start):
            rows = jnp.concatenate([f_ref[table[21, 0]], f_ref[table[21, 1]]], axis=0)
            low, high = rows[:, :HALF], rows[:, HALF:]

            def both(cols):
                return jnp.dot(low, hotw[0, :, cols], preferred_element_type=F32) + jnp.dot(
                    high, hotw[1, :, cols], preferred_element_type=F32
                )

            gate = both(pl.ds(start, HEAD_DIM))
            upper = both(pl.ds(pl.multiple_of(start + hidden, HEAD_DIM), HEAD_DIM))
            hot_inner[:, pl.ds(start, HEAD_DIM)] = (jax.nn.silu(gate) * upper).astype(BF16)

        @pl.loop(0, hidden // HEAD_DIM)
        def _(i):
            rise(pl.multiple_of(i * HEAD_DIM, HEAD_DIM))

    def hot_second():
        @pl.loop(0, width // TILE)
        def _(i):
            start = pl.multiple_of(i * TILE, TILE)
            cols = pl.ds(pl.multiple_of(2 * hidden + start, TILE), TILE)
            result = jnp.dot(hot_inner[:, :HALF], hotw[0, :, cols], preferred_element_type=F32)
            result = result + jnp.dot(
                hot_inner[:, HALF:], hotw[1, 2 * HALF - hidden :, cols], preferred_element_type=F32
            )
            hot_out[:, :, pl.ds(start, TILE)] = result.astype(BF16).reshape(2, ROWS, TILE)

    stages = [widen, select, climb, forward, work, forward_back, give, mirror, build]
    begin(0)
    begin(1)
    hot_begin(1, 0)
    hot_begin(1, 1)
    extras = {
        2: ((hot_relay, 1, 0), (hot_begin, 0, 0)),
        3: ((hot_relay, 1, 1),),
        4: ((hot_last, 1, 0), (hot_relay, 0, 0)),
        5: ((hot_last, 1, 1), (hot_begin, 0, 1)),
        7: ((hot_last, 0, 0), (hot_relay, 0, 1)),
        9: ((hot_last, 0, 1),),
        chunks + 3: ((hot_ready,), (hot_first,)),
        chunks + 4: ((hot_second,),),
    }
    lag_of = len(stages)
    done = 0
    for step in range(chunks + lag_of):
        if step + 2 < chunks:
            begin(step + 2)
        for lag in reversed(range(lag_of)):
            if 0 <= step - lag < chunks:
                stages[lag](step - lag)
        for extra in extras.get(step, ()):
            extra[0](*extra[1:])
        if step > chunks + 4:
            while done <= min(step - lag_of, chunks - 1):
                finish(done)
                done += 1
    for copy in pending:
        copy.wait_send()


def moe(table, weight, ffn_in, base, w_gate, w_up, w_down, hot_slices):
    blocks, rows, width = ffn_in.shape
    packed = hot_slices.shape[2]
    chunks = CHUNKS
    depth = rows // chunks
    pair = 2 * CORES * blocks
    whole = pl.BlockSpec(memory_space=pltpu.VMEM)
    hbm = pl.BlockSpec(memory_space=pl.ANY)
    return pl.pallas_call(
        functools.partial(moe_kernel, blocks, chunks),
        out_shape=jax.ShapeDtypeStruct(base.shape, BF16),
        in_specs=[pl.BlockSpec(memory_space=pltpu.SMEM)] * 2 + [whole] + [hbm] * 4 + [whole],
        out_specs=whole,
        scratch_shapes=[pltpu.VMEM((pair, depth, width), BF16)] * chunks
        + [pltpu.VMEM((CORES * 16, depth, width), BF16)] * chunks
        + [
            pltpu.VMEM((chunks, WAYS, SLOTS, depth, width), BF16),
            pltpu.VMEM((chunks, WAYS, SIDES, SLOTS, depth, width), BF16),
            pltpu.VMEM((chunks, SIDES, SLOTS, depth, width), BF16),
            pltpu.VMEM((chunks, WAYS, SIDES, SLOTS, depth, width), BF16),
            pltpu.VMEM((chunks, WAYS, SIDES, SLOTS, depth, width), BF16),
            pltpu.VMEM((chunks, SIDES, SLOTS, depth, width), BF16),
            pltpu.VMEM((chunks, WAYS * SLOTS, depth, width), BF16),
            pltpu.VMEM((chunks, 2 * blocks, depth, width), BF16),
            pltpu.VMEM((chunks, blocks, depth, width), BF16),
            pltpu.SemaphoreType.DMA((chunks, 4)),
            pltpu.SemaphoreType.DMA((chunks, 22)),
            pltpu.SemaphoreType.DMA((chunks, 22)),
            pltpu.VMEM(base.shape, BF16),
            pltpu.VMEM(w_gate.shape, BF16),
            pltpu.VMEM(w_up.shape, BF16),
            pltpu.VMEM(w_down.shape, BF16),
            pltpu.SemaphoreType.DMA((4,)),
            pltpu.VMEM((WAYS * PART * depth, w_gate.shape[1]), BF16),
            pltpu.VMEM((CORES, HALF, packed), BF16),
            pltpu.VMEM((2 * rows, w_gate.shape[1]), BF16),
            pltpu.VMEM((2, rows, width), BF16),
            pltpu.SemaphoreType.DMA((4,)),
            pltpu.SemaphoreType.DMA((32,)),
            pltpu.SemaphoreType.DMA((32,)),
        ],
        compiler_params=pltpu.CompilerParams(
            collective_id=1, has_side_effects=True, vmem_limit_bytes=67043328
        ),
        name="moe",
    )(table, weight, ffn_in, base, w_gate, w_up, w_down, hot_slices)


def tables_kernel(turn, int_ref, real_ref, out_int, out_real):
    out_int[...] = int_ref[...]
    out_real[...] = real_ref[...]
    out_real[2:3, :] = jnp.zeros((1, LANES), F32)
    tables(
        turn[0], int_ref[17:18, :], int_ref[18:19, :], real_ref[1:2, :], int_ref[19:20, :],
        out_int, out_real,
    )


def later_tables(turn, ints, reals):
    return pl.pallas_call(
        tables_kernel,
        out_shape=[
            jax.ShapeDtypeStruct(ints.shape, ints.dtype),
            jax.ShapeDtypeStruct(reals.shape, reals.dtype),
        ],
        in_specs=[pl.BlockSpec(memory_space=pltpu.SMEM)]
        + [pl.BlockSpec(memory_space=pltpu.VMEM)] * 2,
        out_specs=[pl.BlockSpec(memory_space=pltpu.VMEM)] * 2,
        name="later_tables",
    )(turn, ints, reals)


def body(
    hidden_in, attn_gain, w_qkv, head_gain, w_out, ffn_gain, w_gate, w_up, w_down, pair_ids, gate_codes
):
    tokens, width = hidden_in.shape
    blocks = tokens // ROWS
    groups = lax.axis_size("grp")
    weights = (w_gate[0], w_up[0], w_down[0])
    resid, ffn_in, ints, reals, hot_slices = front(
        hidden_in, attn_gain[None], w_qkv, head_gain[None], w_out, ffn_gain[None], *weights, pair_ids.T,
        gate_codes.T, groups,
    )
    resid = resid.reshape(blocks, ROWS, width)
    ffn_in = ffn_in.reshape(blocks, ROWS, width)

    total = moe(ints, reals, ffn_in, resid, *weights, hot_slices)

    def more(total):
        def one(turn, total):
            later_ints, later_reals = later_tables(turn[None], ints, reals)
            return moe(later_ints, later_reals, ffn_in, total, *weights, hot_slices)

        return lax.fori_loop(1, -(-LIMIT // SLOTS), one, total)

    total = lax.cond(ints[22, 0] > SLOTS, more, lambda total: total, total)
    return total.reshape(tokens, width)


def solution(mesh):
    return jax.shard_map(
        body,
        mesh=mesh,
        in_specs=(
            P(("grp", "seq"), None), P(), P(), P(), P(), P(),
            P("seq", None, None), P("seq", None, None), P("seq", None, None),
            P(("grp", "seq"), None), P(("grp", "seq"), None),
        ),
        out_specs=P(("grp", "seq"), None),
        check_vma=False,
    )
```

```python
import functools

import jax
import jax.numpy as jnp
from jax import lax
from jax.experimental import pallas as pl
from jax.experimental.pallas import tpu as pltpu
from jax.sharding import PartitionSpec as P

HEADS = 8
HEAD_DIM = 128
ROWS = 128
EPS = 1e-06
WAYS = 4
CORES = 2
SLOTS = 2
SIDES = 2
PART = SIDES * SLOTS
CHUNKS = 8
STATE = 144
LIMIT = 8
LANES = 128
HALF = 512
TILE = 256
SLICE = 64
PIECE = 16
HOT = 15
MESH = pl.DeviceIdType.MESH
F32 = jnp.float32
BF16 = jnp.bfloat16
LIMIT_BYTES = 60 * 1024 * 1024


def place():
    seq = lax.axis_index("seq")
    return lax.axis_index("grp"), seq // (WAYS * CORES), (seq // CORES) % WAYS, seq % CORES


def remote(src, dst, send, recv, device):
    return pltpu.make_async_remote_copy(
        src_ref=src, dst_ref=dst, send_sem=send, recv_sem=recv, device_id=device, device_id_type=MESH
    )


def greet(devices):
    barrier = pltpu.get_barrier_semaphore()
    for device in devices:
        pl.semaphore_signal(barrier, inc=1, device_id=device, device_id_type=MESH)
    pl.semaphore_wait(barrier, len(devices))


def norm_rows(values, gain):
    return values * lax.rsqrt(jnp.mean(values * values, axis=-1, keepdims=True) + EPS) * gain


def dot_last(a, b):
    return lax.dot_general(a, b, (((1,), (1,)), ((), ())), preferred_element_type=F32)


def dot_first(a, b):
    return lax.dot_general(a, b, (((0,), (0,)), ((), ())), preferred_element_type=F32)


def lifted(values):
    return jnp.where(values > 0.0, values + 1.0, jnp.exp(jnp.minimum(values, 0.0))).astype(BF16)


def tables(turn, ids, rank, shares, hot, out_int, out_real):
    y, z, x, c = place()
    half = x // 2
    other = (x + 2 * (x % 2) - 1 + WAYS) % WAYS
    span = LANES * 7 // 16
    lane = lax.broadcasted_iota(jnp.int32, (1, LANES), 1)
    local = lane - half * span
    near = (local >= 0) & (local < span)
    place_of = rank - turn * SLOTS
    usable = near & (ids >= 0) & (ids != hot) & (place_of >= 0) & (place_of < SLOTS)
    slot = lax.broadcasted_iota(jnp.int32, (16, LANES), 0)
    column = jnp.where(slot >= 8, other, x)
    expert = ((slot & 7) >> 1) * (WAYS * CORES) + column * CORES + c
    key = jnp.where(usable, ids * SLOTS + place_of, -1)
    hit = key == expert * SLOTS + (slot & 1)
    source = jnp.sum(jnp.where(hit, local >> 1, 0).astype(F32), axis=1, keepdims=True)
    out_int[0:16, :] = jnp.broadcast_to(source, (16, LANES)).astype(jnp.int32)
    here = (ids >> 1) & 3
    which = jnp.where(here == other, 1, 0)
    mine = usable & ((here == x) | (here == other))
    index = (ids & 1) * 16 + which * 8 + (ids >> 3) * SLOTS + place_of
    out_int[16:17, :] = jnp.where(mine, index, 0)
    out_real[0:1, :] = jnp.where(mine, shares, 0.0)


def front_kernel(
    groups, blocks, pairs, codes, x_ref, again_ref, wqkv_ref, hgain_ref, wout_ref, fgain_ref,
    wg_ref, wu_ref, wd_ref, resid_ref, ffn_ref, int_ref, real_ref, hot_ref,
    normed, q, k, v, wcols, state, ratio, numer, denom,
    chip, chips, sib, rows, peak, peaks,
    mine, theirs, sums, xs, row_sum, zs, plane_sum, ys, back, heads_in, sib2,
    near, far, slices, halves_in, loads, stay, send, recv,
):
    y, z, x, c = place()
    lane_count = WAYS * CORES
    tokens, width = x_ref.shape
    tiles = tokens // ROWS
    step = 2 * HEAD_DIM
    steps = width // step
    half = tokens // 2

    def at(yy, zz, xx, cc):
        return (yy, zz * lane_count + xx * CORES + cc)

    sibling = at(y, z, x, 1 - c)
    along_x = [at(y, z, (x + d) % WAYS, c) for d in range(1, WAYS)]
    along_z = [at(y, (z + d) % WAYS, x, c) for d in range(1, WAYS)]
    along_y = [at((y + d) % groups, z, x, c) for d in range(1, groups)]
    fetches = []
    for j in range(3 * steps):
        fetch = pltpu.make_async_copy(
            wqkv_ref.at[:, pl.ds(j * step, step)], wcols.at[j], loads.at[j]
        )
        fetch.start()
        fetches.append(fetch)
    greet([sibling] + along_x + along_z + along_y)
    copies = []

    def go(src, dst, device):
        n = len(copies)
        copy = remote(src, dst, send.at[n], recv.at[n], device)
        copy.start()
        copies.append(copy)
        return copy

    def arrive(waits):
        for copy in waits:
            copy.wait_recv()

    hidden = wg_ref.shape[1]
    offset = wd_ref.shape[0] - HALF
    lanes_of = (
        (wg_ref, HALF, pl.ds(0, hidden)),
        (wu_ref, HALF, pl.ds(hidden, hidden)),
        (wd_ref, offset, pl.ds(2 * hidden, width)),
    )
    ring = (
        (x, along_x[0], along_x[2], along_x[1]),
        (z, along_z[0], along_z[2], along_z[1]),
    )
    swapped = []
    for n, (source, jump, span) in enumerate(lanes_of):
        there = source.at[pl.ds(jump * (1 - c), HALF), :]
        swapped.append(go(there, far.at[:, span], sibling))
        local = pltpu.make_async_copy(
            source.at[pl.ds(jump * c, HALF), :], near.at[:, span], stay.at[n]
        )
        local.start()
        fetches.append(local)

    short = SLICE // 2
    held = {}

    def part_of(order, i, shift=0, size=SLICE):
        row = order * (HALF // 2) + ((ring[order][0] + i + WAYS) % WAYS) * SLICE + shift
        return near.at[pl.ds(row, size)]

    def send_near(order):
        _, plus, minus, _ = ring[order]
        held[order, 0] = go(part_of(order, 1), slices.at[order, 0], plus)
        held[order, 1] = go(part_of(order, -1), slices.at[order, 1], minus)

    def send_far(order):
        _, plus, minus, _ = ring[order]
        held[order, 2] = go(part_of(order, 2, 0, short), halves_in.at[order, 0], plus)
        held[order, 3] = go(part_of(order, 2, short, short), halves_in.at[order, 1], minus)

    def relay_far(order):
        _, plus, minus, _ = ring[order]
        arrive([held[order, 2], held[order, 3]])
        first_half, second_half = slices.at[order, 2, pl.ds(0, short)], slices.at[order, 2, pl.ds(short, short)]
        held[order, 4] = go(halves_in.at[order, 0], first_half, plus)
        held[order, 5] = go(halves_in.at[order, 1], second_half, minus)

    def second_reduce(order):
        arrive([held[order, n] for n in (0, 1, 4, 5)])
        top = order * (HALF // 2) + ring[order][0] * SLICE

        @pl.loop(0, SLICE // PIECE)
        def _(i):
            row = pl.multiple_of(i * PIECE, PIECE)
            base_rows = pl.ds(pl.multiple_of(top + row, PIECE), PIECE)
            row = pl.ds(row, PIECE)
            total = near[base_rows, :] + slices[order, 0, row, :]
            hot_ref[order, row, :] = total + (slices[order, 1, row, :] + slices[order, 2, row, :])

    visits = 2 * blocks
    lane = lax.broadcasted_iota(jnp.int32, (8, LANES), 1)
    sub = lax.broadcasted_iota(jnp.int32, (8, LANES), 0)
    first = (x * CORES + c) * visits
    info = jnp.zeros((8, LANES), jnp.int32)
    for b in range(blocks):
        code = codes[:, b : b + 1]
        pair = pairs[:, b : b + 1] + 1
        both = code[0:1, :] + code[1:2, :]
        for j in range(2):
            here = lane == first + (2 * b + j)
            value = jnp.where(
                sub == 0, pair[j : j + 1, :], jnp.where(sub == 1, code[j : j + 1, :], both)
            )
            info = jnp.where(here & (sub < 3), value, info)
    chip[...] = info
    waits = [go(chip, sib, sibling)]

    @pl.loop(0, tiles)
    def _(i):
        rows_i = pl.ds(pl.multiple_of(i * ROWS, ROWS), ROWS)
        normed[rows_i, :] = norm_rows(x_ref[rows_i, :].astype(F32), again_ref[...]).astype(BF16)

    arrive(waits)
    chips[x] = info + sib[...]
    waits = [go(chips.at[x], chips.at[x], device) for device in along_x]

    def project_query(j):
        fetches[j].wait()
        cols = slice(j * step, (j + 1) * step)

        @pl.loop(0, 2)
        def _(i):
            part = pl.ds(pl.multiple_of(i * half, PIECE), half)
            q[part, cols] = lifted(jnp.dot(normed[part, :], wcols[j], preferred_element_type=F32))

    def project(j):
        for part in range(1, 3):
            fetches[part * steps + j].wait()
        cols = slice(j * step, (j + 1) * step)

        @pl.loop(0, 2)
        def _(i):
            part = pl.ds(pl.multiple_of(i * half, PIECE), half)
            rows_in = normed[part, :]
            k[part, cols] = lifted(jnp.dot(rows_in, wcols[steps + j], preferred_element_type=F32))
            v[part, cols] = jnp.dot(
                rows_in, wcols[2 * steps + j], preferred_element_type=F32
            ).astype(BF16)

        for head in range(2 * j, 2 * j + 2):
            cols = slice(head * HEAD_DIM, (head + 1) * HEAD_DIM)
            keys = k[:, cols]
            total = jnp.sum(keys.astype(F32), axis=0, keepdims=True)
            total = jnp.broadcast_to(total, (STATE - HEAD_DIM, HEAD_DIM))
            outer = dot_first(v[:, cols], keys)
            state[head, :HEAD_DIM, :] = outer
            state[head, HEAD_DIM:, :] = total
            mine[head, :HEAD_DIM, :] = outer.astype(BF16)
            mine[head, HEAD_DIM:, :] = total.astype(BF16)

    project(0)
    arrive(waits)
    info_row = chips[0] + chips[1] + chips[2] + chips[3]
    rows[z] = info_row
    waits = [go(rows.at[z], rows.at[z], device) for device in along_z]
    project(1)
    arrive(waits)
    expert = lax.broadcasted_iota(jnp.int32, (WAYS * lane_count, LANES), 0)
    lanes = lax.broadcasted_iota(jnp.int32, (WAYS * lane_count, LANES), 1)
    counts = jnp.zeros((WAYS * lane_count, 1), F32)
    most = jnp.zeros((WAYS * lane_count, 1), F32)
    for i in range(WAYS):
        there = (rows[i][0:1, :] - 1) == expert
        low = jnp.sum(jnp.where(there & (lanes < 4 * visits), 1.0, 0.0), axis=1, keepdims=True)
        high = jnp.sum(jnp.where(there & (lanes >= 4 * visits), 1.0, 0.0), axis=1, keepdims=True)
        counts = counts + low + high
        most = jnp.maximum(most, jnp.maximum(low, high))
    is_hot = counts > HOT - 0.5
    hot = jnp.sum(jnp.where(is_hot, expert[:, 0:1].astype(F32), 0.0), axis=0, keepdims=True)
    most = jnp.max(jnp.where(is_hot, 0.0, most), axis=0, keepdims=True)
    peak[...] = jnp.broadcast_to(most, (8, LANES))
    peak_waits = [go(peak, peaks.at[y], device) for device in along_y]
    here = (hot == (z * lane_count + x * CORES + c).astype(F32)).astype(BF16)
    beside = (hot == (z * lane_count + x * CORES + 1 - c).astype(F32)).astype(BF16)
    project(2)
    arrive(swapped)
    for fetch in fetches[-3:]:
        fetch.wait()

    @pl.loop(0, HALF // PIECE)
    def _(i):
        row = pl.ds(pl.multiple_of(i * PIECE, PIECE), PIECE)
        near[row, :] = near[row, :] * here + far[row, :] * beside

    send_near(0)
    send_near(1)
    project(3)
    waits = [go(mine, theirs, sibling)]
    project_query(0)
    project_query(1)
    hot = jnp.broadcast_to(hot, (1, LANES)).astype(jnp.int32)
    ids = info_row[0:1, :] - 1
    wide = jnp.broadcast_to(ids, (LANES, LANES))
    tall = wide.T
    rank_lane = lax.broadcasted_iota(jnp.int32, (LANES, LANES), 1)
    rank_sub = lax.broadcasted_iota(jnp.int32, (LANES, LANES), 0)
    earlier = (wide == tall) & (rank_sub < rank_lane)
    halves = (rank_sub < 4 * visits) == (rank_lane < 4 * visits)
    rank = jnp.sum(jnp.where(earlier & halves, 1.0, 0.0), axis=0, keepdims=True).astype(jnp.int32)
    shares = info_row[1:2, :].astype(F32) / jnp.maximum(info_row[2:3, :], 1).astype(F32)
    int_ref[16:24, :] = jnp.zeros((8, LANES), jnp.int32)
    real_ref[...] = jnp.zeros((8, LANES), F32)
    tables(0, ids, rank, shares, hot, int_ref, real_ref)
    lane = lane[0:1, :]
    own = (lane >= first) & (lane < first + visits) & (ids == hot)
    seen = jnp.sum(jnp.where(own, 1.0, 0.0), axis=1, keepdims=True)
    first_lane = jnp.min(jnp.where(own, lane, 1000).astype(F32), axis=1, keepdims=True)
    last_lane = jnp.max(jnp.where(own, lane, -1).astype(F32), axis=1, keepdims=True)
    int_ref[17:18, :] = ids
    int_ref[18:19, :] = rank
    int_ref[19:20, :] = hot
    first_block = jnp.where(seen > 0.5, (first_lane.astype(jnp.int32) - first) >> 1, 0)
    last_block = (last_lane.astype(jnp.int32) - first) >> 1
    following = jnp.where(first_block + 1 >= blocks, 0, first_block + 1)
    second_block = jnp.where(seen > 1.5, last_block, following)
    int_ref[21:22, :] = jnp.where(lane == 0, first_block, second_block)
    lane_real = lane.astype(F32)
    first_share = jnp.sum(
        jnp.where(own & (lane_real == first_lane), shares, 0.0), axis=1, keepdims=True
    )
    last_share = jnp.sum(
        jnp.where(own & (lane_real == last_lane) & (seen > 1.5), shares, 0.0), axis=1, keepdims=True
    )
    real_ref[1:2, :] = shares
    real_ref[2:3, :] = jnp.where(lane == 0, first_share, last_share)
    arrive(peak_waits)
    peaks[y] = peak[...]
    top = peaks[0]
    for i in range(1, groups):
        top = jnp.maximum(top, peaks[i])
    int_ref[22:23, :] = top[0:1, :].astype(jnp.int32)

    causal = lax.broadcasted_iota(jnp.int32, (ROWS, ROWS), 0) >= lax.broadcasted_iota(
        jnp.int32, (ROWS, ROWS), 1
    )

    def within(start, stop):
        @pl.loop(start, stop)
        def _(head):
            cols = pl.ds(pl.multiple_of(head * HEAD_DIM, HEAD_DIM), HEAD_DIM)
            keys = k[:, cols]
            both = jnp.concatenate([v[:, cols], jnp.ones((tokens, HEAD_DIM), BF16)], axis=1)
            for tile in range(tiles):
                part = slice(tile * ROWS, (tile + 1) * ROWS)
                query = q[part, cols]
                scores = jnp.where(causal, dot_last(query, keys[part, :]), 0.0).astype(BF16)
                total = jnp.dot(scores, both[part, :], preferred_element_type=F32)
                if tile > 0:
                    scores = dot_last(query, keys[: tile * ROWS, :]).astype(BF16)
                    total = total + jnp.dot(
                        scores, both[: tile * ROWS, :], preferred_element_type=F32
                    )
                numer[part, cols] = total[:, :HEAD_DIM]
                denom[part, cols] = total[:, HEAD_DIM:]

    arrive(waits)
    base = c * WAYS
    for i in range(WAYS):
        sums[i] = (state[base + i] + theirs[base + i].astype(F32)).astype(BF16)
    xs[x] = sums[x]
    waits = [go(sums.at[(x + d) % WAYS], xs.at[x], along_x[d - 1]) for d in range(1, WAYS)]
    send_far(0)
    send_far(1)
    project_query(2)
    project_query(3)
    arrive(waits)
    row_sum[...] = sum(xs[i].astype(F32) for i in range(WAYS)).astype(BF16)
    zs[z] = row_sum[...]
    waits = [go(row_sum, zs.at[z], along_z[d - 1]) for d in range(1, WAYS)]
    relay_far(0)
    relay_far(1)
    within(0, 3)
    arrive(waits)
    plane_sum[...] = sum(zs[i].astype(F32) for i in range(WAYS)).astype(BF16)
    waits = [go(plane_sum, ys.at[y], along_y[d - 1]) for d in range(1, groups)]
    total = jnp.zeros(row_sum.shape, F32)
    for i in range(WAYS):
        total = total + zs[i].astype(F32) * jnp.where(i < z, 1.0, 0.0)
    within(3, 6)
    arrive(waits)
    ys[y] = plane_sum[...]
    for i in range(groups):
        total = total + ys[i].astype(F32) * jnp.where(i < y, 1.0, 0.0)
    for i in range(WAYS):
        back[i] = total.astype(BF16)
        total = total + xs[i].astype(F32)
    heads_in[x] = back[x]
    waits = [go(back.at[(x + d) % WAYS], heads_in.at[x], along_x[d - 1]) for d in range(1, WAYS)]
    within(6, 8)
    arrive(waits)
    waits = [go(heads_in, sib2, sibling)]
    later = jnp.where(c == 1, 1.0, 0.0)

    def add_prior(first_head, source):
        @pl.loop(0, WAYS)
        def _(i):
            head = first_head + i
            prior = (source[i].astype(F32) + theirs[head].astype(F32) * later).astype(BF16)
            filled = jnp.broadcast_to(prior[HEAD_DIM : HEAD_DIM + 1, :], (HEAD_DIM, HEAD_DIM))
            carried = jnp.concatenate([prior[:HEAD_DIM, :], filled], axis=0)
            cols = pl.ds(pl.multiple_of(head * HEAD_DIM, HEAD_DIM), HEAD_DIM)
            total = dot_last(q[:, cols], carried)
            ratio[:, cols] = (numer[:, cols] + total[:, :HEAD_DIM]) / (
                denom[:, cols] + total[:, HEAD_DIM:]
            )

    add_prior(base, heads_in)
    arrive(waits)
    add_prior((1 - c) * WAYS, sib2)

    @pl.loop(0, 2)
    def _(part):
        part_rows = pl.ds(pl.multiple_of(part * half, PIECE), half)
        attended = norm_rows(ratio[part_rows, :], hgain_ref[...]).astype(BF16)
        resid = x_ref[part_rows, :].astype(F32) + jnp.dot(
            attended, wout_ref[...], preferred_element_type=F32
        )
        resid = resid.astype(BF16)
        resid_ref[part_rows, :] = resid
        ffn_ref[part_rows, :] = norm_rows(resid.astype(F32), fgain_ref[...]).astype(BF16)
    second_reduce(0)
    second_reduce(1)
    for copy in copies:
        copy.wait_send()


def front(
    x, attn_gain, w_qkv, head_gain, w_out, ffn_gain, w_gate, w_up, w_down, pair_ids, gate_codes, groups
):
    tokens, width = x.shape
    packed = 2 * w_gate.shape[1] + width
    blocks = pair_ids.shape[1]
    tile = (8, LANES)
    one = (STATE, HEAD_DIM)
    some = (WAYS,) + one
    every = (HEADS,) + one
    step = 2 * HEAD_DIM
    pieces = 3 * width // step
    count = 1 + 2 * (WAYS - 1) + groups - 1 + 2 + 3 * (WAYS - 1) + groups - 1
    count += 3 + 12

    def wide(*shape):
        return pltpu.VMEM(shape + (packed,), BF16)

    vmem = pl.BlockSpec(memory_space=pltpu.VMEM)
    hbm = pl.BlockSpec(memory_space=pl.ANY)
    return pl.pallas_call(
        functools.partial(front_kernel, groups, blocks),
        out_shape=[jax.ShapeDtypeStruct((tokens, width), BF16)] * 2
        + [jax.ShapeDtypeStruct((24, LANES), jnp.int32), jax.ShapeDtypeStruct(tile, F32)]
        + [jax.ShapeDtypeStruct((2, SLICE, packed), BF16)],
        in_specs=[vmem] * 4 + [hbm] + [vmem] * 3 + [hbm] * 3,
        out_specs=[vmem] * 5,
        scratch_shapes=[pltpu.VMEM((tokens, width), BF16)] * 4
        + [pltpu.VMEM((pieces, width, step), BF16), pltpu.VMEM(every, F32)]
        + [pltpu.VMEM((tokens, width), F32)] * 3
        + [
            pltpu.VMEM(tile, jnp.int32),
            pltpu.VMEM((WAYS,) + tile, jnp.int32),
            pltpu.VMEM(tile, jnp.int32),
            pltpu.VMEM((WAYS,) + tile, jnp.int32),
            pltpu.VMEM(tile, F32),
            pltpu.VMEM((groups,) + tile, F32),
            pltpu.VMEM(every, BF16),
            pltpu.VMEM(every, BF16),
            pltpu.VMEM(some, BF16),
            pltpu.VMEM(some, BF16),
            pltpu.VMEM(one, BF16),
            pltpu.VMEM(some, BF16),
            pltpu.VMEM(one, BF16),
            pltpu.VMEM((groups,) + one, BF16),
            pltpu.VMEM(some, BF16),
            pltpu.VMEM(some, BF16),
            pltpu.VMEM(some, BF16),
            wide(HALF),
            wide(HALF),
            wide(2, WAYS - 1, SLICE),
            wide(2, 2, SLICE // 2),
            pltpu.SemaphoreType.DMA((pieces,)),
            pltpu.SemaphoreType.DMA((3,)),
            pltpu.SemaphoreType.DMA((count,)),
            pltpu.SemaphoreType.DMA((count,)),
        ],
        compiler_params=pltpu.CompilerParams(
            collective_id=0, has_side_effects=True, vmem_limit_bytes=LIMIT_BYTES
        ),
        name="front",
    )(
        pair_ids, gate_codes, x, attn_gain, w_qkv, head_gain, w_out, ffn_gain, w_gate, w_up, w_down
    )


def moe_kernel(
    blocks, chunks, table, weight, f_ref, base_hbm, wg_hbm, wu_hbm, wd_hbm, slice_ref, out_ref,
    *rest
):
    gather, landed = rest[:chunks], rest[chunks : 2 * chunks]
    (
        hand, zs, relay, taken, made_rows, relay_back, hand_back, partial, final, local, send, recv,
        base_ref, wg_ref, wu_ref, wd_ref, fetch_sem, inside, pieces_in, whole, hotw, hot_inner, hot_out, hot_local, hot_send, hot_recv,
    ) = rest[2 * chunks :]
    depth = ROWS // chunks
    width = f_ref.shape[2]
    hidden = wg_ref.shape[1]
    y, z, x, c = place()
    lane = WAYS * CORES
    parity = x % 2

    def at(zz, xx, cc):
        return (y, ((zz + WAYS) % WAYS) * lane + ((xx + WAYS) % WAYS) * CORES + cc)

    sibling = at(z, x, 1 - c)
    mate = at(z, x + 1 - 2 * parity, c)
    across = at(z, x + 2 * parity - 1, c)
    up, down = at(z + 1, x, c), at(z - 1, x, c)
    fetched = []
    for n, (source, place_in) in enumerate(
        ((wg_hbm, wg_ref), (wu_hbm, wu_ref), (wd_hbm, wd_ref), (base_hbm, base_ref))
    ):
        fetch = pltpu.make_async_copy(source, place_in, fetch_sem.at[n])
        fetch.start()
        fetched.append(fetch)
    far_x, far_z = at(z, x + 2, c), at(z + 2, x, c)
    greet([sibling, mate, across, up, down, far_x, far_z])
    me = parity * CORES + c
    friend = (1 - parity) * CORES + c
    pending = []
    made = {}

    def go(k, n, src, dst, device):
        copy = remote(src, dst, send.at[k, n], recv.at[k, n], device)
        copy.start()
        pending.append(copy)
        made[k, n] = copy

    def keep(k, n, src, dst):
        copy = pltpu.make_async_copy(src, dst, local.at[k, n])
        copy.start()
        made[k, "keep", n] = copy

    def arrived(k, *numbers):
        for n in numbers:
            made[k, n].wait_recv()

    def step_of(row):
        return (row + WAYS) % WAYS

    def begin(k):
        own = f_ref.at[:, pl.ds(k * depth, depth), :]
        here = gather[k].at[pl.ds(me * blocks, blocks)]
        go(k, 0, own, here, mate)
        go(k, 1, own, here, sibling)
        keep(k, 0, own, here)

    def widen(k):
        arrived(k, 0)
        there = gather[k].at[pl.ds(friend * blocks, blocks)]
        go(k, 2, there, there, sibling)

    def select(k):
        made[k, "keep", 0].wait()
        arrived(k, 1, 2)
        for row in range(WAYS):
            for j in range(SLOTS):
                hand[k, row, j] = gather[k][table[8 + row * SLOTS + j, 0]]
        go(k, 3, hand.at[k], zs.at[k, :, 1], across)
        for row in range(WAYS):
            for j in range(SLOTS):
                zs[k, row, 0, j] = gather[k][table[row * SLOTS + j, 0]]

    def climb(k):
        arrived(k, 3)
        go(k, 6, zs.at[k, step_of(z + 2), 0], relay.at[k, 0], up)
        go(k, 19, zs.at[k, step_of(z + 2), 1], relay.at[k, 1], down)
        go(k, 4, zs.at[k, step_of(z + 1)], taken.at[k, z], up)
        go(k, 5, zs.at[k, step_of(z - 1)], taken.at[k, z], down)
        keep(k, 1, zs.at[k, z], taken.at[k, z])

    def forward(k):
        arrived(k, 6)
        go(k, 7, relay.at[k, 0], taken.at[k, step_of(z - 1), 0], up)
        arrived(k, 19)
        go(k, 20, relay.at[k, 1], taken.at[k, step_of(z + 1), 1], down)

    def work(k):
        if k == 0:
            for fetch in fetched:
                fetch.wait()
        arrived(k, 4, 5, 7, 20)
        made[k, "keep", 1].wait()
        def rise(cols):
            rows = taken[k].reshape(WAYS * PART * depth, width)
            gate = jnp.dot(rows, wg_ref[:, cols], preferred_element_type=F32)
            upper = jnp.dot(rows, wu_ref[:, cols], preferred_element_type=F32)
            inside[:, cols] = (jax.nn.silu(gate) * upper).astype(BF16)

        @pl.loop(0, hidden // TILE)
        def _(i):
            rise(pl.ds(pl.multiple_of(i * TILE, TILE), TILE))

        if hidden % TILE:
            rise(slice(hidden - hidden % TILE, hidden))

        @pl.loop(0, width // TILE)
        def _(i):
            cols = pl.ds(pl.multiple_of(i * TILE, TILE), TILE)
            result = jnp.dot(inside[...], wd_ref[:, cols], preferred_element_type=F32)
            made_rows[k, :, :, :, :, cols] = result.astype(BF16).reshape(
                WAYS, SIDES, SLOTS, depth, TILE
            )

        go(k, 12, made_rows.at[k, step_of(z + 2), 0], relay_back.at[k, 0], up)
        go(k, 21, made_rows.at[k, step_of(z + 2), 1], relay_back.at[k, 1], down)
        for n, d, device in ((8, 1, up), (10, -1, down)):
            target = step_of(z + d)
            go(k, n, made_rows.at[k, target, 0], landed[k].at[pl.ds(c * 16 + z * SLOTS, SLOTS)], device)
            go(k, n + 1, made_rows.at[k, target, 1], hand_back.at[k, pl.ds(z * SLOTS, SLOTS)], device)
        keep(k, 2, made_rows.at[k, z, 0], landed[k].at[pl.ds(c * 16 + z * SLOTS, SLOTS)])
        keep(k, 3, made_rows.at[k, z, 1], hand_back.at[k, pl.ds(z * SLOTS, SLOTS)])

    def forward_back(k):
        arrived(k, 21)
        origin = step_of(z + 1)
        go(k, 14, relay_back.at[k, 1], hand_back.at[k, pl.ds(origin * SLOTS, SLOTS)], down)
        arrived(k, 12)
        origin = step_of(z - 1)
        go(k, 13, relay_back.at[k, 0], landed[k].at[pl.ds(c * 16 + origin * SLOTS, SLOTS)], up)

    def give(k):
        arrived(k, 9, 11, 14)
        made[k, "keep", 3].wait()
        go(k, 15, hand_back.at[k], landed[k].at[pl.ds(c * 16 + 8, 8)], across)
        arrived(k, 8, 10, 13)
        made[k, "keep", 2].wait()
        there = landed[k].at[pl.ds(c * 16, 8)]
        go(k, 16, there, there, sibling)

    def mirror(k):
        arrived(k, 15)
        there = landed[k].at[pl.ds(c * 16 + 8, 8)]
        go(k, 17, there, there, sibling)

    def build(k):
        arrived(k, 16, 17)

        def one(start, offset):
            def run(b, carry):
                first = start + 2 * b
                total = landed[k][table[16, first]].astype(F32) * weight[0, first]
                total = total + landed[k][table[16, first + 1]].astype(F32) * weight[0, first + 1]
                partial[k, offset + b] = total.astype(BF16)
                return carry

            return run

        row = (x // 2) * 4 * 2 * blocks
        lax.fori_loop(0, blocks, one(row + friend * 2 * blocks, blocks), 0)
        go(k, 18, partial.at[k, pl.ds(blocks, blocks)], final.at[k], mate)
        lax.fori_loop(0, blocks, one(row + me * 2 * blocks, 0), 0)

    def finish(k):
        arrived(k, 18)
        rows = slice(k * depth, (k + 1) * depth)

        def run(b, carry):
            total = base_ref[b, rows, :].astype(F32) + partial[k, b].astype(F32)
            total = total + final[k, b].astype(F32)
            for i in range(2):
                share = jnp.where(table[21, i] == b, weight[2, i], 0.0)
                total = total + hot_out[i, rows, :].astype(F32) * share
            out_ref[b, rows, :] = total.astype(BF16)
            return carry

        lax.fori_loop(0, blocks, run, 0)

    right, left = at(z, x + 1, c), at(z, x - 1, c)
    ring = ((x, right, left, far_x), (z, up, down, far_z))
    hot_made = {}

    def hot_go(n, src, dst, device):
        copy = remote(src, dst, hot_send.at[n], hot_recv.at[n], device)
        copy.start()
        pending.append(copy)
        hot_made[n] = copy

    short = SLICE // 2

    def hot_rows(order, spot, shift=0, size=SLICE):
        row = order * (HALF // 2) + ((spot + WAYS) % WAYS) * SLICE + shift
        return hotw.at[c, pl.ds(row, size)]

    def hot_pieces():
        for order in range(2):
            spot, plus, minus, opposite = ring[1 - order]
            for d, device in ((2, opposite), (1, plus), (3, minus)):
                row = pl.ds(((spot + d) % WAYS) * PIECE, PIECE)
                hot_go(
                    32 + 6 * order + d, slice_ref.at[order, row], pieces_in.at[order, d - 1], device
                )

    def hot_sum():
        for order in range(2):
            spot, plus, minus, opposite = ring[1 - order]
            for d in (1, 2, 3):
                hot_made[32 + 6 * order + d].wait_recv()
            row = pl.ds(pl.multiple_of(spot * PIECE, PIECE), PIECE)
            total = slice_ref[order, row, :] + pieces_in[order, 0]
            whole[order, row, :] = total + (pieces_in[order, 1] + pieces_in[order, 2])
            for d, device in ((2, opposite), (1, plus), (3, minus)):
                there = whole.at[order, row]
                hot_go(35 + 6 * order + d, there, there, device)

    def hot_whole(order):
        for d in (1, 2, 3):
            hot_made[35 + 6 * order + d].wait_recv()

    def hot_begin(order, part):
        spot, plus, minus, _ = ring[order]
        shift = part * short
        piece = whole.at[order, pl.ds(shift, short)]
        there = hot_rows(order, spot, shift, short)
        base = 16 * order + 8 * part
        hot_go(base, piece, there, plus)
        hot_go(base + 1, piece, there, minus)
        hot_go(base + 2, piece, there, sibling)
        copy = pltpu.make_async_copy(piece, there, hot_local.at[2 * order + part])
        copy.start()
        hot_made["keep", order, part] = copy

    def hot_relay(order, part):
        spot, plus, minus, _ = ring[order]
        base = 16 * order + 8 * part
        shift = part * short
        for n, neighbour in ((0, spot - 1), (1, spot + 1)):
            hot_made[base + n].wait_recv()
            there = hot_rows(order, neighbour, shift, short)
            if n == part:
                hot_go(base + 3, there, there, plus if n == 0 else minus)
            hot_go(base + 4 + n, there, there, sibling)

    def hot_last(order, part):
        spot = ring[order][0]
        base = 16 * order + 8 * part
        hot_made[base + 3].wait_recv()
        there = hot_rows(order, spot + 2, part * short, short)
        hot_go(base + 6, there, there, sibling)

    def hot_ready():
        for order in range(2):
            for part in range(2):
                hot_made["keep", order, part].wait()
                for n in (2, 4, 5, 6):
                    hot_made[16 * order + 8 * part + n].wait_recv()

    def hot_first():
        def rise(start):
            rows = jnp.concatenate([f_ref[table[21, 0]], f_ref[table[21, 1]]], axis=0)
            low, high = rows[:, :HALF], rows[:, HALF:]

            def both(cols):
                return jnp.dot(low, hotw[0, :, cols], preferred_element_type=F32) + jnp.dot(
                    high, hotw[1, :, cols], preferred_element_type=F32
                )

            gate = both(pl.ds(start, HEAD_DIM))
            upper = both(pl.ds(pl.multiple_of(start + hidden, HEAD_DIM), HEAD_DIM))
            hot_inner[:, pl.ds(start, HEAD_DIM)] = (jax.nn.silu(gate) * upper).astype(BF16)

        @pl.loop(0, hidden // HEAD_DIM)
        def _(i):
            rise(pl.multiple_of(i * HEAD_DIM, HEAD_DIM))

    def hot_second():
        @pl.loop(0, width // TILE)
        def _(i):
            start = pl.multiple_of(i * TILE, TILE)
            cols = pl.ds(pl.multiple_of(2 * hidden + start, TILE), TILE)
            result = jnp.dot(hot_inner[:, :HALF], hotw[0, :, cols], preferred_element_type=F32)
            result = result + jnp.dot(
                hot_inner[:, HALF:], hotw[1, 2 * HALF - hidden :, cols], preferred_element_type=F32
            )
            hot_out[:, :, pl.ds(start, TILE)] = result.astype(BF16).reshape(2, ROWS, TILE)

    stages = [widen, select, climb, forward, work, forward_back, give, mirror, build]
    begin(0)
    hot_pieces()
    begin(1)
    extras = {
        0: ((hot_sum,),),
        1: ((hot_whole, 1), (hot_begin, 1, 0), (hot_begin, 1, 1)),
        2: ((hot_whole, 0), (hot_begin, 0, 0)),
        3: ((hot_relay, 1, 0),),
        4: ((hot_relay, 1, 1), (hot_relay, 0, 0)),
        5: ((hot_last, 1, 0), (hot_begin, 0, 1)),
        6: ((hot_last, 1, 1), (hot_last, 0, 0)),
        7: ((hot_relay, 0, 1),),
        9: ((hot_last, 0, 1),),
        chunks + 3: ((hot_ready,), (hot_first,)),
        chunks + 4: ((hot_second,),),
    }
    lag_of = len(stages)
    done = 0
    for step in range(chunks + lag_of):
        if step + 2 < chunks:
            begin(step + 2)
        for lag in reversed(range(lag_of)):
            if 0 <= step - lag < chunks:
                stages[lag](step - lag)
        for extra in extras.get(step, ()):
            extra[0](*extra[1:])
        if step > chunks + 4:
            while done <= min(step - lag_of, chunks - 1):
                finish(done)
                done += 1
    for copy in pending:
        copy.wait_send()


def moe(table, weight, ffn_in, base, w_gate, w_up, w_down, hot_slices):
    blocks, rows, width = ffn_in.shape
    packed = hot_slices.shape[2]
    chunks = CHUNKS
    depth = rows // chunks
    pair = 2 * CORES * blocks
    whole = pl.BlockSpec(memory_space=pltpu.VMEM)
    hbm = pl.BlockSpec(memory_space=pl.ANY)
    return pl.pallas_call(
        functools.partial(moe_kernel, blocks, chunks),
        out_shape=jax.ShapeDtypeStruct(base.shape, BF16),
        in_specs=[pl.BlockSpec(memory_space=pltpu.SMEM)] * 2 + [whole] + [hbm] * 4 + [whole],
        out_specs=whole,
        scratch_shapes=[pltpu.VMEM((pair, depth, width), BF16)] * chunks
        + [pltpu.VMEM((CORES * 16, depth, width), BF16)] * chunks
        + [
            pltpu.VMEM((chunks, WAYS, SLOTS, depth, width), BF16),
            pltpu.VMEM((chunks, WAYS, SIDES, SLOTS, depth, width), BF16),
            pltpu.VMEM((chunks, SIDES, SLOTS, depth, width), BF16),
            pltpu.VMEM((chunks, WAYS, SIDES, SLOTS, depth, width), BF16),
            pltpu.VMEM((chunks, WAYS, SIDES, SLOTS, depth, width), BF16),
            pltpu.VMEM((chunks, SIDES, SLOTS, depth, width), BF16),
            pltpu.VMEM((chunks, WAYS * SLOTS, depth, width), BF16),
            pltpu.VMEM((chunks, 2 * blocks, depth, width), BF16),
            pltpu.VMEM((chunks, blocks, depth, width), BF16),
            pltpu.SemaphoreType.DMA((chunks, 4)),
            pltpu.SemaphoreType.DMA((chunks, 22)),
            pltpu.SemaphoreType.DMA((chunks, 22)),
            pltpu.VMEM(base.shape, BF16),
            pltpu.VMEM(w_gate.shape, BF16),
            pltpu.VMEM(w_up.shape, BF16),
            pltpu.VMEM(w_down.shape, BF16),
            pltpu.SemaphoreType.DMA((4,)),
            pltpu.VMEM((WAYS * PART * depth, w_gate.shape[1]), BF16),
            pltpu.VMEM((2, WAYS - 1, PIECE, packed), BF16),
            pltpu.VMEM((2, SLICE, packed), BF16),
            pltpu.VMEM((CORES, HALF, packed), BF16),
            pltpu.VMEM((2 * rows, w_gate.shape[1]), BF16),
            pltpu.VMEM((2, rows, width), BF16),
            pltpu.SemaphoreType.DMA((4,)),
            pltpu.SemaphoreType.DMA((48,)),
            pltpu.SemaphoreType.DMA((48,)),
        ],
        compiler_params=pltpu.CompilerParams(
            collective_id=1, has_side_effects=True, vmem_limit_bytes=67043328
        ),
        name="moe",
    )(table, weight, ffn_in, base, w_gate, w_up, w_down, hot_slices)


def tables_kernel(turn, int_ref, real_ref, out_int, out_real):
    out_int[...] = int_ref[...]
    out_real[...] = real_ref[...]
    out_real[2:3, :] = jnp.zeros((1, LANES), F32)
    tables(
        turn[0], int_ref[17:18, :], int_ref[18:19, :], real_ref[1:2, :], int_ref[19:20, :],
        out_int, out_real,
    )


def later_tables(turn, ints, reals):
    return pl.pallas_call(
        tables_kernel,
        out_shape=[
            jax.ShapeDtypeStruct(ints.shape, ints.dtype),
            jax.ShapeDtypeStruct(reals.shape, reals.dtype),
        ],
        in_specs=[pl.BlockSpec(memory_space=pltpu.SMEM)]
        + [pl.BlockSpec(memory_space=pltpu.VMEM)] * 2,
        out_specs=[pl.BlockSpec(memory_space=pltpu.VMEM)] * 2,
        name="later_tables",
    )(turn, ints, reals)


def body(
    hidden_in, attn_gain, w_qkv, head_gain, w_out, ffn_gain, w_gate, w_up, w_down, pair_ids, gate_codes
):
    tokens, width = hidden_in.shape
    blocks = tokens // ROWS
    groups = lax.axis_size("grp")
    weights = (w_gate[0], w_up[0], w_down[0])
    resid, ffn_in, ints, reals, hot_slices = front(
        hidden_in, attn_gain[None], w_qkv, head_gain[None], w_out, ffn_gain[None], *weights, pair_ids.T,
        gate_codes.T, groups,
    )
    resid = resid.reshape(blocks, ROWS, width)
    ffn_in = ffn_in.reshape(blocks, ROWS, width)

    total = moe(ints, reals, ffn_in, resid, *weights, hot_slices)

    def more(total):
        def one(turn, total):
            later_ints, later_reals = later_tables(turn[None], ints, reals)
            return moe(later_ints, later_reals, ffn_in, total, *weights, hot_slices)

        return lax.fori_loop(1, -(-LIMIT // SLOTS), one, total)

    total = lax.cond(ints[22, 0] > SLOTS, more, lambda total: total, total)
    return total.reshape(tokens, width)


def solution(mesh):
    return jax.shard_map(
        body,
        mesh=mesh,
        in_specs=(
            P(("grp", "seq"), None), P(), P(), P(), P(), P(),
            P("seq", None, None), P("seq", None, None), P("seq", None, None),
            P(("grp", "seq"), None), P(("grp", "seq"), None),
        ),
        out_specs=P(("grp", "seq"), None),
        check_vma=False,
    )
```

```python
import functools

import jax
import jax.numpy as jnp
from jax import lax
from jax.experimental import pallas as pl
from jax.experimental.pallas import tpu as pltpu
from jax.sharding import PartitionSpec as P

HEADS = 8
HEAD_DIM = 128
ROWS = 128
EPS = 1e-06
WAYS = 4
CORES = 2
SLOTS = 2
SIDES = 2
PART = SIDES * SLOTS
DEPTHS = (8, 16, 16, 16, 16, 16, 16, 16, 8)
STATE = 144
LIMIT = 8
LANES = 128
HALF = 512
TILE = 256
SLICE = 64
PIECE = 16
HOT = 15
MESH = pl.DeviceIdType.MESH
F32 = jnp.float32
BF16 = jnp.bfloat16
LIMIT_BYTES = 60 * 1024 * 1024


def place():
    seq = lax.axis_index("seq")
    return lax.axis_index("grp"), seq // (WAYS * CORES), (seq // CORES) % WAYS, seq % CORES


def remote(src, dst, send, recv, device):
    return pltpu.make_async_remote_copy(
        src_ref=src, dst_ref=dst, send_sem=send, recv_sem=recv, device_id=device, device_id_type=MESH
    )


def greet(devices):
    barrier = pltpu.get_barrier_semaphore()
    for device in devices:
        pl.semaphore_signal(barrier, inc=1, device_id=device, device_id_type=MESH)
    pl.semaphore_wait(barrier, len(devices))


def norm_rows(values, gain):
    return values * lax.rsqrt(jnp.mean(values * values, axis=-1, keepdims=True) + EPS) * gain


def dot_last(a, b):
    return lax.dot_general(a, b, (((1,), (1,)), ((), ())), preferred_element_type=F32)


def dot_first(a, b):
    return lax.dot_general(a, b, (((0,), (0,)), ((), ())), preferred_element_type=F32)


def lifted(values):
    return jnp.where(values > 0.0, values + 1.0, jnp.exp(jnp.minimum(values, 0.0))).astype(BF16)


def tables(turn, ids, rank, shares, hot, out_int, out_real):
    y, z, x, c = place()
    half = x // 2
    other = (x + 2 * (x % 2) - 1 + WAYS) % WAYS
    span = LANES * 7 // 16
    lane = lax.broadcasted_iota(jnp.int32, (1, LANES), 1)
    local = lane - half * span
    near = (local >= 0) & (local < span)
    place_of = rank - turn * SLOTS
    usable = near & (ids >= 0) & (ids != hot) & (place_of >= 0) & (place_of < SLOTS)
    slot = lax.broadcasted_iota(jnp.int32, (16, LANES), 0)
    column = jnp.where(slot >= 8, other, x)
    expert = ((slot & 7) >> 1) * (WAYS * CORES) + column * CORES + c
    key = jnp.where(usable, ids * SLOTS + place_of, -1)
    hit = key == expert * SLOTS + (slot & 1)
    source = jnp.sum(jnp.where(hit, local >> 1, 0).astype(F32), axis=1, keepdims=True)
    out_int[0:16, :] = jnp.broadcast_to(source, (16, LANES)).astype(jnp.int32)
    here = (ids >> 1) & 3
    which = jnp.where(here == other, 1, 0)
    mine = usable & ((here == x) | (here == other))
    index = (ids & 1) * 16 + which * 8 + (ids >> 3) * SLOTS + place_of
    out_int[16:17, :] = jnp.where(mine, index, 0)
    out_real[0:1, :] = jnp.where(mine, shares, 0.0)


def front_kernel(
    groups, blocks, pairs, codes, x_ref, again_ref, wqkv_ref, hgain_ref, wout_ref, fgain_ref,
    wg_ref, wu_ref, wd_ref, resid_ref, ffn_ref, int_ref, real_ref, hot_ref,
    normed, q, k, v, wcols, state, ratio, numer, denom,
    chip, chips, sib, rows, peak, peaks,
    mine, theirs, sums, xs, row_sum, zs, plane_sum, ys, back, heads_in, sib2,
    near, far, slices, halves_in, summed, pieces_in, loads, stay, send, recv,
):
    y, z, x, c = place()
    lane_count = WAYS * CORES
    tokens, width = x_ref.shape
    tiles = tokens // ROWS
    step = 2 * HEAD_DIM
    steps = width // step
    half = tokens // 2

    def at(yy, zz, xx, cc):
        return (yy, zz * lane_count + xx * CORES + cc)

    sibling = at(y, z, x, 1 - c)
    along_x = [at(y, z, (x + d) % WAYS, c) for d in range(1, WAYS)]
    along_z = [at(y, (z + d) % WAYS, x, c) for d in range(1, WAYS)]
    along_y = [at((y + d) % groups, z, x, c) for d in range(1, groups)]
    fetches = []
    for j in range(3 * steps):
        fetch = pltpu.make_async_copy(
            wqkv_ref.at[:, pl.ds(j * step, step)], wcols.at[j], loads.at[j]
        )
        fetch.start()
        fetches.append(fetch)
    greet([sibling] + along_x + along_z + along_y)
    copies = []

    def go(src, dst, device):
        n = len(copies)
        copy = remote(src, dst, send.at[n], recv.at[n], device)
        copy.start()
        copies.append(copy)
        return copy

    def arrive(waits):
        for copy in waits:
            copy.wait_recv()

    hidden = wg_ref.shape[1]
    offset = wd_ref.shape[0] - HALF
    lanes_of = (
        (wg_ref, HALF, pl.ds(0, hidden)),
        (wu_ref, HALF, pl.ds(hidden, hidden)),
        (wd_ref, offset, pl.ds(2 * hidden, width)),
    )
    ring = (
        (x, along_x[0], along_x[2], along_x[1]),
        (z, along_z[0], along_z[2], along_z[1]),
    )
    swapped = []
    for n, (source, jump, span) in enumerate(lanes_of):
        there = source.at[pl.ds(jump * (1 - c), HALF), :]
        swapped.append(go(there, far.at[:, span], sibling))
        local = pltpu.make_async_copy(
            source.at[pl.ds(jump * c, HALF), :], near.at[:, span], stay.at[n]
        )
        local.start()
        fetches.append(local)

    def start_reduce(far_half):
        waits = []
        for order, (spot, plus, minus, _) in enumerate(ring):
            top = order * (HALF // 2)

            def part(i, shift=0, size=SLICE):
                row = top + ((spot + i + WAYS) % WAYS) * SLICE + shift
                return near.at[pl.ds(row, size)]

            short = SLICE // 2
            if far_half:
                waits.append(
                    (
                        go(part(2, 0, short), halves_in.at[order, 0], plus),
                        go(part(2, short, short), halves_in.at[order, 1], minus),
                    )
                )
            else:
                waits.append(
                    (
                        go(part(1), slices.at[order, 0], plus),
                        go(part(-1), slices.at[order, 1], minus),
                    )
                )
        return waits

    def relay_reduce(waits):
        short = SLICE // 2
        for order, (_, plus, minus, _) in enumerate(ring):
            arrive(waits[order])
            waits[order] = (
                go(halves_in.at[order, 0], slices.at[order, 2, pl.ds(0, short)], plus),
                go(halves_in.at[order, 1], slices.at[order, 2, pl.ds(short, short)], minus),
            )

    def second_reduce(waits):
        later = []
        for order, (spot, _, _, _) in enumerate(ring):
            arrive(waits[order])
            top = order * (HALF // 2) + spot * SLICE

            @pl.loop(0, SLICE // PIECE)
            def _(i):
                row = pl.multiple_of(i * PIECE, PIECE)
                base_rows = pl.ds(pl.multiple_of(top + row, PIECE), PIECE)
                row = pl.ds(row, PIECE)
                total = near[base_rows, :] + slices[order, 0, row, :]
                summed[order, row, :] = total + (slices[order, 1, row, :] + slices[order, 2, row, :])

            spot, plus, minus, opposite = ring[1 - order]
            for d, device in ((1, plus), (2, opposite), (3, minus)):
                piece = summed.at[order, pl.ds(((spot + d) % WAYS) * PIECE, PIECE)]
                later.append(go(piece, pieces_in.at[order, d - 1], device))
        return later

    def gather_pieces(waits):
        arrive(waits)
        later = []
        for order in range(2):
            spot, plus, minus, opposite = ring[1 - order]
            row = pl.ds(pl.multiple_of(spot * PIECE, PIECE), PIECE)
            total = summed[order, row, :] + pieces_in[order, 0]
            hot_ref[order, row, :] = total + (pieces_in[order, 1] + pieces_in[order, 2])
            for device in (plus, opposite, minus):
                later.append(go(hot_ref.at[order, row], hot_ref.at[order, row], device))
        return later

    visits = 2 * blocks
    lane = lax.broadcasted_iota(jnp.int32, (8, LANES), 1)
    sub = lax.broadcasted_iota(jnp.int32, (8, LANES), 0)
    first = (x * CORES + c) * visits
    info = jnp.zeros((8, LANES), jnp.int32)
    for b in range(blocks):
        code = codes[:, b : b + 1]
        pair = pairs[:, b : b + 1] + 1
        both = code[0:1, :] + code[1:2, :]
        for j in range(2):
            here = lane == first + (2 * b + j)
            value = jnp.where(
                sub == 0, pair[j : j + 1, :], jnp.where(sub == 1, code[j : j + 1, :], both)
            )
            info = jnp.where(here & (sub < 3), value, info)
    chip[...] = info
    waits = [go(chip, sib, sibling)]

    @pl.loop(0, tiles)
    def _(i):
        rows_i = pl.ds(pl.multiple_of(i * ROWS, ROWS), ROWS)
        normed[rows_i, :] = norm_rows(x_ref[rows_i, :].astype(F32), again_ref[...]).astype(BF16)

    arrive(waits)
    chips[x] = info + sib[...]
    waits = [go(chips.at[x], chips.at[x], device) for device in along_x]

    def project(j):
        for part in range(3):
            fetches[part * steps + j].wait()
        cols = slice(j * step, (j + 1) * step)

        @pl.loop(0, 2)
        def _(i):
            part = pl.ds(pl.multiple_of(i * half, PIECE), half)
            rows_in = normed[part, :]
            q[part, cols] = lifted(jnp.dot(rows_in, wcols[j], preferred_element_type=F32))
            k[part, cols] = lifted(jnp.dot(rows_in, wcols[steps + j], preferred_element_type=F32))
            v[part, cols] = jnp.dot(
                rows_in, wcols[2 * steps + j], preferred_element_type=F32
            ).astype(BF16)

        for head in range(2 * j, 2 * j + 2):
            cols = slice(head * HEAD_DIM, (head + 1) * HEAD_DIM)
            keys = k[:, cols]
            total = jnp.sum(keys.astype(F32), axis=0, keepdims=True)
            total = jnp.broadcast_to(total, (STATE - HEAD_DIM, HEAD_DIM))
            outer = dot_first(v[:, cols], keys)
            state[head, :HEAD_DIM, :] = outer
            state[head, HEAD_DIM:, :] = total
            mine[head, :HEAD_DIM, :] = outer.astype(BF16)
            mine[head, HEAD_DIM:, :] = total.astype(BF16)

    project(0)
    arrive(waits)
    info_row = chips[0] + chips[1] + chips[2] + chips[3]
    rows[z] = info_row
    waits = [go(rows.at[z], rows.at[z], device) for device in along_z]
    project(1)
    arrive(waits)
    expert = lax.broadcasted_iota(jnp.int32, (WAYS * lane_count, LANES), 0)
    lanes = lax.broadcasted_iota(jnp.int32, (WAYS * lane_count, LANES), 1)
    counts = jnp.zeros((WAYS * lane_count, 1), F32)
    most = jnp.zeros((WAYS * lane_count, 1), F32)
    for i in range(WAYS):
        there = (rows[i][0:1, :] - 1) == expert
        low = jnp.sum(jnp.where(there & (lanes < 4 * visits), 1.0, 0.0), axis=1, keepdims=True)
        high = jnp.sum(jnp.where(there & (lanes >= 4 * visits), 1.0, 0.0), axis=1, keepdims=True)
        counts = counts + low + high
        most = jnp.maximum(most, jnp.maximum(low, high))
    is_hot = counts > HOT - 0.5
    hot = jnp.sum(jnp.where(is_hot, expert[:, 0:1].astype(F32), 0.0), axis=0, keepdims=True)
    most = jnp.max(jnp.where(is_hot, 0.0, most), axis=0, keepdims=True)
    peak[...] = jnp.broadcast_to(most, (8, LANES))
    peak_waits = [go(peak, peaks.at[y], device) for device in along_y]
    here = (hot == (z * lane_count + x * CORES + c).astype(F32)).astype(BF16)
    beside = (hot == (z * lane_count + x * CORES + 1 - c).astype(F32)).astype(BF16)
    project(2)
    arrive(swapped)
    for fetch in fetches[-3:]:
        fetch.wait()

    @pl.loop(0, HALF // PIECE)
    def _(i):
        row = pl.ds(pl.multiple_of(i * PIECE, PIECE), PIECE)
        near[row, :] = near[row, :] * here + far[row, :] * beside

    reduce_waits = start_reduce(False)
    project(3)
    waits = [go(mine, theirs, sibling)]
    hot = jnp.broadcast_to(hot, (1, LANES)).astype(jnp.int32)
    ids = info_row[0:1, :] - 1
    wide = jnp.broadcast_to(ids, (LANES, LANES))
    tall = wide.T
    rank_lane = lax.broadcasted_iota(jnp.int32, (LANES, LANES), 1)
    rank_sub = lax.broadcasted_iota(jnp.int32, (LANES, LANES), 0)
    earlier = (wide == tall) & (rank_sub < rank_lane)
    halves = (rank_sub < 4 * visits) == (rank_lane < 4 * visits)
    rank = jnp.sum(jnp.where(earlier & halves, 1.0, 0.0), axis=0, keepdims=True).astype(jnp.int32)
    shares = info_row[1:2, :].astype(F32) / jnp.maximum(info_row[2:3, :], 1).astype(F32)
    int_ref[16:24, :] = jnp.zeros((8, LANES), jnp.int32)
    real_ref[...] = jnp.zeros((8, LANES), F32)
    tables(0, ids, rank, shares, hot, int_ref, real_ref)
    lane = lane[0:1, :]
    own = (lane >= first) & (lane < first + visits) & (ids == hot)
    seen = jnp.sum(jnp.where(own, 1.0, 0.0), axis=1, keepdims=True)
    first_lane = jnp.min(jnp.where(own, lane, 1000).astype(F32), axis=1, keepdims=True)
    last_lane = jnp.max(jnp.where(own, lane, -1).astype(F32), axis=1, keepdims=True)
    int_ref[17:18, :] = ids
    int_ref[18:19, :] = rank
    int_ref[19:20, :] = hot
    first_block = jnp.where(seen > 0.5, (first_lane.astype(jnp.int32) - first) >> 1, 0)
    last_block = (last_lane.astype(jnp.int32) - first) >> 1
    following = jnp.where(first_block + 1 >= blocks, 0, first_block + 1)
    second_block = jnp.where(seen > 1.5, last_block, following)
    int_ref[21:22, :] = jnp.where(lane == 0, first_block, second_block)
    lane_real = lane.astype(F32)
    first_share = jnp.sum(
        jnp.where(own & (lane_real == first_lane), shares, 0.0), axis=1, keepdims=True
    )
    last_share = jnp.sum(
        jnp.where(own & (lane_real == last_lane) & (seen > 1.5), shares, 0.0), axis=1, keepdims=True
    )
    real_ref[1:2, :] = shares
    real_ref[2:3, :] = jnp.where(lane == 0, first_share, last_share)
    arrive(peak_waits)
    peaks[y] = peak[...]
    top = peaks[0]
    for i in range(1, groups):
        top = jnp.maximum(top, peaks[i])
    int_ref[22:23, :] = top[0:1, :].astype(jnp.int32)

    causal = lax.broadcasted_iota(jnp.int32, (ROWS, ROWS), 0) >= lax.broadcasted_iota(
        jnp.int32, (ROWS, ROWS), 1
    )

    def within(start, stop):
        @pl.loop(start, stop)
        def _(head):
            cols = pl.ds(pl.multiple_of(head * HEAD_DIM, HEAD_DIM), HEAD_DIM)
            keys = k[:, cols]
            both = jnp.concatenate([v[:, cols], jnp.ones((tokens, HEAD_DIM), BF16)], axis=1)
            for tile in range(tiles):
                part = slice(tile * ROWS, (tile + 1) * ROWS)
                query = q[part, cols]
                scores = jnp.where(causal, dot_last(query, keys[part, :]), 0.0).astype(BF16)
                total = jnp.dot(scores, both[part, :], preferred_element_type=F32)
                if tile > 0:
                    scores = dot_last(query, keys[: tile * ROWS, :]).astype(BF16)
                    total = total + jnp.dot(
                        scores, both[: tile * ROWS, :], preferred_element_type=F32
                    )
                numer[part, cols] = total[:, :HEAD_DIM]
                denom[part, cols] = total[:, HEAD_DIM:]

    within(0, 2)
    arrive(waits)
    base = c * WAYS
    for i in range(WAYS):
        sums[i] = (state[base + i] + theirs[base + i].astype(F32)).astype(BF16)
    xs[x] = sums[x]
    waits = [go(sums.at[(x + d) % WAYS], xs.at[x], along_x[d - 1]) for d in range(1, WAYS)]
    far_waits = start_reduce(True)
    within(2, 4)
    arrive(waits)
    row_sum[...] = sum(xs[i].astype(F32) for i in range(WAYS)).astype(BF16)
    zs[z] = row_sum[...]
    waits = [go(row_sum, zs.at[z], along_z[d - 1]) for d in range(1, WAYS)]
    relay_reduce(far_waits)
    within(4, 6)
    arrive(waits)
    plane_sum[...] = sum(zs[i].astype(F32) for i in range(WAYS)).astype(BF16)
    waits = [go(plane_sum, ys.at[y], along_y[d - 1]) for d in range(1, groups)]
    total = jnp.zeros(row_sum.shape, F32)
    for i in range(WAYS):
        total = total + zs[i].astype(F32) * jnp.where(i < z, 1.0, 0.0)
    within(6, 7)
    arrive(waits)
    ys[y] = plane_sum[...]
    for i in range(groups):
        total = total + ys[i].astype(F32) * jnp.where(i < y, 1.0, 0.0)
    for i in range(WAYS):
        back[i] = total.astype(BF16)
        total = total + xs[i].astype(F32)
    heads_in[x] = back[x]
    waits = [go(back.at[(x + d) % WAYS], heads_in.at[x], along_x[d - 1]) for d in range(1, WAYS)]
    within(7, 8)
    reduce_waits = second_reduce([a + b for a, b in zip(reduce_waits, far_waits)])
    arrive(waits)
    waits = [go(heads_in, sib2, sibling)]
    later = jnp.where(c == 1, 1.0, 0.0)

    def add_prior(first_head, source):
        @pl.loop(0, WAYS)
        def _(i):
            head = first_head + i
            prior = (source[i].astype(F32) + theirs[head].astype(F32) * later).astype(BF16)
            filled = jnp.broadcast_to(prior[HEAD_DIM : HEAD_DIM + 1, :], (HEAD_DIM, HEAD_DIM))
            carried = jnp.concatenate([prior[:HEAD_DIM, :], filled], axis=0)
            cols = pl.ds(pl.multiple_of(head * HEAD_DIM, HEAD_DIM), HEAD_DIM)
            total = dot_last(q[:, cols], carried)
            ratio[:, cols] = (numer[:, cols] + total[:, :HEAD_DIM]) / (
                denom[:, cols] + total[:, HEAD_DIM:]
            )

    add_prior(base, heads_in)
    reduce_waits = gather_pieces(reduce_waits)
    arrive(waits)
    add_prior((1 - c) * WAYS, sib2)

    @pl.loop(0, 2)
    def _(part):
        part_rows = pl.ds(pl.multiple_of(part * half, PIECE), half)
        attended = norm_rows(ratio[part_rows, :], hgain_ref[...]).astype(BF16)
        resid = x_ref[part_rows, :].astype(F32) + jnp.dot(
            attended, wout_ref[...], preferred_element_type=F32
        )
        resid = resid.astype(BF16)
        resid_ref[part_rows, :] = resid
        ffn_ref[part_rows, :] = norm_rows(resid.astype(F32), fgain_ref[...]).astype(BF16)
    arrive(reduce_waits)
    for copy in copies:
        copy.wait_send()


def front(
    x, attn_gain, w_qkv, head_gain, w_out, ffn_gain, w_gate, w_up, w_down, pair_ids, gate_codes, groups
):
    tokens, width = x.shape
    packed = 2 * w_gate.shape[1] + width
    blocks = pair_ids.shape[1]
    tile = (8, LANES)
    one = (STATE, HEAD_DIM)
    some = (WAYS,) + one
    every = (HEADS,) + one
    step = 2 * HEAD_DIM
    pieces = 3 * width // step
    count = 1 + 2 * (WAYS - 1) + groups - 1 + 2 + 3 * (WAYS - 1) + groups - 1
    count += 3 + 12 + 4 * (WAYS - 1)

    def wide(*shape):
        return pltpu.VMEM(shape + (packed,), BF16)

    vmem = pl.BlockSpec(memory_space=pltpu.VMEM)
    hbm = pl.BlockSpec(memory_space=pl.ANY)
    return pl.pallas_call(
        functools.partial(front_kernel, groups, blocks),
        out_shape=[jax.ShapeDtypeStruct((tokens, width), BF16)] * 2
        + [jax.ShapeDtypeStruct((24, LANES), jnp.int32), jax.ShapeDtypeStruct(tile, F32)]
        + [jax.ShapeDtypeStruct((2, SLICE, packed), BF16)],
        in_specs=[vmem] * 4 + [hbm] + [vmem] * 3 + [hbm] * 3,
        out_specs=[vmem] * 5,
        scratch_shapes=[pltpu.VMEM((tokens, width), BF16)] * 4
        + [pltpu.VMEM((pieces, width, step), BF16), pltpu.VMEM(every, F32)]
        + [pltpu.VMEM((tokens, width), F32)] * 3
        + [
            pltpu.VMEM(tile, jnp.int32),
            pltpu.VMEM((WAYS,) + tile, jnp.int32),
            pltpu.VMEM(tile, jnp.int32),
            pltpu.VMEM((WAYS,) + tile, jnp.int32),
            pltpu.VMEM(tile, F32),
            pltpu.VMEM((groups,) + tile, F32),
            pltpu.VMEM(every, BF16),
            pltpu.VMEM(every, BF16),
            pltpu.VMEM(some, BF16),
            pltpu.VMEM(some, BF16),
            pltpu.VMEM(one, BF16),
            pltpu.VMEM(some, BF16),
            pltpu.VMEM(one, BF16),
            pltpu.VMEM((groups,) + one, BF16),
            pltpu.VMEM(some, BF16),
            pltpu.VMEM(some, BF16),
            pltpu.VMEM(some, BF16),
            wide(HALF),
            wide(HALF),
            wide(2, WAYS - 1, SLICE),
            wide(2, 2, SLICE // 2),
            wide(2, SLICE),
            wide(2, WAYS - 1, PIECE),
            pltpu.SemaphoreType.DMA((pieces,)),
            pltpu.SemaphoreType.DMA((3,)),
            pltpu.SemaphoreType.DMA((count,)),
            pltpu.SemaphoreType.DMA((count,)),
        ],
        compiler_params=pltpu.CompilerParams(
            collective_id=0, has_side_effects=True, vmem_limit_bytes=LIMIT_BYTES
        ),
        name="front",
    )(
        pair_ids, gate_codes, x, attn_gain, w_qkv, head_gain, w_out, ffn_gain, w_gate, w_up, w_down
    )


def moe_kernel(
    blocks, chunks, table, weight, f_ref, base_ref, wg_ref, wu_ref, wd_ref, slice_ref, out_ref,
    *rest
):
    lists = [rest[n * chunks : (n + 1) * chunks] for n in range(11)]
    gather, landed, hand, zs, relay, taken, made_rows, relay_back, hand_back, partial, final = lists
    local, send, recv, inside, hotw, hot_inner, hot_out, hot_local, hot_send, hot_recv = rest[
        11 * chunks :
    ]
    width = f_ref.shape[2]
    hidden = wg_ref.shape[1]
    y, z, x, c = place()
    lane = WAYS * CORES
    parity = x % 2

    def at(zz, xx, cc):
        return (y, ((zz + WAYS) % WAYS) * lane + ((xx + WAYS) % WAYS) * CORES + cc)

    sibling = at(z, x, 1 - c)
    mate = at(z, x + 1 - 2 * parity, c)
    across = at(z, x + 2 * parity - 1, c)
    up, down = at(z + 1, x, c), at(z - 1, x, c)
    greet([sibling, mate, across, up, down])
    me = parity * CORES + c
    friend = (1 - parity) * CORES + c
    pending = []
    made = {}

    def go(k, n, src, dst, device):
        copy = remote(src, dst, send.at[k, n], recv.at[k, n], device)
        copy.start()
        pending.append(copy)
        made[k, n] = copy

    def keep(k, n, src, dst):
        copy = pltpu.make_async_copy(src, dst, local.at[k, n])
        copy.start()
        made[k, "keep", n] = copy

    def arrived(k, *numbers):
        for n in numbers:
            made[k, n].wait_recv()

    def step_of(row):
        return (row + WAYS) % WAYS

    def begin(k):
        own = f_ref.at[:, pl.ds(sum(DEPTHS[:k]), DEPTHS[k]), :]
        here = gather[k].at[pl.ds(me * blocks, blocks)]
        go(k, 0, own, here, mate)
        go(k, 1, own, here, sibling)
        keep(k, 0, own, here)

    def widen(k):
        arrived(k, 0)
        there = gather[k].at[pl.ds(friend * blocks, blocks)]
        go(k, 2, there, there, sibling)

    def select(k):
        made[k, "keep", 0].wait()
        arrived(k, 1, 2)
        for row in range(WAYS):
            for j in range(SLOTS):
                hand[k][row, j] = gather[k][table[8 + row * SLOTS + j, 0]]
        go(k, 3, hand[k], zs[k].at[:, 1], across)
        for row in range(WAYS):
            for j in range(SLOTS):
                zs[k][row, 0, j] = gather[k][table[row * SLOTS + j, 0]]

    def climb(k):
        arrived(k, 3)
        go(k, 6, zs[k].at[step_of(z + 2), 0], relay[k].at[0], up)
        go(k, 19, zs[k].at[step_of(z + 2), 1], relay[k].at[1], down)
        go(k, 4, zs[k].at[step_of(z + 1)], taken[k].at[z], up)
        go(k, 5, zs[k].at[step_of(z - 1)], taken[k].at[z], down)
        keep(k, 1, zs[k].at[z], taken[k].at[z])

    def forward(k):
        arrived(k, 6)
        go(k, 7, relay[k].at[0], taken[k].at[step_of(z - 1), 0], up)
        arrived(k, 19)
        go(k, 20, relay[k].at[1], taken[k].at[step_of(z + 1), 1], down)

    def work(k):
        arrived(k, 4, 5, 7, 20)
        made[k, "keep", 1].wait()
        def rise(cols):
            rows = taken[k][...].reshape(WAYS * PART * DEPTHS[k], width)
            gate = jnp.dot(rows, wg_ref[:, cols], preferred_element_type=F32)
            upper = jnp.dot(rows, wu_ref[:, cols], preferred_element_type=F32)
            inside[: rows.shape[0], cols] = (jax.nn.silu(gate) * upper).astype(BF16)

        @pl.loop(0, hidden // TILE)
        def _(i):
            rise(pl.ds(pl.multiple_of(i * TILE, TILE), TILE))

        if hidden % TILE:
            rise(slice(hidden - hidden % TILE, hidden))

        @pl.loop(0, width // TILE)
        def _(i):
            cols = pl.ds(pl.multiple_of(i * TILE, TILE), TILE)
            result = jnp.dot(inside[: WAYS * PART * DEPTHS[k], :], wd_ref[:, cols], preferred_element_type=F32)
            made_rows[k][:, :, :, :, cols] = result.astype(BF16).reshape(
                WAYS, SIDES, SLOTS, DEPTHS[k], TILE
            )

        go(k, 12, made_rows[k].at[step_of(z + 2), 0], relay_back[k].at[0], up)
        go(k, 21, made_rows[k].at[step_of(z + 2), 1], relay_back[k].at[1], down)
        for n, d, device in ((8, 1, up), (10, -1, down)):
            target = step_of(z + d)
            go(k, n, made_rows[k].at[target, 0], landed[k].at[pl.ds(c * 16 + z * SLOTS, SLOTS)], device)
            go(k, n + 1, made_rows[k].at[target, 1], hand_back[k].at[pl.ds(z * SLOTS, SLOTS)], device)
        keep(k, 2, made_rows[k].at[z, 0], landed[k].at[pl.ds(c * 16 + z * SLOTS, SLOTS)])
        keep(k, 3, made_rows[k].at[z, 1], hand_back[k].at[pl.ds(z * SLOTS, SLOTS)])

    def forward_back(k):
        arrived(k, 21)
        origin = step_of(z + 1)
        go(k, 14, relay_back[k].at[1], hand_back[k].at[pl.ds(origin * SLOTS, SLOTS)], down)
        arrived(k, 12)
        origin = step_of(z - 1)
        go(k, 13, relay_back[k].at[0], landed[k].at[pl.ds(c * 16 + origin * SLOTS, SLOTS)], up)

    def give(k):
        arrived(k, 9, 11, 14)
        made[k, "keep", 3].wait()
        go(k, 15, hand_back[k], landed[k].at[pl.ds(c * 16 + 8, 8)], across)
        arrived(k, 8, 10, 13)
        made[k, "keep", 2].wait()
        there = landed[k].at[pl.ds(c * 16, 8)]
        go(k, 16, there, there, sibling)

    def mirror(k):
        arrived(k, 15)
        there = landed[k].at[pl.ds(c * 16 + 8, 8)]
        go(k, 17, there, there, sibling)

    def build(k):
        arrived(k, 16, 17)

        def one(start, offset):
            def run(b, carry):
                first = start + 2 * b
                total = landed[k][table[16, first]].astype(F32) * weight[0, first]
                total = total + landed[k][table[16, first + 1]].astype(F32) * weight[0, first + 1]
                partial[k][offset + b] = total.astype(BF16)
                return carry

            return run

        row = (x // 2) * 4 * 2 * blocks
        lax.fori_loop(0, blocks, one(row + friend * 2 * blocks, blocks), 0)
        go(k, 18, partial[k].at[pl.ds(blocks, blocks)], final[k], mate)
        lax.fori_loop(0, blocks, one(row + me * 2 * blocks, 0), 0)

    def finish(k):
        arrived(k, 18)
        rows = slice(sum(DEPTHS[:k]), sum(DEPTHS[: k + 1]))

        def run(b, carry):
            total = base_ref[b, rows, :].astype(F32) + partial[k][b].astype(F32)
            total = total + final[k][b].astype(F32)
            for i in range(2):
                share = jnp.where(table[21, i] == b, weight[2, i], 0.0)
                total = total + hot_out[i, rows, :].astype(F32) * share
            out_ref[b, rows, :] = total.astype(BF16)
            return carry

        lax.fori_loop(0, blocks, run, 0)

    right, left = at(z, x + 1, c), at(z, x - 1, c)
    ring = ((x, right, left), (z, up, down))
    hot_made = {}

    def hot_go(n, src, dst, device):
        copy = remote(src, dst, hot_send.at[n], hot_recv.at[n], device)
        copy.start()
        pending.append(copy)
        hot_made[n] = copy

    short = SLICE // 2

    def hot_rows(order, spot, shift=0, size=SLICE):
        row = order * (HALF // 2) + ((spot + WAYS) % WAYS) * SLICE + shift
        return hotw.at[c, pl.ds(row, size)]

    def hot_begin(order, part):
        spot, plus, minus = ring[order]
        shift = part * short
        piece = slice_ref.at[order, pl.ds(shift, short)]
        there = hot_rows(order, spot, shift, short)
        base = 16 * order + 8 * part
        hot_go(base, piece, there, plus)
        hot_go(base + 1, piece, there, minus)
        hot_go(base + 2, piece, there, sibling)
        copy = pltpu.make_async_copy(piece, there, hot_local.at[2 * order + part])
        copy.start()
        hot_made["keep", order, part] = copy

    def hot_relay(order, part):
        spot, plus, minus = ring[order]
        base = 16 * order + 8 * part
        shift = part * short
        for n, neighbour in ((0, spot - 1), (1, spot + 1)):
            hot_made[base + n].wait_recv()
            there = hot_rows(order, neighbour, shift, short)
            if n == part:
                hot_go(base + 3, there, there, plus if n == 0 else minus)
            hot_go(base + 4 + n, there, there, sibling)

    def hot_last(order, part):
        spot = ring[order][0]
        base = 16 * order + 8 * part
        hot_made[base + 3].wait_recv()
        there = hot_rows(order, spot + 2, part * short, short)
        hot_go(base + 6, there, there, sibling)

    def hot_ready():
        for order in range(2):
            for part in range(2):
                hot_made["keep", order, part].wait()
                for n in (2, 4, 5, 6):
                    hot_made[16 * order + 8 * part + n].wait_recv()

    def hot_first():
        def rise(start):
            rows = jnp.concatenate([f_ref[table[21, 0]], f_ref[table[21, 1]]], axis=0)
            low, high = rows[:, :HALF], rows[:, HALF:]

            def both(cols):
                return jnp.dot(low, hotw[0, :, cols], preferred_element_type=F32) + jnp.dot(
                    high, hotw[1, :, cols], preferred_element_type=F32
                )

            gate = both(pl.ds(start, HEAD_DIM))
            upper = both(pl.ds(pl.multiple_of(start + hidden, HEAD_DIM), HEAD_DIM))
            hot_inner[:, pl.ds(start, HEAD_DIM)] = (jax.nn.silu(gate) * upper).astype(BF16)

        @pl.loop(0, hidden // HEAD_DIM)
        def _(i):
            rise(pl.multiple_of(i * HEAD_DIM, HEAD_DIM))

    def hot_second():
        @pl.loop(0, width // TILE)
        def _(i):
            start = pl.multiple_of(i * TILE, TILE)
            cols = pl.ds(pl.multiple_of(2 * hidden + start, TILE), TILE)
            result = jnp.dot(hot_inner[:, :HALF], hotw[0, :, cols], preferred_element_type=F32)
            result = result + jnp.dot(
                hot_inner[:, HALF:], hotw[1, 2 * HALF - hidden :, cols], preferred_element_type=F32
            )
            hot_out[:, :, pl.ds(start, TILE)] = result.astype(BF16).reshape(2, ROWS, TILE)

    stages = [widen, select, climb, forward, work, forward_back, give, mirror, build]
    begin(0)
    begin(1)
    hot_begin(1, 0)
    hot_begin(1, 1)
    extras = {
        2: ((hot_relay, 1, 0), (hot_begin, 0, 0)),
        3: ((hot_relay, 1, 1),),
        4: ((hot_last, 1, 0), (hot_relay, 0, 0)),
        5: ((hot_last, 1, 1), (hot_begin, 0, 1)),
        7: ((hot_last, 0, 0), (hot_relay, 0, 1)),
        9: ((hot_last, 0, 1),),
        chunks + 3: ((hot_ready,), (hot_first,)),
        chunks + 4: ((hot_second,),),
    }
    lag_of = len(stages)
    done = 0
    for step in range(chunks + lag_of):
        if step + 2 < chunks:
            begin(step + 2)
        for lag in reversed(range(lag_of)):
            if 0 <= step - lag < chunks:
                stages[lag](step - lag)
        for extra in extras.get(step, ()):
            extra[0](*extra[1:])
        if step > chunks + 4:
            while done <= min(step - lag_of, chunks - 1):
                finish(done)
                done += 1
    for copy in pending:
        copy.wait_send()


def moe(table, weight, ffn_in, base, w_gate, w_up, w_down, hot_slices):
    blocks, rows, width = ffn_in.shape
    packed = hot_slices.shape[2]
    chunks = len(DEPTHS)
    depth = max(DEPTHS)

    def each(*shape):
        return [pltpu.VMEM(shape + (deep, width), BF16) for deep in DEPTHS]

    pair = 2 * CORES * blocks
    whole = pl.BlockSpec(memory_space=pltpu.VMEM)
    return pl.pallas_call(
        functools.partial(moe_kernel, blocks, chunks),
        out_shape=jax.ShapeDtypeStruct(base.shape, BF16),
        in_specs=[pl.BlockSpec(memory_space=pltpu.SMEM)] * 2 + [whole] * 6,
        out_specs=whole,
        scratch_shapes=each(pair)
        + each(CORES * 16)
        + each(WAYS, SLOTS)
        + each(WAYS, SIDES, SLOTS)
        + each(SIDES, SLOTS)
        + each(WAYS, SIDES, SLOTS)
        + each(WAYS, SIDES, SLOTS)
        + each(SIDES, SLOTS)
        + each(WAYS * SLOTS)
        + each(2 * blocks)
        + each(blocks)
        + [
            pltpu.SemaphoreType.DMA((chunks, 4)),
            pltpu.SemaphoreType.DMA((chunks, 22)),
            pltpu.SemaphoreType.DMA((chunks, 22)),
            pltpu.VMEM((WAYS * PART * depth, w_gate.shape[1]), BF16),
            pltpu.VMEM((CORES, HALF, packed), BF16),
            pltpu.VMEM((2 * rows, w_gate.shape[1]), BF16),
            pltpu.VMEM((2, rows, width), BF16),
            pltpu.SemaphoreType.DMA((4,)),
            pltpu.SemaphoreType.DMA((32,)),
            pltpu.SemaphoreType.DMA((32,)),
        ],
        compiler_params=pltpu.CompilerParams(
            collective_id=1, has_side_effects=True, vmem_limit_bytes=67043328
        ),
        name="moe",
    )(table, weight, ffn_in, base, w_gate, w_up, w_down, hot_slices)


def tables_kernel(turn, int_ref, real_ref, out_int, out_real):
    out_int[...] = int_ref[...]
    out_real[...] = real_ref[...]
    out_real[2:3, :] = jnp.zeros((1, LANES), F32)
    tables(
        turn[0], int_ref[17:18, :], int_ref[18:19, :], real_ref[1:2, :], int_ref[19:20, :],
        out_int, out_real,
    )


def later_tables(turn, ints, reals):
    return pl.pallas_call(
        tables_kernel,
        out_shape=[
            jax.ShapeDtypeStruct(ints.shape, ints.dtype),
            jax.ShapeDtypeStruct(reals.shape, reals.dtype),
        ],
        in_specs=[pl.BlockSpec(memory_space=pltpu.SMEM)]
        + [pl.BlockSpec(memory_space=pltpu.VMEM)] * 2,
        out_specs=[pl.BlockSpec(memory_space=pltpu.VMEM)] * 2,
        name="later_tables",
    )(turn, ints, reals)


def body(
    hidden_in, attn_gain, w_qkv, head_gain, w_out, ffn_gain, w_gate, w_up, w_down, pair_ids, gate_codes
):
    tokens, width = hidden_in.shape
    blocks = tokens // ROWS
    groups = lax.axis_size("grp")
    weights = (w_gate[0], w_up[0], w_down[0])
    resid, ffn_in, ints, reals, hot_slices = front(
        hidden_in, attn_gain[None], w_qkv, head_gain[None], w_out, ffn_gain[None], *weights, pair_ids.T,
        gate_codes.T, groups,
    )
    resid = resid.reshape(blocks, ROWS, width)
    ffn_in = ffn_in.reshape(blocks, ROWS, width)

    total = moe(ints, reals, ffn_in, resid, *weights, hot_slices)

    def more(total):
        def one(turn, total):
            later_ints, later_reals = later_tables(turn[None], ints, reals)
            return moe(later_ints, later_reals, ffn_in, total, *weights, hot_slices)

        return lax.fori_loop(1, -(-LIMIT // SLOTS), one, total)

    total = lax.cond(ints[22, 0] > SLOTS, more, lambda total: total, total)
    return total.reshape(tokens, width)


def solution(mesh):
    return jax.shard_map(
        body,
        mesh=mesh,
        in_specs=(
            P(("grp", "seq"), None), P(), P(), P(), P(), P(),
            P("seq", None, None), P("seq", None, None), P("seq", None, None),
            P(("grp", "seq"), None), P(("grp", "seq"), None),
        ),
        out_specs=P(("grp", "seq"), None),
        check_vma=False,
    )
```
